32 devices in a mesh: ctx: 4 (over z), head: 4 (over x, core), rep: 2 (over y).
Axes of the slice: x: 2, y: 2, z: 4, core: 2. Of those that a mesh axis runs over, the one named last changes fastest.
Arguments:
- queries: bfloat16 [4, 256, 2048], P('rep', 'ctx', 'head'), may hold values from -6 to 6
- keyvals: bfloat16 [4, 256, 4, 128], P('rep', 'ctx', 'head'), may hold values from -6 to 6
- sinks: float32 [32], P('head'), may hold values from -1 to 3
- stream: bfloat16 [4, 256, 2880], P('rep', 'ctx', 'head'), may hold values from -6 to 6
- out_weight: bfloat16 [2048, 2880], P('head', 'ctx'), may hold values from -0.75 to 0.75
- norm_gain: float32 [2880], replicated, may hold values from 0.1 to 1.9
- router: bfloat16 [2880, 32], replicated, may hold values from -0.12 to 0.12
- expert_ids: int32 [4, 256, 4], P('rep', 'ctx'), may hold values from 0 to 31, all different within a row; in each aligned block of 64 rows (0 to 63, 64 to 127, ..., all dimensions but the last counted through in order) at most 12 rows name the same one
- w_gate_up: bfloat16 [64, 720, 5760], P('ctx', 'head'), may hold values from -0.109375 to 0.109375
- w_down: bfloat16 [64, 720, 2880], P('ctx', None, 'head'), may hold values from -0.15625 to 0.15625
Outputs:
- layer_out: bfloat16 [4, 256, 2880], P('rep', 'ctx', 'head')
The draws below stay inside these ranges and needn't reach their ends.
Inputs may be any that keep to these rules, and one draw needn't show every extreme that they name: `expert_ids`: each position names 4 different experts. Within each aligned block of 64 positions of a sequence no expert is named by more than 12 positions, and in every draw some block has an expert named by exactly 12.
All inputs are finite; a program needn't handle non-finite values.
Results may differ from the reference program's by a relative error of at most 0.015.
Values may be sent and summed in bfloat16 or wider, within the bound.
A program may use at most 192 MiB of HBM per device.

```python
import math
import jax
import jax.numpy as jnp
import numpy as np
from jax import lax

D = 2880
HEAD_SIZE = 64
QUERY_HEADS = 32
KEYVALUE_HEADS = 4
H = 1440
EXPERTS = 32
TOPK = 4
SEQUENCE_COUNT = 4
SEQUENCE_LENGTH = 256
BLOCK = 64
CAP = 12


def drawn_draw(key):
    base_key = jax.random.fold_in(key, 29)
    key_query, key_keys, key_values = jax.random.split(base_key, 3)
    shape_query = (SEQUENCE_COUNT, SEQUENCE_LENGTH, QUERY_HEADS, HEAD_SIZE)
    key_tensor_shape = (SEQUENCE_COUNT, SEQUENCE_LENGTH, KEYVALUE_HEADS, HEAD_SIZE)
    query_vals = jnp.clip(jax.random.normal(key_query, shape_query, jnp.float32), -5.0, 5.0)
    key_vals = jnp.clip(jax.random.normal(key_keys, key_tensor_shape, jnp.float32), -5.0, 5.0)
    value_vals = jnp.clip(jax.random.normal(key_values, key_tensor_shape, jnp.float32), -5.0, 5.0)
    return (query_vals, key_vals, value_vals)


def draw_queries(key, part):
    query_vals, key_vals, value_vals = drawn_draw(key)
    return query_vals.reshape(SEQUENCE_COUNT, SEQUENCE_LENGTH, QUERY_HEADS * HEAD_SIZE).astype(jnp.bfloat16)


def draw_keyvals(key, part):
    query_vals, key_vals, value_vals = drawn_draw(key)
    return jnp.concatenate([key_vals, value_vals], axis=-1).astype(jnp.bfloat16)


def draw_router(key, part):
    key_noise = jax.random.fold_in(jax.random.fold_in(key, 43), 0)
    values = jnp.clip(jax.random.normal(key_noise, (D, EXPERTS), jnp.float32), -5.0, 5.0) * D ** (-0.5)
    return values.astype(jnp.bfloat16)


def draw_stream(key, part):
    key_noise = jax.random.fold_in(jax.random.fold_in(key, 47), 0)
    shape_stream = (SEQUENCE_COUNT, SEQUENCE_LENGTH, D)
    values = jnp.clip(jax.random.normal(key_noise, shape_stream, jnp.float32), -6.0, 6.0)
    return values.astype(jnp.bfloat16)


def shard_levels(rng, dims, cuts, smallest, high):
    factor_of, own = 1.0, jax.random.fold_in(rng, 6)
    for axis_at, shards_of in cuts:
        steps = jnp.exp(jax.random.uniform(jax.random.fold_in(own, axis_at), (shards_of,), jnp.float32, smallest / len(cuts), high / len(cuts)))
        factor_of = factor_of * jnp.repeat(steps, dims[axis_at] // shards_of).reshape([-1 if axis == axis_at else 1 for axis in range(len(dims))])
    return factor_of


def routed_block(stream_key, own, number, rows, number_of, top, most, slope):
    ranking = jax.random.permutation(stream_key, number_of)
    heavy_load, usual = portions_of(number_of, rows * top, most, slope, True), portions_of(number_of, rows * top, most, slope, False)
    places = jnp.arange(number_of)

    def named(sizes, offset_by):
        used = int((sizes > 0).sum())
        fixed = max(1, used // 4)
        moved = fixed + (places - fixed + offset_by * (used - fixed)) % max(1, number_of - fixed)
        return jnp.zeros((number_of,), jnp.int32).at[ranking[jnp.where(places < fixed, places, moved)]].set(jnp.asarray(sizes, jnp.int32))

    sizes = jnp.where(number % 4 == 0, named(heavy_load, number // 4), named(usual, number - number // 4 - 1))
    mixed = jax.random.permutation(jax.random.fold_in(own, 3), number_of)
    source_of, sink = mixed[0:number_of // 2 * 2:2], mixed[1:number_of // 2 * 2:2]
    room = jnp.minimum(sizes[source_of] - 1, most - sizes[sink]) // 2
    room = jnp.where((source_of == ranking[0]) | (sink == ranking[0]) | (sizes[sink] == 0), 0, jnp.maximum(room, 0))
    moved = jax.random.randint(jax.random.fold_in(own, 4), (number_of // 2,), 0, 1 << 20) % (room + 1)
    sizes = sizes.at[source_of].add(-moved).at[sink].add(moved)
    members = jnp.searchsorted(jnp.cumsum(sizes), jnp.arange(rows * top), side="right").astype(jnp.int32)
    listing = members.reshape(top, rows).T
    listing = listing[jax.random.permutation(jax.random.fold_in(own, 1), rows)]
    offset_by = jax.random.randint(jax.random.fold_in(own, 2), (rows, 1), 0, top)
    return jnp.take_along_axis(listing, (jnp.arange(top)[None, :] + offset_by) % top, axis=1)


def portions_of(count, total, most, skew, full):
    loads = [(1 << 20) // math.isqrt(grade ** skew) + 1 for grade in range(1, count + 1)]
    largest = most if full else min(most, max(-(-total // count), total * loads[0] // sum(loads)))
    least = 1 if total - largest >= count - 1 else 0
    holding, spare = [largest] + [least] * (count - 1), total - largest - least * (count - 1)
    while spare > 0:
        free = [i for i in range(1, count) if holding[i] < largest] or [i for i in range(1, count) if holding[i] < most]
        pool, budget = sum([loads[i] for i in free]), spare
        for i in free:
            addition = min(most - holding[i], max(1, budget * loads[i] // pool), spare)
            holding[i] = holding[i] + addition
            spare = spare - addition
    return np.array(holding)


def scatter_about(rng, dims, spread, most, cuts=(), kind=jnp.bfloat16):
    level = shard_levels(rng, dims, cuts, -0.22, 0.18) if cuts else 1.0
    drawn = jax.random.normal(rng, dims, jnp.float32) * spread * level
    return jnp.minimum(jnp.maximum(drawn, -most), most).astype(kind)


def setup_inputs(seed: int = 0) -> dict:
    key_of = jax.random.split(jax.random.key(seed), 11)
    queries = draw_queries(jax.random.fold_in(key_of[10], 71), 0)
    keyvals = draw_keyvals(jax.random.fold_in(key_of[10], 71), 0)
    sinks = jnp.clip(-1.0 + 4.0 * jax.random.uniform(key_of[2], (QUERY_HEADS,), jnp.float32) ** shard_levels(key_of[2], (QUERY_HEADS,), ((0, 4),), -0.2, 0.2), -1.0, 3.0)
    stream = draw_stream(jax.random.fold_in(key_of[10], 71), 0)
    out_weight = scatter_about(key_of[4], (QUERY_HEADS * HEAD_SIZE, D), HEAD_SIZE ** -0.5, 0.75, ((0, 4), (1, 4)))
    norm_gain = jnp.clip(1.0 + 0.18 * jax.random.normal(key_of[5], (D,), jnp.float32), 0.1, 1.9)
    router = draw_router(jax.random.fold_in(key_of[10], 71), 0)
    expert_ids_keys = jax.random.split(jax.random.fold_in(key_of[7], 1), SEQUENCE_COUNT * SEQUENCE_LENGTH // BLOCK)
    expert_ids_turns = jax.random.permutation(jax.random.fold_in(key_of[7], 3), SEQUENCE_COUNT * SEQUENCE_LENGTH // BLOCK)
    expert_ids = jax.vmap(lambda own, number: routed_block(jax.random.fold_in(key_of[7], 2), own, number, BLOCK, EXPERTS, TOPK, CAP, 2))(expert_ids_keys, expert_ids_turns).reshape((SEQUENCE_COUNT, SEQUENCE_LENGTH, TOPK))
    w_gate_up = scatter_about(key_of[8], (2 * EXPERTS, H // 2, 2 * D), D ** -0.5, 0.109375, ((0, 4), (1, 4)))
    w_down = scatter_about(key_of[9], (2 * EXPERTS, H // 2, D), H ** -0.5, 0.15625, ((0, 4), (2, 4)))
    return {"queries": queries, "keyvals": keyvals, "sinks": sinks, "stream": stream, "out_weight": out_weight, "norm_gain": norm_gain, "router": router, "expert_ids": expert_ids, "w_gate_up": w_gate_up, "w_down": w_down}


def attend_sequence(query_seq, keyval_seq, sinks):
    length = query_seq.shape[0]
    query_heads = query_seq.reshape(length, QUERY_HEADS, HEAD_SIZE)
    key_heads = keyval_seq[:, :, :HEAD_SIZE]
    value_heads = keyval_seq[:, :, HEAD_SIZE:]
    query_group_size = QUERY_HEADS // KEYVALUE_HEADS
    causal = jnp.arange(length)[None, :] <= jnp.arange(length)[:, None]

    def one_head(head_index):
        query_mat = lax.dynamic_index_in_dim(query_heads, head_index, 1, keepdims=False)
        kv_index = head_index // query_group_size
        key_mat = lax.dynamic_index_in_dim(key_heads, kv_index, 1, keepdims=False)
        value_mat = lax.dynamic_index_in_dim(value_heads, kv_index, 1, keepdims=False)
        scores = jnp.dot(query_mat, key_mat.T, preferred_element_type=jnp.float32) * HEAD_SIZE ** (-0.5)
        sink_value = lax.dynamic_index_in_dim(sinks, head_index, 0, keepdims=False)
        peak = jnp.maximum(sink_value, lax.optimization_barrier(jnp.max(jnp.where(causal, scores, -jnp.inf), axis=-1)))
        exp_terms = jnp.where(causal, jnp.exp(scores - peak[:, None]), 0.0)
        total = jnp.exp(sink_value - peak) + lax.optimization_barrier(jnp.sum(exp_terms, axis=-1))
        weighted = jnp.dot(exp_terms.astype(jnp.bfloat16), value_mat, preferred_element_type=jnp.float32)
        return (weighted / total[:, None]).astype(jnp.bfloat16)
    heads_out = lax.map(one_head, jnp.arange(QUERY_HEADS, dtype=jnp.int32))
    return jnp.transpose(heads_out, (1, 0, 2)).reshape(length, QUERY_HEADS * HEAD_SIZE)

def reference(queries, keyvals, sinks, stream, out_weight, norm_gain, router, expert_ids, w_gate_up, w_down):
    attended = jnp.stack([attend_sequence(queries[seq_index], keyvals[seq_index], sinks) for seq_index in range(SEQUENCE_COUNT)])
    flat_attended = attended.reshape(SEQUENCE_COUNT * SEQUENCE_LENGTH, QUERY_HEADS * HEAD_SIZE)
    projected = jnp.dot(flat_attended, out_weight, preferred_element_type=jnp.float32)
    hidden_state = (stream.reshape(SEQUENCE_COUNT * SEQUENCE_LENGTH, D).astype(jnp.float32) + projected).astype(jnp.bfloat16)
    state_float = hidden_state.astype(jnp.float32)
    inverse = lax.rsqrt(lax.optimization_barrier(jnp.mean(state_float * state_float, axis=-1, keepdims=True)) + 1e-05)
    normed = (state_float * inverse * norm_gain).astype(jnp.bfloat16)
    logits = jnp.dot(normed, router, preferred_element_type=jnp.float32)
    chosen_ids = expert_ids.reshape(SEQUENCE_COUNT * SEQUENCE_LENGTH, TOPK)
    chosen = jnp.take_along_axis(logits, chosen_ids, axis=1)
    mix_weights = jax.nn.softmax(chosen, axis=-1)
    bound = SEQUENCE_COUNT * SEQUENCE_LENGTH // BLOCK * CAP
    pair_experts = chosen_ids.reshape(-1)
    pair_mix = mix_weights.reshape(-1)

    def one_row(running, weight_row):
        expert = weight_row // 2
        is_member = pair_experts == expert
        picked = jnp.nonzero(is_member, size=bound, fill_value=0)[0].astype(jnp.int32)
        member_count = jnp.sum(is_member.astype(jnp.int32))
        valid = jnp.arange(bound, dtype=jnp.int32) < member_count
        token_rows = picked // TOPK
        inputs = normed[token_rows]
        weights_in = lax.dynamic_index_in_dim(w_gate_up, weight_row, 0, keepdims=False).reshape(H // 2, 2, D)
        gate_part = jnp.dot(inputs, weights_in[:, 0, :].T, preferred_element_type=jnp.float32)
        up_part = jnp.dot(inputs, weights_in[:, 1, :].T, preferred_element_type=jnp.float32)
        active = (gate_part * jax.nn.sigmoid(1.702 * gate_part) * (up_part + 1.0)).astype(jnp.bfloat16)
        weights_out = lax.dynamic_index_in_dim(w_down, weight_row, 0, keepdims=False)
        part_out = jnp.dot(active, weights_out, preferred_element_type=jnp.float32).astype(jnp.bfloat16)
        scale = jnp.where(valid, pair_mix[picked], 0.0)
        running = running.at[token_rows].add(scale[:, None] * part_out.astype(jnp.float32))
        return (running, None)
    experts_out, unused = lax.scan(one_row, jnp.zeros((SEQUENCE_COUNT * SEQUENCE_LENGTH, D), jnp.float32), jnp.arange(2 * EXPERTS, dtype=jnp.int32))
    layer_out = (state_float + experts_out).astype(jnp.bfloat16)
    return layer_out.reshape(SEQUENCE_COUNT, SEQUENCE_LENGTH, D)
```

```python
import functools

import jax
import jax.numpy as jnp
from jax import lax
from jax.experimental import pallas as pl
from jax.experimental.pallas import tpu as pltpu
from jax.sharding import PartitionSpec as P


NT = (((1,), (1,)), ((), ()))
TN = (((0,), (0,)), ((), ()))
LANES = 128


def one_hot_rows(slots, cap, value):
    rows = lax.broadcasted_iota(jnp.int32, (cap, slots.shape[1]), 0)
    return jnp.where(rows == slots, value, 0.0).astype(jnp.bfloat16)


def gate_up_kernel(
    halves,
    units,
    state_ref,
    gain_ref,
    router_ref,
    w_ref,
    slot_ref,
    out_ref,
    logits_ref,
    act_ref,
    xg_ref,
    xu_ref,
):
    step = pl.program_id(1)
    groups, shards, group_rows, cols = state_ref.shape

    @pl.when(step == 0)
    def _():
        for group in range(groups):
            pieces = [state_ref[group, shard].astype(jnp.float32) for shard in range(shards)]
            square = sum(jnp.sum(piece * piece, axis=1, keepdims=True) for piece in pieces)
            inverse = lax.rsqrt(square / (shards * cols) + 1e-05)
            scaled = [
                (piece * inverse * gain_ref[shard]).astype(jnp.bfloat16)
                for shard, piece in enumerate(pieces)
            ]
            extra = xg_ref.shape[1] - shards * cols
            blank = [jnp.zeros((group_rows, extra), jnp.bfloat16)] if extra else []
            here = slice(group * group_rows, (group + 1) * group_rows)
            xg_ref[here, :] = jnp.concatenate(scaled + blank, axis=1)
            xu_ref[here, :] = jnp.concatenate(blank + scaled, axis=1)
        logits_ref[...] = lax.dot_general(
            router_ref[...], xg_ref[...], NT, preferred_element_type=jnp.float32
        )

    rows, wide = w_ref.shape[0], xg_ref.shape[1]
    gate = lax.dot_general(w_ref[:, :wide], xg_ref[...], NT, preferred_element_type=jnp.float32)
    up = lax.dot_general(
        w_ref[:, w_ref.shape[1] - wide :], xu_ref[...], NT, preferred_element_type=jnp.float32
    )
    active = gate * jax.nn.sigmoid(1.702 * gate) * (up + 1.0)
    slabs = act_ref.shape[0]
    for slab in range(slabs):
        act_ref[slab, pl.ds(step * rows, rows), :] = active[:, slab * LANES : (slab + 1) * LANES]

    @pl.when(step == pl.num_programs(1) - 1)
    def _():
        for row in range(halves):
            wanted = pl.ds(row, units, stride=halves) if halves > 1 else pl.ds(0, units)
            picked = jnp.concatenate([act_ref[slab, wanted, :] for slab in range(slabs)], axis=1)
            spread = one_hot_rows(slot_ref[row], out_ref.shape[2], 1.0)
            out_ref[row, 0] = lax.dot_general(
                spread, picked.astype(jnp.bfloat16), NT, preferred_element_type=jnp.float32
            ).astype(jnp.bfloat16)


def gate_up_call(state, gain, router, weights, slots, units, token_block, cap):
    halves = slots.shape[0]
    sources, shards, group_rows, cols = state.shape
    groups = token_block // group_rows
    blocks = sources // groups
    experts, wide = router.shape
    wide_w = weights.shape[1]
    sizes = [
        size
        for size in range(1, units + 1)
        if units % size == 0
        and (size == units or (size * halves) % 16 == 0)
        and size * halves * wide_w * 2 <= 4 << 20
    ]
    size = sizes[-1]
    return pl.pallas_call(
        functools.partial(gate_up_kernel, halves, units),
        grid=(blocks, units // size),
        out_shape=(
            jax.ShapeDtypeStruct((halves, blocks, cap, units), jnp.bfloat16),
            jax.ShapeDtypeStruct((experts, blocks * token_block), jnp.float32),
        ),
        in_specs=[
            pl.BlockSpec((groups, shards, group_rows, cols), lambda i, j: (i, 0, 0, 0)),
            pl.BlockSpec((shards, 1, cols), lambda i, j: (0, 0, 0)),
            pl.BlockSpec((experts, wide), lambda i, j: (0, 0)),
            pl.BlockSpec((size * halves, wide_w), lambda i, j: (j, 0)),
            pl.BlockSpec((halves, 1, token_block), lambda i, j: (0, 0, i)),
        ],
        out_specs=(
            pl.BlockSpec((halves, 1, cap, units), lambda i, j: (0, i, 0, 0)),
            pl.BlockSpec((experts, token_block), lambda i, j: (0, i)),
        ),
        scratch_shapes=[
            pltpu.VMEM((token_block // LANES, units * halves, LANES), jnp.float32),
            pltpu.VMEM((token_block, wide), jnp.bfloat16),
            pltpu.VMEM((token_block, wide), jnp.bfloat16),
        ],
        compiler_params=pltpu.CompilerParams(vmem_limit_bytes=56 << 20),
    )(state, gain, router, weights, slots)


def down_kernel(act_ref, w_ref, slot_ref, mix_ref, out_ref, total_ref):
    step = pl.program_id(1)
    part = None
    for row in range(w_ref.shape[0]):
        pieces = [act_ref[shard, row, 0] for shard in range(act_ref.shape[0])]
        hidden = jnp.concatenate(pieces, axis=1)
        piece = jnp.dot(hidden, w_ref[row], preferred_element_type=jnp.float32)
        part = piece if part is None else part + piece
    spread = one_hot_rows(slot_ref[0], act_ref.shape[3], mix_ref[0])
    added = lax.dot_general(
        spread, part.astype(jnp.bfloat16), TN, preferred_element_type=jnp.float32
    )

    @pl.when(step == 0)
    def _():
        total_ref[...] = added

    @pl.when(step != 0)
    def _():
        total_ref[...] += added

    @pl.when(step == pl.num_programs(1) - 1)
    def _():
        out_ref[...] = total_ref[...].astype(jnp.bfloat16)


def down_call(act, weights, slots, mix, token_block):
    shards, halves, blocks, cap, units = act.shape
    hidden, cols = weights.shape[1:]
    pair = 2 if halves % 2 == 0 else 1
    return pl.pallas_call(
        down_kernel,
        grid=(blocks, halves // pair),
        out_shape=jax.ShapeDtypeStruct((blocks * token_block, cols), jnp.bfloat16),
        in_specs=[
            pl.BlockSpec((shards, pair, 1, cap, units), lambda i, r: (0, r, i, 0, 0)),
            pl.BlockSpec((pair, hidden, cols), lambda i, r: (r, 0, 0)),
            pl.BlockSpec((1, 1, token_block), lambda i, r: (r * pair, 0, i)),
            pl.BlockSpec((1, 1, token_block), lambda i, r: (r * pair, 0, i)),
        ],
        out_specs=pl.BlockSpec((token_block, cols), lambda i, r: (i, 0)),
        scratch_shapes=[pltpu.VMEM((token_block, cols), jnp.float32)],
        compiler_params=pltpu.CompilerParams(vmem_limit_bytes=48 << 20),
    )(act, weights, slots, mix)


MESH = pl.DeviceIdType.MESH
NN = (((1,), (0,)), ((), ()))


def layer_kernel(
    sizes,
    q_ref,
    kv_ref,
    ids_ref,
    sink_ref,
    gain_ref,
    stream_ref,
    ow_hbm,
    router_hbm,
    wg_hbm,
    wd_hbm,
    out_ref,
    kv_all,
    ids_all,
    stream_in,
    ow,
    router,
    wg,
    wd,
    att_all,
    core_out,
    core_in,
    keep,
    x_out,
    x_in,
    h_all,
    y_all,
    pick,
    spread,
    xg,
    scale_ref,
    act_all,
    parts,
    rs_out,
    rs_in,
    local_sem,
    wg_sem,
    wd_sem,
    kv_send,
    kv_recv,
    ids_send,
    ids_recv,
    stream_send,
    stream_recv,
    att_send,
    att_recv,
    core_send,
    core_recv,
    x_send,
    x_recv,
    h_send,
    h_recv,
    act_send,
    act_recv,
    rs_send,
    rs_recv,
):
    seqs, tokens, rows, ctxs, width, cols, cap, local_experts, units, slots = sizes
    c, h, r = lax.axis_index("ctx"), lax.axis_index("head"), lax.axis_index("rep")
    all_rows = ctxs * rows
    wide = y_all.shape[1]
    pad_cols = h_all.shape[3]
    core_dev, x_dev = (c, h ^ 1, r), (c, h ^ 2, r)
    partner = (h, c, r)

    def remote(src, dst, send, recv, device):
        return pltpu.make_async_remote_copy(
            src_ref=src,
            dst_ref=dst,
            send_sem=send,
            recv_sem=recv,
            device_id=device,
            device_id_type=MESH,
        )

    ow_copy = pltpu.make_async_copy(ow_hbm, ow, local_sem.at[0])
    router_copy = pltpu.make_async_copy(router_hbm, router, local_sem.at[1])

    def wg_copy(e, slot):
        return pltpu.make_async_copy(
            wg_hbm.at[pl.ds(2 * e, 2)], wg.at[slot], wg_sem.at[slot]
        )

    def wd_copy(e):
        return pltpu.make_async_copy(
            wd_hbm.at[pl.ds(2 * e, 2)], wd.at[pl.ds(2 * e, 2)], wd_sem.at[e]
        )

    barrier = pltpu.get_barrier_semaphore()
    for step in range(1, ctxs):
        pl.semaphore_signal(
            barrier, inc=1, device_id=(lax.rem(c + step, ctxs), h, r), device_id_type=MESH
        )
    pl.semaphore_signal(barrier, inc=1, device_id=core_dev, device_id_type=MESH)
    pl.semaphore_signal(barrier, inc=1, device_id=x_dev, device_id_type=MESH)

    @pl.when(c != h)
    def _():
        pl.semaphore_signal(barrier, inc=1, device_id=partner, device_id_type=MESH)

    ow_copy.start()
    for e in range(min(slots, local_experts)):
        wg_copy(e, e).start()
    router_copy.start()
    for e in range(local_experts):
        wd_copy(e).start()
    own_ids = ids_ref[...].reshape(rows, ids_ref.shape[2]).astype(jnp.float32)
    topk = ids_ref.shape[2]
    padded_ids = jnp.concatenate(
        [own_ids, jnp.full((rows, LANES - topk), -1.0, jnp.float32)], axis=1
    )
    ids_all[c] = jnp.transpose(padded_ids)[:8]
    kv_all[c] = kv_ref[...]
    for other in range(ctxs):

        @pl.when(other > c)
        def _():
            kv_all[other] = jnp.zeros(kv_all.shape[1:], jnp.bfloat16)

    parts[...] = jnp.zeros(parts.shape, jnp.bfloat16)
    pl.semaphore_wait(barrier, ctxs + 1 + (c != h).astype(jnp.int32))

    def kv_copy(src, dst):
        return remote(
            kv_all.at[src], kv_all.at[src], kv_send.at[dst], kv_recv.at[src], (dst, h, r)
        )

    def ids_copy(src, dst):
        return remote(
            ids_all.at[src], ids_all.at[src], ids_send.at[dst], ids_recv.at[src], (dst, h, r)
        )

    def att_copy(src, dst):
        return remote(
            att_all.at[src], att_all.at[src], att_send.at[dst], att_recv.at[src], (dst, h, r)
        )

    for dst in range(ctxs):

        @pl.when(dst > c)
        def _():
            kv_copy(c, dst).start()

    stream_copy = remote(
        stream_ref, stream_in, stream_send.at[0], stream_recv.at[0], partner
    )
    stream_local = pltpu.make_async_copy(stream_ref, stream_in, local_sem.at[2])

    @pl.when(c != h)
    def _():
        stream_copy.start()

    @pl.when(c == h)
    def _():
        stream_local.start()

    for dst in range(ctxs):

        @pl.when(dst != c)
        def _():
            ids_copy(c, dst).start()

    for src in range(ctxs):

        @pl.when(src < c)
        def _():
            kv_copy(src, c).wait_recv()

    pairs = q_ref.shape[2] // LANES
    half = LANES // 2
    keys = ctxs * tokens
    group = pairs * tokens
    low_k = lax.broadcasted_iota(jnp.int32, (keys, LANES), 1) < half
    low_q = lax.broadcasted_iota(jnp.int32, (group, LANES), 1) < half
    key_pos = lax.broadcasted_iota(jnp.int32, (group, keys), 1)
    row_pos = lax.rem(lax.broadcasted_iota(jnp.int32, (group, keys), 0), tokens)
    visible = key_pos <= row_pos + c * tokens
    for s in range(seqs):
        kv = jnp.concatenate([kv_all[src, s] for src in range(ctxs)], axis=0).astype(jnp.float32)
        turned = pltpu.roll(kv, half, 1)
        key_sides = [jnp.where(low_k, kv, 0.0), jnp.where(low_k, 0.0, turned)]
        value_sides = [jnp.where(low_k, turned, 0.0), jnp.where(low_k, 0.0, kv)]
        q = jnp.concatenate(
            [q_ref[s, :, p * LANES : (p + 1) * LANES] for p in range(pairs)], axis=0
        )
        acc, totals = None, []
        for side in range(2):
            sink = jnp.concatenate(
                [
                    jnp.full((tokens, 1), sink_ref[2 * p + side], jnp.float32)
                    for p in range(pairs)
                ],
                axis=0,
            )
            scores = lax.dot_general(
                q, key_sides[side].astype(jnp.bfloat16), NT, preferred_element_type=jnp.float32
            ) * (half ** (-0.5))
            scores = jnp.where(visible, scores, -1e30)
            peak = jnp.maximum(sink, jnp.max(scores, axis=1, keepdims=True))
            terms = jnp.where(visible, jnp.exp(scores - peak), 0.0)
            totals.append(jnp.exp(sink - peak) + jnp.sum(terms, axis=1, keepdims=True))
            piece = lax.dot_general(
                terms.astype(jnp.bfloat16),
                value_sides[side].astype(jnp.bfloat16),
                NN,
                preferred_element_type=jnp.float32,
            )
            acc = piece if acc is None else acc + piece
        attended = (acc / jnp.where(low_q, totals[0], totals[1])).astype(jnp.bfloat16)
        for p in range(pairs):
            att_all[c, s * tokens : (s + 1) * tokens, p * LANES : (p + 1) * LANES] = attended[
                p * tokens : (p + 1) * tokens
            ]
    for dst in range(ctxs):

        @pl.when(dst != c)
        def _():
            att_copy(c, dst).start()

    for src in range(ctxs):

        @pl.when(src != c)
        def _():
            ids_copy(src, c).wait_recv()

    ids_row = jnp.concatenate([ids_all[src] for src in range(ctxs)], axis=1)
    mine = (
        lax.broadcasted_iota(jnp.int32, (local_experts, all_rows), 0) + c * local_experts
    ).astype(jnp.float32)
    member = jnp.zeros((local_experts, all_rows), jnp.bool_)
    for k in range(topk):
        member = member | (mine == ids_row[k : k + 1])
    before = lax.broadcasted_iota(jnp.int32, (all_rows, all_rows), 0) <= lax.broadcasted_iota(
        jnp.int32, (all_rows, all_rows), 1
    )
    rank = lax.dot_general(
        jnp.where(member, 1.0, 0.0).astype(jnp.bfloat16),
        jnp.where(before, 1.0, 0.0).astype(jnp.bfloat16),
        NN,
        preferred_element_type=jnp.float32,
    )
    slot_row = jnp.where(member, rank - 1.0, -1.0)
    slot_rows = lax.broadcasted_iota(jnp.int32, (cap, all_rows), 0).astype(jnp.float32)
    for e in range(local_experts):
        pick[e * cap : (e + 1) * cap, :] = jnp.where(
            slot_rows == slot_row[e : e + 1], 1.0, 0.0
        ).astype(jnp.bfloat16)
    both = jnp.concatenate(
        [ids_row, slot_row, jnp.zeros((LANES - 8 - local_experts, all_rows), jnp.float32)], axis=0
    )
    by_token = jnp.transpose(both)

    ow_copy.wait()
    side, core = h // 2, lax.rem(h, 2)

    def projected(block):
        @pl.when(block != c)
        def _():
            att_copy(block, c).wait_recv()

        out = lax.dot_general(att_all[block], ow[...], NN, preferred_element_type=jnp.float32)
        return jnp.concatenate(
            [out, jnp.zeros((rows, pad_cols - cols), jnp.float32)], axis=1
        )

    def core_copy(i):
        return remote(core_out.at[i], core_in.at[i], core_send.at[i], core_recv.at[i], core_dev)

    for i in range(2):
        across = (1 - side) if i == 0 else side
        core_out[i] = projected(2 * across + 1 - core).astype(jnp.bfloat16)
        core_copy(i).start()
    for i in range(2):
        across = (1 - side) if i == 0 else side
        keep[i] = projected(2 * across + core)
    core_copy(0).wait_recv()
    x_out[...] = (keep[0] + core_in[0].astype(jnp.float32)).astype(jnp.bfloat16)
    x_copy = remote(x_out, x_in, x_send.at[0], x_recv.at[0], x_dev)
    x_copy.start()

    @pl.when(c != h)
    def _():
        stream_copy.wait_recv()

    @pl.when(c == h)
    def _():
        stream_local.wait()

    core_copy(1).wait_recv()
    turned_stream = stream_in[...].reshape(rows, cols).astype(jnp.float32)
    kept = (
        keep[1]
        + core_in[1].astype(jnp.float32)
        + jnp.concatenate(
            [turned_stream, jnp.zeros((rows, pad_cols - cols), jnp.float32)], axis=1
        )
    )
    x_copy.wait_recv()
    h_all[c, h] = (kept + x_in[...].astype(jnp.float32)).astype(jnp.bfloat16)

    def h_copy(way, block, row, device):
        return remote(
            h_all.at[block, row],
            h_all.at[block, row],
            h_send.at[way, block],
            h_recv.at[block, row],
            device,
        )

    def h_core(block, row):
        return h_copy(jnp.where(row == h, 0, 1), block, row, core_dev)

    def h_x(block):
        return h_copy(2, block, h, x_dev)

    def h_right(block):
        return h_copy(3, block, h, (jnp.minimum(c + 1, ctxs - 1), h, r))

    def h_left(block):
        return h_copy(4, block, h, (jnp.maximum(c - 1, 0), h, r))

    def arrived(block, row):
        h_copy(0, block, row, core_dev).wait_recv()

    h_x(c).start()

    @pl.when(c < ctxs - 1)
    def _():
        h_right(c).start()

    @pl.when(c > 0)
    def _():
        h_left(c).start()

    h_core(c, h).start()
    for d in range(1, ctxs + 1):

        @pl.when(c - d >= 0)
        def _():
            arrived(c - d, h)

            @pl.when(c < ctxs - 1)
            def _():
                h_right(c - d).start()

            h_x(c - d).start()
            h_core(c - d, h).start()

        @pl.when(c + d < ctxs)
        def _():
            arrived(c + d, h)

            @pl.when(c > 0)
            def _():
                h_left(c + d).start()

            h_x(c + d).start()
            h_core(c + d, h).start()

        @pl.when(c - (d - 1) >= 0)
        def _():
            arrived(c - (d - 1), h ^ 2)
            h_core(c - (d - 1), h ^ 2).start()

        if d > 1:

            @pl.when(c + (d - 1) < ctxs)
            def _():
                arrived(c + (d - 1), h ^ 2)
                h_core(c + (d - 1), h ^ 2).start()

    for block in range(ctxs):
        arrived(block, h ^ 1)
        arrived(block, h ^ 3)

    gain = gain_ref[...]
    squares = []
    for row in range(ctxs):
        pieces = [h_all[block, row].astype(jnp.float32)[:, :cols] for block in range(ctxs)]
        squares.append(sum(jnp.sum(piece * piece, axis=1, keepdims=True) for piece in pieces))
        flat = jnp.concatenate(pieces, axis=1) * gain
        y_all[row * rows : (row + 1) * rows, :] = jnp.concatenate(
            [flat, jnp.zeros((rows, wide - width), jnp.float32)], axis=1
        ).astype(jnp.bfloat16)
    inverse = lax.rsqrt(jnp.concatenate(squares, axis=0) / width + 1e-05)
    router_copy.wait()
    logits = lax.dot_general(
        y_all[:, :width], router[...], NN, preferred_element_type=jnp.float32
    ) * inverse
    experts = router.shape[1]
    expert_lane = lax.broadcasted_iota(jnp.int32, (all_rows, experts), 1).astype(jnp.float32)
    named = jnp.zeros((all_rows, experts), jnp.bool_)
    for k in range(topk):
        named = named | (expert_lane == by_token[:, k : k + 1])
    top = jnp.max(jnp.where(named, logits, -1e30), axis=1, keepdims=True)
    weight = jnp.where(named, jnp.exp(logits - top), 0.0)
    mix = weight / jnp.sum(weight, axis=1, keepdims=True)
    mix = jnp.concatenate([mix, jnp.zeros((all_rows, LANES - experts), jnp.float32)], axis=1)
    mix = pltpu.roll(mix, lax.rem(LANES - c * local_experts, LANES), 1)
    slot_lane = lax.broadcasted_iota(jnp.int32, (all_rows, LANES), 1).astype(jnp.float32)
    for e in range(local_experts):
        spread[:, e * LANES : (e + 1) * LANES] = jnp.where(
            slot_lane == by_token[:, 8 + e : 9 + e], mix[:, e : e + 1], 0.0
        ).astype(jnp.bfloat16)

    inverse_row = jnp.transpose(jnp.broadcast_to(inverse, (all_rows, LANES)))[:8]
    first = inverse_row.astype(jnp.bfloat16)
    rest = inverse_row - first.astype(jnp.float32)
    second = rest.astype(jnp.bfloat16)
    third = (rest - second.astype(jnp.float32)).astype(jnp.bfloat16)
    for e in range(local_experts):
        here = pick[e * cap : (e + 1) * cap, :]
        scale_ref[e] = sum(
            lax.dot_general(part, here, NT, preferred_element_type=jnp.float32)
            for part in (first, second, third)
        )

    @pl.loop(0, wide // LANES)
    def _(j):
        at = pl.multiple_of(j * LANES, LANES)
        xg[:, pl.ds(at, LANES)] = lax.dot_general(
            pick[...], y_all[:, pl.ds(at, LANES)], NN, preferred_element_type=jnp.float32
        ).astype(jnp.bfloat16)

    def act_core(shard, e):
        return remote(
            act_all.at[shard, e],
            act_all.at[shard, e],
            act_send.at[jnp.where(shard == h, 0, 1), e],
            act_recv.at[shard, e],
            core_dev,
        )

    def act_x(e):
        return remote(
            act_all.at[h, e], act_all.at[h, e], act_send.at[2, e], act_recv.at[h, e], x_dev
        )

    def act_arrived(shard, e):
        remote(
            act_all.at[shard, e],
            act_all.at[shard, e],
            act_send.at[0, e],
            act_recv.at[shard, e],
            core_dev,
        ).wait_recv()

    lead = wide - width
    packed = act_all.shape[3]

    @pl.loop(0, local_experts)
    def _(e):
        slot = lax.rem(e, slots)
        wg_copy(e, slot).wait()
        rows_in = xg[pl.ds(pl.multiple_of(e * cap, cap), cap), :]
        shifted = jnp.concatenate(
            [jnp.zeros((cap, lead), jnp.bfloat16), rows_in[:, :width]], axis=1
        )
        factor = scale_ref[e][:1]
        active = []
        for u in range(2):
            gate = factor * lax.dot_general(
                wg[slot, u, :, :wide], rows_in, NT, preferred_element_type=jnp.float32
            )
            up = factor * lax.dot_general(
                wg[slot, u, :, 2 * width - wide :],
                shifted,
                NT,
                preferred_element_type=jnp.float32,
            )
            active.append(gate * jax.nn.sigmoid(1.702 * gate) * (up + 1.0))
        stacked = jnp.concatenate(
            active + [jnp.zeros((packed - 2 * units, cap), jnp.float32)], axis=0
        )
        stacked = jnp.concatenate(
            [stacked, jnp.zeros((packed, LANES - cap), jnp.float32)], axis=1
        )
        act_all[h, e] = jnp.transpose(stacked)[:cap].astype(jnp.bfloat16)
        act_x(e).start()
        act_core(h, e).start()

        @pl.when(e + slots < local_experts)
        def _():
            wg_copy(e + slots, slot).start()

        @pl.when(e >= 2)
        def _():
            act_arrived(h ^ 2, e - 2)
            act_core(h ^ 2, e - 2).start()

    for e in range(local_experts - 2, local_experts):
        act_arrived(h ^ 2, e)
        act_core(h ^ 2, e).start()

    @pl.loop(0, local_experts)
    def _(e):
        wd_copy(e).wait()
        act_arrived(h ^ 1, e)
        act_arrived(h ^ 3, e)
        total = None
        for u in range(2):
            hidden = jnp.concatenate(
                [act_all[shard, e][:, u * units : (u + 1) * units] for shard in range(4)], axis=1
            )
            piece = lax.dot_general(
                hidden, wd[2 * e + u], NN, preferred_element_type=jnp.float32
            )
            total = piece if total is None else total + piece
        parts[pl.ds(pl.multiple_of(e * LANES, LANES), cap), :] = jnp.concatenate(
            [total, jnp.zeros((cap, pad_cols - cols), jnp.float32)], axis=1
        ).astype(jnp.bfloat16)

    def rs_copy(src, dst):
        return remote(rs_out.at[dst], rs_in.at[src], rs_send.at[dst], rs_recv.at[src], (dst, h, r))

    def combined(block):
        return lax.dot_general(
            spread[pl.ds(pl.multiple_of(block * rows, rows), rows), :],
            parts[...],
            NN,
            preferred_element_type=jnp.float32,
        )

    for d in range(1, ctxs):
        dst = lax.rem(c + d, ctxs)
        rs_out[dst] = combined(dst).astype(jnp.bfloat16)
        rs_copy(c, dst).start()
    total = combined(c) + h_all[h, c].astype(jnp.float32)
    for d in range(1, ctxs):
        src = lax.rem(c + d, ctxs)
        rs_copy(src, c).wait_recv()
        total = total + rs_in[src].astype(jnp.float32)
    out_ref[...] = total[:, :cols].astype(jnp.bfloat16).reshape(out_ref.shape)

    for dst in range(ctxs):

        @pl.when(dst > c)
        def _():
            kv_copy(c, dst).wait_send()

        @pl.when(dst != c)
        def _():
            ids_copy(c, dst).wait_send()
            att_copy(c, dst).wait_send()
            rs_copy(c, dst).wait_send()

    @pl.when(c != h)
    def _():
        stream_copy.wait_send()

    x_copy.wait_send()
    for i in range(2):
        core_copy(i).wait_send()
    for block in range(ctxs):
        h_x(block).wait_send()
        h_core(block, h).wait_send()
        h_core(block, h ^ 2).wait_send()

        @pl.when((c < ctxs - 1) & (block <= c))
        def _():
            h_right(block).wait_send()

        @pl.when((c > 0) & (block >= c))
        def _():
            h_left(block).wait_send()

    for e in range(local_experts):
        act_x(e).wait_send()
        act_core(h, e).wait_send()
        act_core(h ^ 2, e).wait_send()


def layer_call(queries, keyvals, sinks, stream, out_weight, gain, router, ids, w_gate_up, w_down):
    seqs, tokens, q_cols = queries.shape
    cols = stream.shape[2]
    ctxs = lax.axis_size("ctx")
    rows = seqs * tokens
    width = gain.shape[0]
    halves, units, wide_w = w_gate_up.shape
    local_experts = halves // 2
    all_rows = ctxs * rows
    cap = all_rows * 3 // 16
    wide = pl.cdiv(width, LANES) * LANES
    pad_cols = pl.cdiv(cols, LANES) * LANES
    packed = pl.cdiv(2 * units, LANES) * LANES
    slots = min(4, local_experts)
    sizes = (seqs, tokens, rows, ctxs, width, cols, cap, local_experts, units, slots)
    bf16, f32 = jnp.bfloat16, jnp.float32
    dma = pltpu.SemaphoreType.DMA
    vmem = pl.BlockSpec(memory_space=pltpu.VMEM)
    hbm = pl.BlockSpec(memory_space=pl.ANY)
    return pl.pallas_call(
        functools.partial(layer_kernel, sizes),
        out_shape=jax.ShapeDtypeStruct((seqs, tokens, cols), bf16),
        in_specs=[vmem, vmem, vmem, pl.BlockSpec(memory_space=pltpu.SMEM), vmem, vmem]
        + [hbm] * 4,
        out_specs=vmem,
        scratch_shapes=[
            pltpu.VMEM((ctxs, seqs, tokens, keyvals.shape[3]), bf16),
            pltpu.VMEM((ctxs, 8, LANES), f32),
            pltpu.VMEM((seqs, tokens, cols), bf16),
            pltpu.VMEM(out_weight.shape, bf16),
            pltpu.VMEM(router.shape, bf16),
            pltpu.VMEM((slots, 2, units, wide_w), bf16),
            pltpu.VMEM(w_down.shape, bf16),
            pltpu.VMEM((ctxs, rows, q_cols), bf16),
            pltpu.VMEM((2, rows, pad_cols), bf16),
            pltpu.VMEM((2, rows, pad_cols), bf16),
            pltpu.VMEM((2, rows, pad_cols), f32),
            pltpu.VMEM((rows, pad_cols), bf16),
            pltpu.VMEM((rows, pad_cols), bf16),
            pltpu.VMEM((ctxs, 4, rows, pad_cols), bf16),
            pltpu.VMEM((all_rows, wide), bf16),
            pltpu.VMEM((local_experts * cap, all_rows), bf16),
            pltpu.VMEM((all_rows, local_experts * LANES), bf16),
            pltpu.VMEM((local_experts * cap, wide), bf16),
            pltpu.VMEM((local_experts, 8, cap), f32),
            pltpu.VMEM((4, local_experts, cap, packed), bf16),
            pltpu.VMEM((local_experts * LANES, pad_cols), bf16),
            pltpu.VMEM((ctxs, rows, pad_cols), bf16),
            pltpu.VMEM((ctxs, rows, pad_cols), bf16),
            dma((3,)),
            dma((slots,)),
            dma((local_experts,)),
            dma((ctxs,)),
            dma((ctxs,)),
            dma((ctxs,)),
            dma((ctxs,)),
            dma((1,)),
            dma((1,)),
            dma((ctxs,)),
            dma((ctxs,)),
            dma((2,)),
            dma((2,)),
            dma((1,)),
            dma((1,)),
            dma((5, ctxs)),
            dma((ctxs, 4)),
            dma((3, local_experts)),
            dma((4, local_experts)),
            dma((ctxs,)),
            dma((ctxs,)),
        ],
        compiler_params=pltpu.CompilerParams(
            vmem_limit_bytes=67043328, collective_id=0, has_side_effects=True
        ),
    )(
        queries,
        keyvals.reshape(seqs, tokens, keyvals.shape[3]),
        ids,
        sinks,
        gain.reshape(1, width),
        stream,
        out_weight,
        router,
        w_gate_up,
        w_down,
    )


def one_chip_row(queries, keyvals, stream, out_weight, router, ids, w_gate_up):
    ctxs, heads = lax.axis_size("ctx"), lax.axis_size("head")
    rows = queries.shape[0] * queries.shape[1]
    return (
        ctxs == heads == 4
        and rows == LANES
        and keyvals.shape[2] == 1
        and keyvals.shape[3] == LANES
        and out_weight.shape[1] == stream.shape[2]
        and w_gate_up.shape[0] == 16
        and ids.shape[2] <= 8
        and router.shape[1] <= LANES
    )


def on_device(
    queries, keyvals, sinks, stream, out_weight, norm_gain, router, expert_ids, w_gate_up, w_down
):
    if one_chip_row(queries, keyvals, stream, out_weight, router, expert_ids, w_gate_up):
        return layer_call(
            queries,
            keyvals,
            sinks,
            stream,
            out_weight,
            norm_gain,
            router,
            expert_ids,
            w_gate_up,
            w_down,
        )
    ctx_count = lax.axis_size("ctx")
    local_seqs = queries.shape[0]
    tokens = queries.shape[1]
    row_count = local_seqs * tokens
    kv_local = keyvals.shape[2]
    head_dim = keyvals.shape[3] // 2
    q_local = queries.shape[2] // head_dim
    query_group_size = q_local // kv_local
    wide_rows = query_group_size * tokens
    col_width = stream.shape[2]
    first_pos = lax.axis_index("ctx") * tokens
    last_pos = first_pos + tokens - 1
    score_scale = head_dim ** (-0.5)
    scaled_queries = queries * jnp.asarray(score_scale, jnp.bfloat16)
    query_grid = scaled_queries.reshape(local_seqs, tokens, kv_local, query_group_size, head_dim)
    query_wide = jnp.transpose(query_grid, (0, 2, 3, 1, 4)).reshape(
        local_seqs, kv_local, wide_rows, head_dim
    )
    positions = first_pos + jnp.tile(jnp.arange(tokens), query_group_size)
    sink_rows = jnp.repeat(sinks.reshape(kv_local, query_group_size), tokens, axis=1)
    sink_grid = jnp.broadcast_to(sink_rows[None], (local_seqs, kv_local, wide_rows))
    start_state = (
        sink_grid,
        jnp.ones_like(sink_grid),
        jnp.zeros((local_seqs, kv_local, head_dim, wide_rows), jnp.float32),
    )

    def attend_block(running, shard_piece):
        peak_old, denom_old, accum_old = running
        key_block = shard_piece[..., :head_dim]
        value_block = shard_piece[..., head_dim:]
        scores = jnp.einsum(
            "skmd,snkd->sknm", query_wide, key_block, preferred_element_type=jnp.float32
        )
        key_pos = jnp.arange(shard_piece.shape[1])
        visible = key_pos[:, None] <= positions[None, :]
        masked = jnp.where(visible[None, None], scores, -jnp.inf)
        peak_new = jnp.maximum(peak_old, jnp.max(masked, axis=2))
        exp_terms = jnp.exp(masked - peak_new[:, :, None, :])
        factor = jnp.exp(peak_old - peak_new)
        denom_new = denom_old * factor + jnp.sum(exp_terms, axis=2)
        accum_new = accum_old * factor[:, :, None, :] + jnp.einsum(
            "sknm,snkd->skdm",
            exp_terms.astype(jnp.bfloat16),
            value_block,
            preferred_element_type=jnp.float32,
        )
        return (peak_new, denom_new, accum_new)

    shard_piece = lax.all_gather(keyvals, "ctx", axis=1, tiled=True)

    def keep_state(state_in):
        return state_in

    def update_state(state_in):
        return attend_block(state_in, shard_piece)

    peak_fin, denom_fin, accum_fin = lax.cond(
        jnp.int32(0) > last_pos, keep_state, update_state, start_state
    )
    normalized = (accum_fin / denom_fin[:, :, None, :]).reshape(
        local_seqs, kv_local, head_dim, query_group_size, tokens
    )
    attended = (
        jnp.transpose(normalized, (0, 4, 1, 3, 2))
        .reshape(row_count, q_local * head_dim)
        .astype(jnp.bfloat16)
    )
    token_ids = lax.all_gather(
        expert_ids.reshape(row_count, expert_ids.shape[2]).T, "ctx", axis=1, tiled=True
    )
    all_rows = ctx_count * row_count
    halves = w_gate_up.shape[0]
    units = w_gate_up.shape[1]
    token_block = min(all_rows, 8 * tokens)
    cap = token_block // tokens * (3 * tokens // 16)
    row_expert = (lax.axis_index("ctx") * halves + jnp.arange(halves)) // 2
    named = jnp.any(token_ids[:, None, :] == row_expert[None, :, None], axis=0)
    counted = named.astype(jnp.int32).reshape(halves, all_rows // token_block, token_block)
    rank = jnp.cumsum(counted, axis=2) - 1
    slots = jnp.where(named, rank.reshape(halves, all_rows), -1).reshape(halves, 1, all_rows)
    width = norm_gain.shape[0]
    head_count = lax.axis_size("head")
    swapped = ctx_count == head_count and out_weight.shape[1] == col_width
    if swapped:
        pairs = [
            (first * head_count + second, second * head_count + first)
            for first in range(ctx_count)
            for second in range(head_count)
        ]
        turned = lax.ppermute(
            stream.reshape(row_count, col_width), ("ctx", "head"), perm=pairs
        )
        every_row = lax.all_gather(attended, "ctx", axis=0, tiled=True)
        partial_proj = jnp.dot(every_row, out_weight, preferred_element_type=jnp.float32)
        summed = lax.psum_scatter(
            partial_proj.astype(jnp.bfloat16), "head", scatter_dimension=0, tiled=True
        )
        turned_state = summed.astype(jnp.float32) + turned.astype(jnp.float32)
        every_state = lax.all_gather(
            turned_state.astype(jnp.bfloat16), ("head", "ctx"), axis=0, tiled=False
        )
    else:
        partial_proj = jnp.dot(attended, lax.all_gather(out_weight, "ctx", axis=1, tiled=True), preferred_element_type=jnp.float32)
        own_stream = stream.reshape(row_count, col_width).astype(jnp.float32)
        summed = lax.psum_scatter(
            partial_proj.astype(jnp.bfloat16), "head", scatter_dimension=1, tiled=True
        )
        own_state = (summed.astype(jnp.float32) + own_stream).astype(jnp.bfloat16)
        every_state = lax.all_gather(own_state, ("ctx", "head"), axis=0, tiled=False)
    every_state = every_state.reshape(ctx_count, width // col_width, row_count, col_width)
    expert_count = router.shape[1]
    unit_rows = jnp.transpose(w_gate_up, (1, 0, 2)).reshape(units * halves, w_gate_up.shape[2])
    router_rows = jnp.pad(router.T, ((0, 0), (0, -width % LANES)))
    gain = norm_gain.reshape(width // col_width, 1, col_width)
    active, logits = gate_up_call(
        every_state, gain, router_rows, unit_rows, slots, units, token_block, cap
    )
    member = jnp.any(token_ids[:, None, :] == jnp.arange(expert_count)[None, :, None], axis=0)
    masked = jnp.where(member, logits, -jnp.inf)
    mix_all = jax.nn.softmax(masked, axis=0)
    chosen_rows = (row_expert[:, None] == jnp.arange(expert_count)[None, :]).astype(jnp.float32)
    mix_rows = jnp.dot(chosen_rows, mix_all, precision=lax.Precision.HIGHEST)
    mix_rows = mix_rows.reshape(halves, 1, all_rows)
    every_active = lax.all_gather(active.reshape(-1, units), "head", axis=0, tiled=True)
    every_active = every_active.reshape(width // col_width, *active.shape)
    partial_out = down_call(every_active, w_down, slots, mix_rows, token_block)
    combined = lax.psum_scatter(partial_out, "ctx", scatter_dimension=0, tiled=True)
    if swapped:
        own_state = every_state[lax.axis_index("ctx"), lax.axis_index("head")]
    layer_out = (own_state.astype(jnp.float32) + combined.astype(jnp.float32)).astype(jnp.bfloat16)
    return layer_out.reshape(local_seqs, tokens, col_width)


def solution(mesh):
    placed = (
        P("rep", "ctx", "head"),
        P("rep", "ctx", "head", None),
        P("head"),
        P("rep", "ctx", "head"),
        P("head", "ctx"),
        P(),
        P(),
        P("rep", "ctx", None),
        P("ctx", "head", None),
        P("ctx", None, "head"),
    )
    return jax.shard_map(
        on_device, mesh=mesh, in_specs=placed, out_specs=P("rep", "ctx", "head"), check_vma=False
    )
```

```python
import functools

import jax
import jax.numpy as jnp
from jax import lax
from jax.experimental import pallas as pl
from jax.experimental.pallas import tpu as pltpu
from jax.sharding import PartitionSpec as P


NT = (((1,), (1,)), ((), ()))
TN = (((0,), (0,)), ((), ()))
LANES = 128


def one_hot_rows(slots, cap, value):
    rows = lax.broadcasted_iota(jnp.int32, (cap, slots.shape[1]), 0)
    return jnp.where(rows == slots, value, 0.0).astype(jnp.bfloat16)


def gate_up_kernel(
    halves,
    units,
    state_ref,
    gain_ref,
    router_ref,
    w_ref,
    slot_ref,
    out_ref,
    logits_ref,
    act_ref,
    xg_ref,
    xu_ref,
):
    step = pl.program_id(1)
    groups, shards, group_rows, cols = state_ref.shape

    @pl.when(step == 0)
    def _():
        for group in range(groups):
            pieces = [state_ref[group, shard].astype(jnp.float32) for shard in range(shards)]
            square = sum(jnp.sum(piece * piece, axis=1, keepdims=True) for piece in pieces)
            inverse = lax.rsqrt(square / (shards * cols) + 1e-05)
            scaled = [
                (piece * inverse * gain_ref[shard]).astype(jnp.bfloat16)
                for shard, piece in enumerate(pieces)
            ]
            extra = xg_ref.shape[1] - shards * cols
            blank = [jnp.zeros((group_rows, extra), jnp.bfloat16)] if extra else []
            here = slice(group * group_rows, (group + 1) * group_rows)
            xg_ref[here, :] = jnp.concatenate(scaled + blank, axis=1)
            xu_ref[here, :] = jnp.concatenate(blank + scaled, axis=1)
        logits_ref[...] = lax.dot_general(
            router_ref[...], xg_ref[...], NT, preferred_element_type=jnp.float32
        )

    rows, wide = w_ref.shape[0], xg_ref.shape[1]
    gate = lax.dot_general(w_ref[:, :wide], xg_ref[...], NT, preferred_element_type=jnp.float32)
    up = lax.dot_general(
        w_ref[:, w_ref.shape[1] - wide :], xu_ref[...], NT, preferred_element_type=jnp.float32
    )
    active = gate * jax.nn.sigmoid(1.702 * gate) * (up + 1.0)
    slabs = act_ref.shape[0]
    for slab in range(slabs):
        act_ref[slab, pl.ds(step * rows, rows), :] = active[:, slab * LANES : (slab + 1) * LANES]

    @pl.when(step == pl.num_programs(1) - 1)
    def _():
        for row in range(halves):
            wanted = pl.ds(row, units, stride=halves) if halves > 1 else pl.ds(0, units)
            picked = jnp.concatenate([act_ref[slab, wanted, :] for slab in range(slabs)], axis=1)
            spread = one_hot_rows(slot_ref[row], out_ref.shape[2], 1.0)
            out_ref[row, 0] = lax.dot_general(
                spread, picked.astype(jnp.bfloat16), NT, preferred_element_type=jnp.float32
            ).astype(jnp.bfloat16)


def gate_up_call(state, gain, router, weights, slots, units, token_block, cap):
    halves = slots.shape[0]
    sources, shards, group_rows, cols = state.shape
    groups = token_block // group_rows
    blocks = sources // groups
    experts, wide = router.shape
    wide_w = weights.shape[1]
    sizes = [
        size
        for size in range(1, units + 1)
        if units % size == 0
        and (size == units or (size * halves) % 16 == 0)
        and size * halves * wide_w * 2 <= 4 << 20
    ]
    size = sizes[-1]
    return pl.pallas_call(
        functools.partial(gate_up_kernel, halves, units),
        grid=(blocks, units // size),
        out_shape=(
            jax.ShapeDtypeStruct((halves, blocks, cap, units), jnp.bfloat16),
            jax.ShapeDtypeStruct((experts, blocks * token_block), jnp.float32),
        ),
        in_specs=[
            pl.BlockSpec((groups, shards, group_rows, cols), lambda i, j: (i, 0, 0, 0)),
            pl.BlockSpec((shards, 1, cols), lambda i, j: (0, 0, 0)),
            pl.BlockSpec((experts, wide), lambda i, j: (0, 0)),
            pl.BlockSpec((size * halves, wide_w), lambda i, j: (j, 0)),
            pl.BlockSpec((halves, 1, token_block), lambda i, j: (0, 0, i)),
        ],
        out_specs=(
            pl.BlockSpec((halves, 1, cap, units), lambda i, j: (0, i, 0, 0)),
            pl.BlockSpec((experts, token_block), lambda i, j: (0, i)),
        ),
        scratch_shapes=[
            pltpu.VMEM((token_block // LANES, units * halves, LANES), jnp.float32),
            pltpu.VMEM((token_block, wide), jnp.bfloat16),
            pltpu.VMEM((token_block, wide), jnp.bfloat16),
        ],
        compiler_params=pltpu.CompilerParams(vmem_limit_bytes=56 << 20),
    )(state, gain, router, weights, slots)


def down_kernel(act_ref, w_ref, slot_ref, mix_ref, out_ref, total_ref):
    step = pl.program_id(1)
    part = None
    for row in range(w_ref.shape[0]):
        pieces = [act_ref[shard, row, 0] for shard in range(act_ref.shape[0])]
        hidden = jnp.concatenate(pieces, axis=1)
        piece = jnp.dot(hidden, w_ref[row], preferred_element_type=jnp.float32)
        part = piece if part is None else part + piece
    spread = one_hot_rows(slot_ref[0], act_ref.shape[3], mix_ref[0])
    added = lax.dot_general(
        spread, part.astype(jnp.bfloat16), TN, preferred_element_type=jnp.float32
    )

    @pl.when(step == 0)
    def _():
        total_ref[...] = added

    @pl.when(step != 0)
    def _():
        total_ref[...] += added

    @pl.when(step == pl.num_programs(1) - 1)
    def _():
        out_ref[...] = total_ref[...].astype(jnp.bfloat16)


def down_call(act, weights, slots, mix, token_block):
    shards, halves, blocks, cap, units = act.shape
    hidden, cols = weights.shape[1:]
    pair = 2 if halves % 2 == 0 else 1
    return pl.pallas_call(
        down_kernel,
        grid=(blocks, halves // pair),
        out_shape=jax.ShapeDtypeStruct((blocks * token_block, cols), jnp.bfloat16),
        in_specs=[
            pl.BlockSpec((shards, pair, 1, cap, units), lambda i, r: (0, r, i, 0, 0)),
            pl.BlockSpec((pair, hidden, cols), lambda i, r: (r, 0, 0)),
            pl.BlockSpec((1, 1, token_block), lambda i, r: (r * pair, 0, i)),
            pl.BlockSpec((1, 1, token_block), lambda i, r: (r * pair, 0, i)),
        ],
        out_specs=pl.BlockSpec((token_block, cols), lambda i, r: (i, 0)),
        scratch_shapes=[pltpu.VMEM((token_block, cols), jnp.float32)],
        compiler_params=pltpu.CompilerParams(vmem_limit_bytes=48 << 20),
    )(act, weights, slots, mix)


MESH = pl.DeviceIdType.MESH
NN = (((1,), (0,)), ((), ()))


def layer_kernel(
    sizes,
    q_ref,
    kv_ref,
    ids_ref,
    sink_ref,
    gain_ref,
    stream_ref,
    ow_hbm,
    router_hbm,
    wg_hbm,
    wd_hbm,
    out_ref,
    kv_all,
    ids_all,
    stream_in,
    ow,
    router,
    wg,
    wd,
    att_all,
    core_out,
    core_in,
    keep,
    x_out,
    x_in,
    h_all,
    y_all,
    pick,
    spread,
    xg,
    scale_ref,
    unit_rows,
    act_all,
    parts,
    rs_out,
    rs_in,
    local_sem,
    wg_sem,
    wd_sem,
    kv_send,
    kv_recv,
    ids_send,
    ids_recv,
    stream_send,
    stream_recv,
    att_send,
    att_recv,
    core_send,
    core_recv,
    x_send,
    x_recv,
    h_send,
    h_recv,
    act_send,
    act_recv,
    rs_send,
    rs_recv,
):
    seqs, tokens, rows, ctxs, width, cols, cap, local_experts, units, slots = sizes
    c, h, r = lax.axis_index("ctx"), lax.axis_index("head"), lax.axis_index("rep")
    all_rows = ctxs * rows
    wide = y_all.shape[1]
    pad_cols = h_all.shape[3]
    core_dev, x_dev = (c, h ^ 1, r), (c, h ^ 2, r)
    partner = (h, c, r)

    def remote(src, dst, send, recv, device):
        return pltpu.make_async_remote_copy(
            src_ref=src,
            dst_ref=dst,
            send_sem=send,
            recv_sem=recv,
            device_id=device,
            device_id_type=MESH,
        )

    ow_copy = pltpu.make_async_copy(ow_hbm, ow, local_sem.at[0])
    router_copy = pltpu.make_async_copy(router_hbm, router, local_sem.at[1])

    def wg_copy(e, slot):
        return pltpu.make_async_copy(
            wg_hbm.at[:, pl.ds(2 * e, 2), :], wg.at[slot], wg_sem.at[slot]
        )

    def wd_copy(e):
        return pltpu.make_async_copy(
            wd_hbm.at[pl.ds(2 * e, 2)], wd.at[pl.ds(2 * e, 2)], wd_sem.at[e]
        )

    barrier = pltpu.get_barrier_semaphore()
    for step in range(1, ctxs):
        pl.semaphore_signal(
            barrier, inc=1, device_id=(lax.rem(c + step, ctxs), h, r), device_id_type=MESH
        )
    pl.semaphore_signal(barrier, inc=1, device_id=core_dev, device_id_type=MESH)
    pl.semaphore_signal(barrier, inc=1, device_id=x_dev, device_id_type=MESH)

    @pl.when(c != h)
    def _():
        pl.semaphore_signal(barrier, inc=1, device_id=partner, device_id_type=MESH)

    ow_copy.start()
    for e in range(min(slots, local_experts)):
        wg_copy(e, e).start()
    router_copy.start()
    for e in range(local_experts):
        wd_copy(e).start()
    topk = ids_ref.shape[1]
    own_ids = jnp.concatenate([ids_ref[s] for s in range(seqs)], axis=1).astype(jnp.float32)
    ids_all[c] = jnp.concatenate(
        [own_ids, jnp.full((8 - topk, rows), -1.0, jnp.float32)], axis=0
    )
    kv_all[c] = kv_ref[...]
    for other in range(ctxs):

        @pl.when(other > c)
        def _():
            kv_all[other] = jnp.zeros(kv_all.shape[1:], jnp.bfloat16)

    parts[...] = jnp.zeros(parts.shape, jnp.bfloat16)
    pl.semaphore_wait(barrier, ctxs + 1 + (c != h).astype(jnp.int32))

    def kv_copy(src, dst):
        return remote(
            kv_all.at[src], kv_all.at[src], kv_send.at[dst], kv_recv.at[src], (dst, h, r)
        )

    def ids_copy(src, dst):
        return remote(
            ids_all.at[src], ids_all.at[src], ids_send.at[dst], ids_recv.at[src], (dst, h, r)
        )

    def att_copy(src, dst):
        return remote(
            att_all.at[src], att_all.at[src], att_send.at[dst], att_recv.at[src], (dst, h, r)
        )

    for dst in range(ctxs):

        @pl.when(dst > c)
        def _():
            kv_copy(c, dst).start()

    stream_copy = remote(
        stream_ref, stream_in, stream_send.at[0], stream_recv.at[0], partner
    )
    stream_local = pltpu.make_async_copy(stream_ref, stream_in, local_sem.at[2])

    @pl.when(c != h)
    def _():
        stream_copy.start()

    @pl.when(c == h)
    def _():
        stream_local.start()

    for dst in range(ctxs):

        @pl.when(dst != c)
        def _():
            ids_copy(c, dst).start()

    for src in range(ctxs):

        @pl.when(src < c)
        def _():
            kv_copy(src, c).wait_recv()

    pairs = q_ref.shape[2] // LANES
    half = LANES // 2
    keys = ctxs * tokens
    group = pairs * tokens
    low_k = lax.broadcasted_iota(jnp.int32, (keys, LANES), 1) < half
    low_q = lax.broadcasted_iota(jnp.int32, (group, LANES), 1) < half
    key_pos = lax.broadcasted_iota(jnp.int32, (group, keys), 1)
    row_pos = lax.rem(lax.broadcasted_iota(jnp.int32, (group, keys), 0), tokens)
    visible = key_pos <= row_pos + c * tokens
    for s in range(seqs):
        kv = jnp.concatenate([kv_all[src, s] for src in range(ctxs)], axis=0).astype(jnp.float32)
        turned = pltpu.roll(kv, half, 1)
        key_sides = [jnp.where(low_k, kv, 0.0), jnp.where(low_k, 0.0, turned)]
        value_sides = [jnp.where(low_k, turned, 0.0), jnp.where(low_k, 0.0, kv)]
        q = jnp.concatenate(
            [q_ref[s, :, p * LANES : (p + 1) * LANES] for p in range(pairs)], axis=0
        )
        acc, totals = None, []
        for side in range(2):
            sink = jnp.concatenate(
                [
                    jnp.full((tokens, 1), sink_ref[2 * p + side], jnp.float32)
                    for p in range(pairs)
                ],
                axis=0,
            )
            scores = lax.dot_general(
                q, key_sides[side].astype(jnp.bfloat16), NT, preferred_element_type=jnp.float32
            ) * (half ** (-0.5))
            scores = jnp.where(visible, scores, -1e30)
            peak = jnp.maximum(sink, jnp.max(scores, axis=1, keepdims=True))
            terms = jnp.where(visible, jnp.exp(scores - peak), 0.0)
            totals.append(jnp.exp(sink - peak) + jnp.sum(terms, axis=1, keepdims=True))
            piece = lax.dot_general(
                terms.astype(jnp.bfloat16),
                value_sides[side].astype(jnp.bfloat16),
                NN,
                preferred_element_type=jnp.float32,
            )
            acc = piece if acc is None else acc + piece
        attended = (acc / jnp.where(low_q, totals[0], totals[1])).astype(jnp.bfloat16)
        for p in range(pairs):
            att_all[c, s * tokens : (s + 1) * tokens, p * LANES : (p + 1) * LANES] = attended[
                p * tokens : (p + 1) * tokens
            ]
    for dst in range(ctxs):

        @pl.when(dst != c)
        def _():
            att_copy(c, dst).start()

    for src in range(ctxs):

        @pl.when(src != c)
        def _():
            ids_copy(src, c).wait_recv()

    ids_row = jnp.concatenate([ids_all[src] for src in range(ctxs)], axis=1)
    mine = (
        lax.broadcasted_iota(jnp.int32, (local_experts, all_rows), 0) + c * local_experts
    ).astype(jnp.float32)
    member = jnp.zeros((local_experts, all_rows), jnp.bool_)
    for k in range(topk):
        member = member | (mine == ids_row[k : k + 1])
    before = lax.broadcasted_iota(jnp.int32, (all_rows, all_rows), 0) <= lax.broadcasted_iota(
        jnp.int32, (all_rows, all_rows), 1
    )
    rank = lax.dot_general(
        jnp.where(member, 1.0, 0.0).astype(jnp.bfloat16),
        jnp.where(before, 1.0, 0.0).astype(jnp.bfloat16),
        NN,
        preferred_element_type=jnp.float32,
    )
    slot_row = jnp.where(member, rank - 1.0, -1.0)
    slot_rows = lax.broadcasted_iota(jnp.int32, (cap, all_rows), 0).astype(jnp.float32)
    for e in range(local_experts):
        pick[e * cap : (e + 1) * cap, :] = jnp.where(
            slot_rows == slot_row[e : e + 1], 1.0, 0.0
        ).astype(jnp.bfloat16)
    both = jnp.concatenate(
        [ids_row, slot_row, jnp.zeros((LANES - 8 - local_experts, all_rows), jnp.float32)], axis=0
    )
    by_token = jnp.transpose(both)

    ow_copy.wait()
    side, core = h // 2, lax.rem(h, 2)

    def projected(block):
        @pl.when(block != c)
        def _():
            att_copy(block, c).wait_recv()

        out = lax.dot_general(att_all[block], ow[...], NT, preferred_element_type=jnp.float32)
        return jnp.concatenate(
            [out, jnp.zeros((rows, pad_cols - cols), jnp.float32)], axis=1
        )

    def core_copy(i):
        return remote(core_out.at[i], core_in.at[i], core_send.at[i], core_recv.at[i], core_dev)

    for i in range(2):
        across = (1 - side) if i == 0 else side
        core_out[i] = projected(2 * across + 1 - core).astype(jnp.bfloat16)
        core_copy(i).start()
    for i in range(2):
        across = (1 - side) if i == 0 else side
        keep[i] = projected(2 * across + core)
    core_copy(0).wait_recv()
    x_out[...] = (keep[0] + core_in[0].astype(jnp.float32)).astype(jnp.bfloat16)
    x_copy = remote(x_out, x_in, x_send.at[0], x_recv.at[0], x_dev)
    x_copy.start()

    @pl.when(c != h)
    def _():
        stream_copy.wait_recv()

    @pl.when(c == h)
    def _():
        stream_local.wait()

    core_copy(1).wait_recv()
    turned_stream = stream_in[...].reshape(rows, cols).astype(jnp.float32)
    kept = (
        keep[1]
        + core_in[1].astype(jnp.float32)
        + jnp.concatenate(
            [turned_stream, jnp.zeros((rows, pad_cols - cols), jnp.float32)], axis=1
        )
    )
    x_copy.wait_recv()
    h_all[c, h] = (kept + x_in[...].astype(jnp.float32)).astype(jnp.bfloat16)

    def h_copy(way, block, row, device):
        return remote(
            h_all.at[block, row],
            h_all.at[block, row],
            h_send.at[way, block],
            h_recv.at[block, row],
            device,
        )

    def h_core(block, row):
        return h_copy(jnp.where(row == h, 0, 1), block, row, core_dev)

    def h_x(block):
        return h_copy(2, block, h, x_dev)

    def h_right(block):
        return h_copy(3, block, h, (jnp.minimum(c + 1, ctxs - 1), h, r))

    def h_left(block):
        return h_copy(4, block, h, (jnp.maximum(c - 1, 0), h, r))

    def arrived(block, row):
        h_copy(0, block, row, core_dev).wait_recv()

    h_x(c).start()

    @pl.when(c < ctxs - 1)
    def _():
        h_right(c).start()

    @pl.when(c > 0)
    def _():
        h_left(c).start()

    h_core(c, h).start()
    for d in range(1, ctxs + 1):

        @pl.when(c - d >= 0)
        def _():
            arrived(c - d, h)

            @pl.when(c < ctxs - 1)
            def _():
                h_right(c - d).start()

            h_x(c - d).start()
            h_core(c - d, h).start()

        @pl.when(c + d < ctxs)
        def _():
            arrived(c + d, h)

            @pl.when(c > 0)
            def _():
                h_left(c + d).start()

            h_x(c + d).start()
            h_core(c + d, h).start()

        @pl.when(c - (d - 1) >= 0)
        def _():
            arrived(c - (d - 1), h ^ 2)
            h_core(c - (d - 1), h ^ 2).start()

        if d > 1:

            @pl.when(c + (d - 1) < ctxs)
            def _():
                arrived(c + (d - 1), h ^ 2)
                h_core(c + (d - 1), h ^ 2).start()

    for block in range(ctxs):
        arrived(block, h ^ 1)
        arrived(block, h ^ 3)

    gain = gain_ref[...].reshape(1, width)
    squares = []
    for row in range(ctxs):
        pieces = [h_all[block, row].astype(jnp.float32)[:, :cols] for block in range(ctxs)]
        squares.append(sum(jnp.sum(piece * piece, axis=1, keepdims=True) for piece in pieces))
        flat = jnp.concatenate(pieces, axis=1) * gain
        y_all[row * rows : (row + 1) * rows, :] = jnp.concatenate(
            [flat, jnp.zeros((rows, wide - width), jnp.float32)], axis=1
        ).astype(jnp.bfloat16)
    inverse = lax.rsqrt(jnp.concatenate(squares, axis=0) / width + 1e-05)
    router_copy.wait()
    logits = lax.dot_general(
        y_all[:, :width], router[...], NT, preferred_element_type=jnp.float32
    ) * inverse
    experts = router.shape[0]
    expert_lane = lax.broadcasted_iota(jnp.int32, (all_rows, experts), 1).astype(jnp.float32)
    named = jnp.zeros((all_rows, experts), jnp.bool_)
    for k in range(topk):
        named = named | (expert_lane == by_token[:, k : k + 1])
    top = jnp.max(jnp.where(named, logits, -1e30), axis=1, keepdims=True)
    weight = jnp.where(named, jnp.exp(logits - top), 0.0)
    mix = weight / jnp.sum(weight, axis=1, keepdims=True)
    mix = jnp.concatenate([mix, jnp.zeros((all_rows, LANES - experts), jnp.float32)], axis=1)
    mix = pltpu.roll(mix, lax.rem(LANES - c * local_experts, LANES), 1)
    slot_lane = lax.broadcasted_iota(jnp.int32, (all_rows, LANES), 1).astype(jnp.float32)
    for e in range(local_experts):
        spread[:, e * LANES : (e + 1) * LANES] = jnp.where(
            slot_lane == by_token[:, 8 + e : 9 + e], mix[:, e : e + 1], 0.0
        ).astype(jnp.bfloat16)

    inverse_row = jnp.transpose(jnp.broadcast_to(inverse, (all_rows, LANES)))[:8]
    first = inverse_row.astype(jnp.bfloat16)
    rest = inverse_row - first.astype(jnp.float32)
    second = rest.astype(jnp.bfloat16)
    third = (rest - second.astype(jnp.float32)).astype(jnp.bfloat16)
    for e in range(local_experts):
        here = pick[e * cap : (e + 1) * cap, :]
        scale_ref[e] = sum(
            lax.dot_general(part, here, NT, preferred_element_type=jnp.float32)
            for part in (first, second, third)
        )

    @pl.loop(0, wide // LANES)
    def _(j):
        at = pl.multiple_of(j * LANES, LANES)
        xg[:, pl.ds(at, LANES)] = lax.dot_general(
            pick[...], y_all[:, pl.ds(at, LANES)], NN, preferred_element_type=jnp.float32
        ).astype(jnp.bfloat16)

    def act_core(shard, e):
        return remote(
            act_all.at[shard, e],
            act_all.at[shard, e],
            act_send.at[jnp.where(shard == h, 0, 1), e],
            act_recv.at[shard, e],
            core_dev,
        )

    def act_x(e):
        return remote(
            act_all.at[h, e], act_all.at[h, e], act_send.at[2, e], act_recv.at[h, e], x_dev
        )

    def act_arrived(shard, e):
        remote(
            act_all.at[shard, e],
            act_all.at[shard, e],
            act_send.at[0, e],
            act_recv.at[shard, e],
            core_dev,
        ).wait_recv()

    lead = wide - width
    packed = act_all.shape[3]

    @pl.loop(0, local_experts)
    def _(e):
        slot = lax.rem(e, slots)
        wg_copy(e, slot).wait()
        rows_in = xg[pl.ds(pl.multiple_of(e * cap, cap), cap), :]
        shifted = jnp.concatenate(
            [jnp.zeros((cap, lead), jnp.bfloat16), rows_in[:, :width]], axis=1
        )
        factor = scale_ref[e][:1]
        gate = factor * lax.dot_general(
            wg[slot, :, :, :wide].reshape(2 * units, wide),
            rows_in,
            NT,
            preferred_element_type=jnp.float32,
        )
        up = factor * lax.dot_general(
            wg[slot, :, :, 2 * width - wide :].reshape(2 * units, wide),
            shifted,
            NT,
            preferred_element_type=jnp.float32,
        )
        active = gate * jax.nn.sigmoid(1.702 * gate) * (up + 1.0)
        unit_rows[...] = jnp.concatenate(
            [active, jnp.zeros((2 * units, LANES - cap), jnp.float32)], axis=1
        )
        stacked = jnp.concatenate(
            [unit_rows[pl.ds(u, units, stride=2), :] for u in range(2)]
            + [jnp.zeros((packed - 2 * units, LANES), jnp.float32)],
            axis=0,
        )
        act_all[h, e] = jnp.transpose(stacked)[:cap].astype(jnp.bfloat16)
        act_x(e).start()
        act_core(h, e).start()

        @pl.when(e + slots < local_experts)
        def _():
            wg_copy(e + slots, slot).start()

        @pl.when(e >= 2)
        def _():
            act_arrived(h ^ 2, e - 2)
            act_core(h ^ 2, e - 2).start()

    for e in range(local_experts - 2, local_experts):
        act_arrived(h ^ 2, e)
        act_core(h ^ 2, e).start()

    @pl.loop(0, local_experts)
    def _(e):
        wd_copy(e).wait()
        act_arrived(h ^ 1, e)
        act_arrived(h ^ 3, e)
        total = None
        for u in range(2):
            hidden = jnp.concatenate(
                [act_all[shard, e][:, u * units : (u + 1) * units] for shard in range(4)], axis=1
            )
            piece = lax.dot_general(
                hidden, wd[2 * e + u], NN, preferred_element_type=jnp.float32
            )
            total = piece if total is None else total + piece
        parts[pl.ds(pl.multiple_of(e * LANES, LANES), cap), :] = jnp.concatenate(
            [total, jnp.zeros((cap, pad_cols - cols), jnp.float32)], axis=1
        ).astype(jnp.bfloat16)

    def rs_copy(src, dst):
        return remote(rs_out.at[dst], rs_in.at[src], rs_send.at[dst], rs_recv.at[src], (dst, h, r))

    def combined(block):
        return lax.dot_general(
            spread[pl.ds(pl.multiple_of(block * rows, rows), rows), :],
            parts[...],
            NN,
            preferred_element_type=jnp.float32,
        )

    for d in range(1, ctxs):
        dst = lax.rem(c + d, ctxs)
        rs_out[dst] = combined(dst).astype(jnp.bfloat16)
        rs_copy(c, dst).start()
    total = combined(c) + h_all[h, c].astype(jnp.float32)
    for d in range(1, ctxs):
        src = lax.rem(c + d, ctxs)
        rs_copy(src, c).wait_recv()
        total = total + rs_in[src].astype(jnp.float32)
    out_ref[...] = total[:, :cols].astype(jnp.bfloat16).reshape(out_ref.shape)

    for dst in range(ctxs):

        @pl.when(dst > c)
        def _():
            kv_copy(c, dst).wait_send()

        @pl.when(dst != c)
        def _():
            ids_copy(c, dst).wait_send()
            att_copy(c, dst).wait_send()
            rs_copy(c, dst).wait_send()

    @pl.when(c != h)
    def _():
        stream_copy.wait_send()

    x_copy.wait_send()
    for i in range(2):
        core_copy(i).wait_send()
    for block in range(ctxs):
        h_x(block).wait_send()
        h_core(block, h).wait_send()
        h_core(block, h ^ 2).wait_send()

        @pl.when((c < ctxs - 1) & (block <= c))
        def _():
            h_right(block).wait_send()

        @pl.when((c > 0) & (block >= c))
        def _():
            h_left(block).wait_send()

    for e in range(local_experts):
        act_x(e).wait_send()
        act_core(h, e).wait_send()
        act_core(h ^ 2, e).wait_send()


def layer_call(queries, keyvals, sinks, stream, out_weight, gain, router, ids, w_gate_up, w_down):
    seqs, tokens, q_cols = queries.shape
    cols = stream.shape[2]
    ctxs = lax.axis_size("ctx")
    rows = seqs * tokens
    width = gain.shape[0]
    halves, units, wide_w = w_gate_up.shape
    local_experts = halves // 2
    all_rows = ctxs * rows
    cap = all_rows * 3 // 16
    wide = pl.cdiv(width, LANES) * LANES
    pad_cols = pl.cdiv(cols, LANES) * LANES
    packed = pl.cdiv(2 * units, LANES) * LANES
    slots = min(4, local_experts)
    sizes = (seqs, tokens, rows, ctxs, width, cols, cap, local_experts, units, slots)
    bf16, f32 = jnp.bfloat16, jnp.float32
    dma = pltpu.SemaphoreType.DMA
    vmem = pl.BlockSpec(memory_space=pltpu.VMEM)
    hbm = pl.BlockSpec(memory_space=pl.ANY)
    return pl.pallas_call(
        functools.partial(layer_kernel, sizes),
        out_shape=jax.ShapeDtypeStruct((seqs, tokens, cols), bf16),
        in_specs=[vmem, vmem, vmem, pl.BlockSpec(memory_space=pltpu.SMEM), vmem, vmem]
        + [hbm] * 4,
        out_specs=vmem,
        scratch_shapes=[
            pltpu.VMEM((ctxs, seqs, tokens, keyvals.shape[3]), bf16),
            pltpu.VMEM((ctxs, 8, LANES), f32),
            pltpu.VMEM((seqs, tokens, cols), bf16),
            pltpu.VMEM(out_weight.shape[::-1], bf16),
            pltpu.VMEM(router.shape[::-1], bf16),
            pltpu.VMEM((slots, units, 2, wide_w), bf16),
            pltpu.VMEM(w_down.shape, bf16),
            pltpu.VMEM((ctxs, rows, q_cols), bf16),
            pltpu.VMEM((2, rows, pad_cols), bf16),
            pltpu.VMEM((2, rows, pad_cols), bf16),
            pltpu.VMEM((2, rows, pad_cols), f32),
            pltpu.VMEM((rows, pad_cols), bf16),
            pltpu.VMEM((rows, pad_cols), bf16),
            pltpu.VMEM((ctxs, 4, rows, pad_cols), bf16),
            pltpu.VMEM((all_rows, wide), bf16),
            pltpu.VMEM((local_experts * cap, all_rows), bf16),
            pltpu.VMEM((all_rows, local_experts * LANES), bf16),
            pltpu.VMEM((local_experts * cap, wide), bf16),
            pltpu.VMEM((local_experts, 8, cap), f32),
            pltpu.VMEM((2 * units, LANES), f32),
            pltpu.VMEM((4, local_experts, cap, packed), bf16),
            pltpu.VMEM((local_experts * LANES, pad_cols), bf16),
            pltpu.VMEM((ctxs, rows, pad_cols), bf16),
            pltpu.VMEM((ctxs, rows, pad_cols), bf16),
            dma((3,)),
            dma((slots,)),
            dma((local_experts,)),
            dma((ctxs,)),
            dma((ctxs,)),
            dma((ctxs,)),
            dma((ctxs,)),
            dma((1,)),
            dma((1,)),
            dma((ctxs,)),
            dma((ctxs,)),
            dma((2,)),
            dma((2,)),
            dma((1,)),
            dma((1,)),
            dma((5, ctxs)),
            dma((ctxs, 4)),
            dma((3, local_experts)),
            dma((4, local_experts)),
            dma((ctxs,)),
            dma((ctxs,)),
        ],
        compiler_params=pltpu.CompilerParams(
            vmem_limit_bytes=67043328, collective_id=0, has_side_effects=True
        ),
    )(
        queries,
        keyvals.reshape(seqs, tokens, keyvals.shape[3]),
        jnp.transpose(ids, (0, 2, 1)),
        sinks,
        gain,
        stream,
        out_weight.T,
        router.T,
        jnp.transpose(w_gate_up, (1, 0, 2)),
        w_down,
    )


def one_chip_row(queries, keyvals, stream, out_weight, router, ids, w_gate_up):
    ctxs, heads = lax.axis_size("ctx"), lax.axis_size("head")
    rows = queries.shape[0] * queries.shape[1]
    return (
        ctxs == heads == 4
        and rows == LANES
        and keyvals.shape[2] == 1
        and keyvals.shape[3] == LANES
        and out_weight.shape[1] == stream.shape[2]
        and w_gate_up.shape[0] == 16
        and ids.shape[2] <= 8
        and router.shape[1] <= LANES
    )


def on_device(
    queries, keyvals, sinks, stream, out_weight, norm_gain, router, expert_ids, w_gate_up, w_down
):
    if one_chip_row(queries, keyvals, stream, out_weight, router, expert_ids, w_gate_up):
        return layer_call(
            queries,
            keyvals,
            sinks,
            stream,
            out_weight,
            norm_gain,
            router,
            expert_ids,
            w_gate_up,
            w_down,
        )
    ctx_count = lax.axis_size("ctx")
    local_seqs = queries.shape[0]
    tokens = queries.shape[1]
    row_count = local_seqs * tokens
    kv_local = keyvals.shape[2]
    head_dim = keyvals.shape[3] // 2
    q_local = queries.shape[2] // head_dim
    query_group_size = q_local // kv_local
    wide_rows = query_group_size * tokens
    col_width = stream.shape[2]
    first_pos = lax.axis_index("ctx") * tokens
    last_pos = first_pos + tokens - 1
    score_scale = head_dim ** (-0.5)
    scaled_queries = queries * jnp.asarray(score_scale, jnp.bfloat16)
    query_grid = scaled_queries.reshape(local_seqs, tokens, kv_local, query_group_size, head_dim)
    query_wide = jnp.transpose(query_grid, (0, 2, 3, 1, 4)).reshape(
        local_seqs, kv_local, wide_rows, head_dim
    )
    positions = first_pos + jnp.tile(jnp.arange(tokens), query_group_size)
    sink_rows = jnp.repeat(sinks.reshape(kv_local, query_group_size), tokens, axis=1)
    sink_grid = jnp.broadcast_to(sink_rows[None], (local_seqs, kv_local, wide_rows))
    start_state = (
        sink_grid,
        jnp.ones_like(sink_grid),
        jnp.zeros((local_seqs, kv_local, head_dim, wide_rows), jnp.float32),
    )

    def attend_block(running, shard_piece):
        peak_old, denom_old, accum_old = running
        key_block = shard_piece[..., :head_dim]
        value_block = shard_piece[..., head_dim:]
        scores = jnp.einsum(
            "skmd,snkd->sknm", query_wide, key_block, preferred_element_type=jnp.float32
        )
        key_pos = jnp.arange(shard_piece.shape[1])
        visible = key_pos[:, None] <= positions[None, :]
        masked = jnp.where(visible[None, None], scores, -jnp.inf)
        peak_new = jnp.maximum(peak_old, jnp.max(masked, axis=2))
        exp_terms = jnp.exp(masked - peak_new[:, :, None, :])
        factor = jnp.exp(peak_old - peak_new)
        denom_new = denom_old * factor + jnp.sum(exp_terms, axis=2)
        accum_new = accum_old * factor[:, :, None, :] + jnp.einsum(
            "sknm,snkd->skdm",
            exp_terms.astype(jnp.bfloat16),
            value_block,
            preferred_element_type=jnp.float32,
        )
        return (peak_new, denom_new, accum_new)

    shard_piece = lax.all_gather(keyvals, "ctx", axis=1, tiled=True)

    def keep_state(state_in):
        return state_in

    def update_state(state_in):
        return attend_block(state_in, shard_piece)

    peak_fin, denom_fin, accum_fin = lax.cond(
        jnp.int32(0) > last_pos, keep_state, update_state, start_state
    )
    normalized = (accum_fin / denom_fin[:, :, None, :]).reshape(
        local_seqs, kv_local, head_dim, query_group_size, tokens
    )
    attended = (
        jnp.transpose(normalized, (0, 4, 1, 3, 2))
        .reshape(row_count, q_local * head_dim)
        .astype(jnp.bfloat16)
    )
    token_ids = lax.all_gather(
        expert_ids.reshape(row_count, expert_ids.shape[2]).T, "ctx", axis=1, tiled=True
    )
    all_rows = ctx_count * row_count
    halves = w_gate_up.shape[0]
    units = w_gate_up.shape[1]
    token_block = min(all_rows, 8 * tokens)
    cap = token_block // tokens * (3 * tokens // 16)
    row_expert = (lax.axis_index("ctx") * halves + jnp.arange(halves)) // 2
    named = jnp.any(token_ids[:, None, :] == row_expert[None, :, None], axis=0)
    counted = named.astype(jnp.int32).reshape(halves, all_rows // token_block, token_block)
    rank = jnp.cumsum(counted, axis=2) - 1
    slots = jnp.where(named, rank.reshape(halves, all_rows), -1).reshape(halves, 1, all_rows)
    width = norm_gain.shape[0]
    head_count = lax.axis_size("head")
    swapped = ctx_count == head_count and out_weight.shape[1] == col_width
    if swapped:
        pairs = [
            (first * head_count + second, second * head_count + first)
            for first in range(ctx_count)
            for second in range(head_count)
        ]
        turned = lax.ppermute(
            stream.reshape(row_count, col_width), ("ctx", "head"), perm=pairs
        )
        every_row = lax.all_gather(attended, "ctx", axis=0, tiled=True)
        partial_proj = jnp.dot(every_row, out_weight, preferred_element_type=jnp.float32)
        summed = lax.psum_scatter(
            partial_proj.astype(jnp.bfloat16), "head", scatter_dimension=0, tiled=True
        )
        turned_state = summed.astype(jnp.float32) + turned.astype(jnp.float32)
        every_state = lax.all_gather(
            turned_state.astype(jnp.bfloat16), ("head", "ctx"), axis=0, tiled=False
        )
    else:
        partial_proj = jnp.dot(attended, lax.all_gather(out_weight, "ctx", axis=1, tiled=True), preferred_element_type=jnp.float32)
        own_stream = stream.reshape(row_count, col_width).astype(jnp.float32)
        summed = lax.psum_scatter(
            partial_proj.astype(jnp.bfloat16), "head", scatter_dimension=1, tiled=True
        )
        own_state = (summed.astype(jnp.float32) + own_stream).astype(jnp.bfloat16)
        every_state = lax.all_gather(own_state, ("ctx", "head"), axis=0, tiled=False)
    every_state = every_state.reshape(ctx_count, width // col_width, row_count, col_width)
    expert_count = router.shape[1]
    unit_rows = jnp.transpose(w_gate_up, (1, 0, 2)).reshape(units * halves, w_gate_up.shape[2])
    router_rows = jnp.pad(router.T, ((0, 0), (0, -width % LANES)))
    gain = norm_gain.reshape(width // col_width, 1, col_width)
    active, logits = gate_up_call(
        every_state, gain, router_rows, unit_rows, slots, units, token_block, cap
    )
    member = jnp.any(token_ids[:, None, :] == jnp.arange(expert_count)[None, :, None], axis=0)
    masked = jnp.where(member, logits, -jnp.inf)
    mix_all = jax.nn.softmax(masked, axis=0)
    chosen_rows = (row_expert[:, None] == jnp.arange(expert_count)[None, :]).astype(jnp.float32)
    mix_rows = jnp.dot(chosen_rows, mix_all, precision=lax.Precision.HIGHEST)
    mix_rows = mix_rows.reshape(halves, 1, all_rows)
    every_active = lax.all_gather(active.reshape(-1, units), "head", axis=0, tiled=True)
    every_active = every_active.reshape(width // col_width, *active.shape)
    partial_out = down_call(every_active, w_down, slots, mix_rows, token_block)
    combined = lax.psum_scatter(partial_out, "ctx", scatter_dimension=0, tiled=True)
    if swapped:
        own_state = every_state[lax.axis_index("ctx"), lax.axis_index("head")]
    layer_out = (own_state.astype(jnp.float32) + combined.astype(jnp.float32)).astype(jnp.bfloat16)
    return layer_out.reshape(local_seqs, tokens, col_width)


def solution(mesh):
    placed = (
        P("rep", "ctx", "head"),
        P("rep", "ctx", "head", None),
        P("head"),
        P("rep", "ctx", "head"),
        P("head", "ctx"),
        P(),
        P(),
        P("rep", "ctx", None),
        P("ctx", "head", None),
        P("ctx", None, "head"),
    )
    return jax.shard_map(
        on_device, mesh=mesh, in_specs=placed, out_specs=P("rep", "ctx", "head"), check_vma=False
    )
```

```python
import functools

import jax
import jax.numpy as jnp
from jax import lax
from jax.experimental import pallas as pl
from jax.experimental.pallas import tpu as pltpu
from jax.sharding import PartitionSpec as P


NT = (((1,), (1,)), ((), ()))
TN = (((0,), (0,)), ((), ()))
LANES = 128


def one_hot_rows(slots, cap, value):
    rows = lax.broadcasted_iota(jnp.int32, (cap, slots.shape[1]), 0)
    return jnp.where(rows == slots, value, 0.0).astype(jnp.bfloat16)


def gate_up_kernel(
    halves,
    units,
    state_ref,
    gain_ref,
    router_ref,
    w_ref,
    slot_ref,
    out_ref,
    logits_ref,
    act_ref,
    xg_ref,
    xu_ref,
):
    step = pl.program_id(1)
    groups, shards, group_rows, cols = state_ref.shape

    @pl.when(step == 0)
    def _():
        for group in range(groups):
            pieces = [state_ref[group, shard].astype(jnp.float32) for shard in range(shards)]
            square = sum(jnp.sum(piece * piece, axis=1, keepdims=True) for piece in pieces)
            inverse = lax.rsqrt(square / (shards * cols) + 1e-05)
            scaled = [
                (piece * inverse * gain_ref[shard]).astype(jnp.bfloat16)
                for shard, piece in enumerate(pieces)
            ]
            extra = xg_ref.shape[1] - shards * cols
            blank = [jnp.zeros((group_rows, extra), jnp.bfloat16)] if extra else []
            here = slice(group * group_rows, (group + 1) * group_rows)
            xg_ref[here, :] = jnp.concatenate(scaled + blank, axis=1)
            xu_ref[here, :] = jnp.concatenate(blank + scaled, axis=1)
        logits_ref[...] = lax.dot_general(
            router_ref[...], xg_ref[...], NT, preferred_element_type=jnp.float32
        )

    rows, wide = w_ref.shape[0], xg_ref.shape[1]
    gate = lax.dot_general(w_ref[:, :wide], xg_ref[...], NT, preferred_element_type=jnp.float32)
    up = lax.dot_general(
        w_ref[:, w_ref.shape[1] - wide :], xu_ref[...], NT, preferred_element_type=jnp.float32
    )
    active = gate * jax.nn.sigmoid(1.702 * gate) * (up + 1.0)
    slabs = act_ref.shape[0]
    for slab in range(slabs):
        act_ref[slab, pl.ds(step * rows, rows), :] = active[:, slab * LANES : (slab + 1) * LANES]

    @pl.when(step == pl.num_programs(1) - 1)
    def _():
        for row in range(halves):
            wanted = pl.ds(row, units, stride=halves) if halves > 1 else pl.ds(0, units)
            picked = jnp.concatenate([act_ref[slab, wanted, :] for slab in range(slabs)], axis=1)
            spread = one_hot_rows(slot_ref[row], out_ref.shape[2], 1.0)
            out_ref[row, 0] = lax.dot_general(
                spread, picked.astype(jnp.bfloat16), NT, preferred_element_type=jnp.float32
            ).astype(jnp.bfloat16)


def gate_up_call(state, gain, router, weights, slots, units, token_block, cap):
    halves = slots.shape[0]
    sources, shards, group_rows, cols = state.shape
    groups = token_block // group_rows
    blocks = sources // groups
    experts, wide = router.shape
    wide_w = weights.shape[1]
    sizes = [
        size
        for size in range(1, units + 1)
        if units % size == 0
        and (size == units or (size * halves) % 16 == 0)
        and size * halves * wide_w * 2 <= 4 << 20
    ]
    size = sizes[-1]
    return pl.pallas_call(
        functools.partial(gate_up_kernel, halves, units),
        grid=(blocks, units // size),
        out_shape=(
            jax.ShapeDtypeStruct((halves, blocks, cap, units), jnp.bfloat16),
            jax.ShapeDtypeStruct((experts, blocks * token_block), jnp.float32),
        ),
        in_specs=[
            pl.BlockSpec((groups, shards, group_rows, cols), lambda i, j: (i, 0, 0, 0)),
            pl.BlockSpec((shards, 1, cols), lambda i, j: (0, 0, 0)),
            pl.BlockSpec((experts, wide), lambda i, j: (0, 0)),
            pl.BlockSpec((size * halves, wide_w), lambda i, j: (j, 0)),
            pl.BlockSpec((halves, 1, token_block), lambda i, j: (0, 0, i)),
        ],
        out_specs=(
            pl.BlockSpec((halves, 1, cap, units), lambda i, j: (0, i, 0, 0)),
            pl.BlockSpec((experts, token_block), lambda i, j: (0, i)),
        ),
        scratch_shapes=[
            pltpu.VMEM((token_block // LANES, units * halves, LANES), jnp.float32),
            pltpu.VMEM((token_block, wide), jnp.bfloat16),
            pltpu.VMEM((token_block, wide), jnp.bfloat16),
        ],
        compiler_params=pltpu.CompilerParams(vmem_limit_bytes=56 << 20),
    )(state, gain, router, weights, slots)


def down_kernel(act_ref, w_ref, slot_ref, mix_ref, out_ref, total_ref):
    step = pl.program_id(1)
    part = None
    for row in range(w_ref.shape[0]):
        pieces = [act_ref[shard, row, 0] for shard in range(act_ref.shape[0])]
        hidden = jnp.concatenate(pieces, axis=1)
        piece = jnp.dot(hidden, w_ref[row], preferred_element_type=jnp.float32)
        part = piece if part is None else part + piece
    spread = one_hot_rows(slot_ref[0], act_ref.shape[3], mix_ref[0])
    added = lax.dot_general(
        spread, part.astype(jnp.bfloat16), TN, preferred_element_type=jnp.float32
    )

    @pl.when(step == 0)
    def _():
        total_ref[...] = added

    @pl.when(step != 0)
    def _():
        total_ref[...] += added

    @pl.when(step == pl.num_programs(1) - 1)
    def _():
        out_ref[...] = total_ref[...].astype(jnp.bfloat16)


def down_call(act, weights, slots, mix, token_block):
    shards, halves, blocks, cap, units = act.shape
    hidden, cols = weights.shape[1:]
    pair = 2 if halves % 2 == 0 else 1
    return pl.pallas_call(
        down_kernel,
        grid=(blocks, halves // pair),
        out_shape=jax.ShapeDtypeStruct((blocks * token_block, cols), jnp.bfloat16),
        in_specs=[
            pl.BlockSpec((shards, pair, 1, cap, units), lambda i, r: (0, r, i, 0, 0)),
            pl.BlockSpec((pair, hidden, cols), lambda i, r: (r, 0, 0)),
            pl.BlockSpec((1, 1, token_block), lambda i, r: (r * pair, 0, i)),
            pl.BlockSpec((1, 1, token_block), lambda i, r: (r * pair, 0, i)),
        ],
        out_specs=pl.BlockSpec((token_block, cols), lambda i, r: (i, 0)),
        scratch_shapes=[pltpu.VMEM((token_block, cols), jnp.float32)],
        compiler_params=pltpu.CompilerParams(vmem_limit_bytes=48 << 20),
    )(act, weights, slots, mix)


MESH = pl.DeviceIdType.MESH
NN = (((1,), (0,)), ((), ()))


def layer_kernel(
    sizes,
    q_hbm,
    kv_hbm,
    ids_ref,
    sink_ref,
    gain_hbm,
    stream_hbm,
    ow_hbm,
    router_hbm,
    wg_hbm,
    wd_hbm,
    out_ref,
    q_ref,
    gain_ref,
    gains,
    kv_all,
    ids_all,
    stream_in,
    ow,
    router,
    routers,
    wg,
    wd,
    att_all,
    core_out,
    core_in,
    keep,
    x_out,
    x_in,
    h_all,
    y_ref,
    square_ref,
    logits_ref,
    token_ref,
    pick,
    spread,
    xg,
    scale_ref,
    unit_rows,
    act_all,
    parts,
    rs_out,
    rs_in,
    relay_in,
    local_sem,
    wg_sem,
    wd_sem,
    kv_send,
    kv_recv,
    ids_send,
    ids_recv,
    stream_send,
    stream_recv,
    att_send,
    att_recv,
    core_send,
    core_recv,
    x_send,
    x_recv,
    h_send,
    h_recv,
    act_send,
    act_recv,
    rs_send,
    rs_recv,
    relay_recv,
):
    seqs, tokens, rows, ctxs, width, cols, cap, local_experts, units, slots = sizes
    c, h, r = lax.axis_index("ctx"), lax.axis_index("head"), lax.axis_index("rep")
    all_rows = ctxs * rows
    wide = pl.cdiv(width, LANES) * LANES
    pad_cols = h_all.shape[3]
    core_dev, x_dev = (c, h ^ 1, r), (c, h ^ 2, r)
    partner = (h, c, r)

    def remote(src, dst, send, recv, device):
        return pltpu.make_async_remote_copy(
            src_ref=src,
            dst_ref=dst,
            send_sem=send,
            recv_sem=recv,
            device_id=device,
            device_id_type=MESH,
        )

    ow_copy = pltpu.make_async_copy(ow_hbm, ow, local_sem.at[0])
    router_copy = pltpu.make_async_copy(router_hbm, router, local_sem.at[1])
    q_copy = pltpu.make_async_copy(q_hbm, q_ref, local_sem.at[3])
    kv_local = pltpu.make_async_copy(kv_hbm, kv_all.at[c], local_sem.at[4])
    gain_copy = pltpu.make_async_copy(gain_hbm, gain_ref, local_sem.at[5])

    def wg_copy(e, slot):
        return pltpu.make_async_copy(
            wg_hbm.at[:, pl.ds(2 * e, 2), :], wg.at[slot], wg_sem.at[slot]
        )

    def wd_copy(e):
        return pltpu.make_async_copy(
            wd_hbm.at[pl.ds(2 * e, 2)], wd.at[pl.ds(2 * e, 2)], wd_sem.at[e]
        )

    barrier = pltpu.get_barrier_semaphore()
    for step in range(1, ctxs):
        pl.semaphore_signal(
            barrier, inc=1, device_id=(lax.rem(c + step, ctxs), h, r), device_id_type=MESH
        )
    pl.semaphore_signal(barrier, inc=1, device_id=core_dev, device_id_type=MESH)
    pl.semaphore_signal(barrier, inc=1, device_id=x_dev, device_id_type=MESH)

    @pl.when(c != h)
    def _():
        pl.semaphore_signal(barrier, inc=1, device_id=partner, device_id_type=MESH)

    kv_local.start()
    q_copy.start()
    gain_copy.start()
    router_copy.start()
    ow_copy.start()
    for e in range(min(slots, local_experts)):
        wg_copy(e, e).start()
    for e in range(local_experts):
        wd_copy(e).start()
    topk = ids_ref.shape[1]
    own_ids = jnp.concatenate([ids_ref[s] for s in range(seqs)], axis=1).astype(jnp.float32)
    ids_all[c] = jnp.concatenate(
        [own_ids, jnp.full((8 - topk, rows), -1.0, jnp.float32)], axis=0
    )
    for other in range(ctxs):

        @pl.when(other > c)
        def _():
            kv_all[other] = jnp.zeros(kv_all.shape[1:], jnp.bfloat16)

    parts[...] = jnp.zeros(parts.shape, jnp.bfloat16)
    pl.semaphore_wait(barrier, ctxs + 1 + (c != h).astype(jnp.int32))

    def kv_copy(src, dst):
        return remote(kv_hbm, kv_all.at[src], kv_send.at[dst], kv_recv.at[src], (dst, h, r))

    def ids_copy(src, dst):
        return remote(
            ids_all.at[src], ids_all.at[src], ids_send.at[dst], ids_recv.at[src], (dst, h, r)
        )

    def att_copy(src, dst, s):
        part = att_all.at[src, pl.ds(s * tokens, tokens)]
        return remote(part, part, att_send.at[dst, s], att_recv.at[src, s], (dst, h, r))

    for dst in range(ctxs):

        @pl.when(dst > c)
        def _():
            kv_copy(c, dst).start()

    stream_copy = remote(
        stream_hbm, stream_in, stream_send.at[0], stream_recv.at[0], partner
    )
    stream_local = pltpu.make_async_copy(stream_hbm, stream_in, local_sem.at[2])

    @pl.when(c != h)
    def _():
        stream_copy.start()

    @pl.when(c == h)
    def _():
        stream_local.start()

    for dst in range(ctxs):

        @pl.when(dst != c)
        def _():
            ids_copy(c, dst).start()

    kv_local.wait()
    q_copy.wait()
    for src in range(ctxs):

        @pl.when(src < c)
        def _():
            kv_copy(src, c).wait_recv()

    pairs = q_ref.shape[2] // LANES
    half = LANES // 2
    keys = ctxs * tokens
    group = pairs * tokens
    low_k = lax.broadcasted_iota(jnp.int32, (keys, LANES), 1) < half
    low_q = lax.broadcasted_iota(jnp.int32, (group, LANES), 1) < half
    key_pos = lax.broadcasted_iota(jnp.int32, (group, keys), 1)
    row_pos = lax.rem(lax.broadcasted_iota(jnp.int32, (group, keys), 0), tokens)
    visible = key_pos <= row_pos + c * tokens
    for s in range(seqs):
        kv = jnp.concatenate([kv_all[src, s] for src in range(ctxs)], axis=0).astype(jnp.float32)
        turned = pltpu.roll(kv, half, 1)
        key_sides = [jnp.where(low_k, kv, 0.0), jnp.where(low_k, 0.0, turned)]
        value_sides = [jnp.where(low_k, turned, 0.0), jnp.where(low_k, 0.0, kv)]
        q = jnp.concatenate(
            [q_ref[s, :, p * LANES : (p + 1) * LANES] for p in range(pairs)], axis=0
        )
        acc, totals = None, []
        for side in range(2):
            sink = jnp.concatenate(
                [
                    jnp.full((tokens, 1), sink_ref[2 * p + side], jnp.float32)
                    for p in range(pairs)
                ],
                axis=0,
            )
            scores = lax.dot_general(
                q, key_sides[side].astype(jnp.bfloat16), NT, preferred_element_type=jnp.float32
            ) * (half ** (-0.5))
            scores = jnp.where(visible, scores, -1e30)
            peak = jnp.maximum(sink, jnp.max(scores, axis=1, keepdims=True))
            terms = jnp.where(visible, jnp.exp(scores - peak), 0.0)
            totals.append(jnp.exp(sink - peak) + jnp.sum(terms, axis=1, keepdims=True))
            piece = lax.dot_general(
                terms.astype(jnp.bfloat16),
                value_sides[side].astype(jnp.bfloat16),
                NN,
                preferred_element_type=jnp.float32,
            )
            acc = piece if acc is None else acc + piece
        attended = (acc / jnp.where(low_q, totals[0], totals[1])).astype(jnp.bfloat16)
        for p in range(pairs):
            att_all[c, s * tokens : (s + 1) * tokens, p * LANES : (p + 1) * LANES] = attended[
                p * tokens : (p + 1) * tokens
            ]
        for dst in range(ctxs):

            @pl.when(dst != c)
            def _():
                att_copy(c, dst, s).start()

    for src in range(ctxs):

        @pl.when(src != c)
        def _():
            ids_copy(src, c).wait_recv()

    ids_row = jnp.concatenate([ids_all[src] for src in range(ctxs)], axis=1)
    mine = (
        lax.broadcasted_iota(jnp.int32, (local_experts, all_rows), 0) + c * local_experts
    ).astype(jnp.float32)
    member = jnp.zeros((local_experts, all_rows), jnp.bool_)
    for k in range(topk):
        member = member | (mine == ids_row[k : k + 1])
    before = lax.broadcasted_iota(jnp.int32, (all_rows, all_rows), 0) <= lax.broadcasted_iota(
        jnp.int32, (all_rows, all_rows), 1
    )
    rank = lax.dot_general(
        jnp.where(member, 1.0, 0.0).astype(jnp.bfloat16),
        jnp.where(before, 1.0, 0.0).astype(jnp.bfloat16),
        NN,
        preferred_element_type=jnp.float32,
    )
    slot_row = jnp.where(member, rank - 1.0, -1.0)
    slot_rows = lax.broadcasted_iota(jnp.int32, (cap, all_rows), 0).astype(jnp.float32)
    for e in range(local_experts):
        pick[e * cap : (e + 1) * cap, :] = jnp.where(
            slot_rows == slot_row[e : e + 1], 1.0, 0.0
        ).astype(jnp.bfloat16)
    both = jnp.concatenate(
        [ids_row, slot_row, jnp.zeros((LANES - 8 - local_experts, all_rows), jnp.float32)], axis=0
    )
    token_ref[...] = jnp.transpose(both)
    gain_copy.wait()
    router_copy.wait()
    gain = gain_ref[...].reshape(1, width)
    for block in range(ctxs):
        here = slice(block * cols, (block + 1) * cols)
        gains[block] = jnp.concatenate(
            [jnp.broadcast_to(gain[:, here], (8, cols)), jnp.zeros((8, pad_cols - cols), jnp.float32)],
            axis=1,
        )
        routers[block] = jnp.concatenate(
            [
                router[:, here],
                jnp.zeros((router.shape[0], pad_cols - cols), jnp.bfloat16),
            ],
            axis=1,
        )

    ow_copy.wait()
    side, core = h // 2, lax.rem(h, 2)

    def widened(values):
        extra = jnp.zeros((values.shape[0], pad_cols - cols), jnp.float32)
        return jnp.concatenate([values, extra], axis=1)

    def projected(blocks, s):
        stacked = jnp.concatenate(
            [att_all[block, s * tokens : (s + 1) * tokens] for block in blocks], axis=0
        )
        return widened(
            lax.dot_general(stacked, ow[...], NT, preferred_element_type=jnp.float32)
        )

    def core_copy(s):
        return remote(core_out.at[s], core_in.at[s], core_send.at[s], core_recv.at[s], core_dev)

    def x_copy(s):
        return remote(x_out.at[s], x_in.at[s], x_send.at[s], x_recv.at[s], x_dev)

    for s in range(seqs):
        for block in range(ctxs):

            @pl.when(block != c)
            def _():
                att_copy(block, c, s).wait_recv()

        across = (1 - side, side)
        core_out[s] = projected([2 * to + 1 - core for to in across], s).astype(jnp.bfloat16)
        core_copy(s).start()
        keep[s] = projected([2 * to + core for to in across], s)
        core_copy(s).wait_recv()
        x_out[s] = (keep[s, :tokens] + core_in[s, :tokens].astype(jnp.float32)).astype(
            jnp.bfloat16
        )
        x_copy(s).start()

    @pl.when(c != h)
    def _():
        stream_copy.wait_recv()

    @pl.when(c == h)
    def _():
        stream_local.wait()

    def h_copy(way, block, row, s, device):
        part = h_all.at[block, row, pl.ds(s * tokens, tokens)]
        return remote(part, part, h_send.at[way, block, s], h_recv.at[block, row, s], device)

    def h_core(block, row, s):
        return h_copy(jnp.where(row == h, 0, 1), block, row, s, core_dev)

    def h_x(block, s):
        return h_copy(2, block, h, s, x_dev)

    def h_right(block, s):
        return h_copy(3, block, h, s, (jnp.minimum(c + 1, ctxs - 1), h, r))

    def h_left(block, s):
        return h_copy(4, block, h, s, (jnp.maximum(c - 1, 0), h, r))

    def arrived(block, row, s):
        h_copy(0, block, row, s, core_dev).wait_recv()

    for s in range(seqs):
        kept = (
            keep[s, tokens:]
            + core_in[s, tokens:].astype(jnp.float32)
            + widened(stream_in[s].astype(jnp.float32))
        )
        x_copy(s).wait_recv()
        h_all[c, h, s * tokens : (s + 1) * tokens] = (
            kept + x_in[s].astype(jnp.float32)
        ).astype(jnp.bfloat16)
        h_x(c, s).start()

        @pl.when(c < ctxs - 1)
        def _():
            h_right(c, s).start()

        @pl.when(c > 0)
        def _():
            h_left(c, s).start()

        h_core(c, h, s).start()

    square_ref[...] = jnp.zeros(square_ref.shape, jnp.float32)
    logits_ref[...] = jnp.zeros(logits_ref.shape, jnp.float32)

    def take(block):
        for s in range(seqs):
            arrived(block, h ^ 1, s)
            arrived(block, h ^ 3, s)
        for row in range(ctxs):
            here = slice(row * rows, (row + 1) * rows)
            piece = h_all[block, row].astype(jnp.float32)
            y_ref[here, :] = (piece * gains[block][:1]).astype(jnp.bfloat16)
            square = piece * piece
            square_ref[here, :] += sum(
                square[:, i : i + LANES] for i in range(0, pad_cols, LANES)
            )
        xg[block] = lax.dot_general(
            pick[...], y_ref[...], NN, preferred_element_type=jnp.float32
        ).astype(jnp.bfloat16)
        logits_ref[...] += lax.dot_general(
            y_ref[...], routers[block], NT, preferred_element_type=jnp.float32
        )

    for d in range(1, ctxs + 1):
        for s in range(seqs):

            @pl.when(c - d >= 0)
            def _():
                arrived(c - d, h, s)

                @pl.when(c < ctxs - 1)
                def _():
                    h_right(c - d, s).start()

                h_x(c - d, s).start()
                h_core(c - d, h, s).start()

            @pl.when(c + d < ctxs)
            def _():
                arrived(c + d, h, s)

                @pl.when(c > 0)
                def _():
                    h_left(c + d, s).start()

                h_x(c + d, s).start()
                h_core(c + d, h, s).start()

            @pl.when(c - (d - 1) >= 0)
            def _():
                arrived(c - (d - 1), h ^ 2, s)
                h_core(c - (d - 1), h ^ 2, s).start()

            if d > 1:

                @pl.when(c + (d - 1) < ctxs)
                def _():
                    arrived(c + (d - 1), h ^ 2, s)
                    h_core(c + (d - 1), h ^ 2, s).start()

        @pl.when(c - (d - 1) >= 0)
        def _():
            take(c - (d - 1))

        if d > 1:

            @pl.when(c + (d - 1) < ctxs)
            def _():
                take(c + (d - 1))

    inverse = lax.rsqrt(jnp.sum(square_ref[...], axis=1, keepdims=True) / width + 1e-05)
    square_ref[...] = jnp.broadcast_to(inverse, square_ref.shape)
    inverse_row = jnp.transpose(square_ref[...])[:1]
    first = inverse_row.astype(jnp.bfloat16)
    rest = inverse_row - first.astype(jnp.float32)
    second = rest.astype(jnp.bfloat16)
    third = (rest - second.astype(jnp.float32)).astype(jnp.bfloat16)
    in_parts = jnp.concatenate(
        [part.astype(jnp.float32) for part in (first, second, third)]
        + [jnp.zeros((5, all_rows), jnp.float32)],
        axis=0,
    ).astype(jnp.bfloat16)
    for e in range(local_experts):
        found = lax.dot_general(
            in_parts, pick[e * cap : (e + 1) * cap, :], NT, preferred_element_type=jnp.float32
        )
        scale_ref[e] = jnp.broadcast_to(jnp.sum(found, axis=0, keepdims=True), (8, cap))

    def act_core(shard, e):
        return remote(
            act_all.at[shard, e],
            act_all.at[shard, e],
            act_send.at[jnp.where(shard == h, 0, 1), e],
            act_recv.at[shard, e],
            core_dev,
        )

    def act_x(e):
        return remote(
            act_all.at[h, e], act_all.at[h, e], act_send.at[2, e], act_recv.at[h, e], x_dev
        )

    def act_arrived(shard, e):
        remote(
            act_all.at[shard, e],
            act_all.at[shard, e],
            act_send.at[0, e],
            act_recv.at[shard, e],
            core_dev,
        ).wait_recv()

    lead = wide - width
    packed = act_all.shape[3]

    @pl.loop(0, local_experts)
    def _(e):
        slot = lax.rem(e, slots)
        wg_copy(e, slot).wait()
        pieces = [
            xg[block, pl.ds(pl.multiple_of(e * cap, cap), cap), :][:, :cols]
            for block in range(ctxs)
        ]
        blank = [jnp.zeros((cap, lead), jnp.bfloat16)]
        rows_in = jnp.concatenate(pieces + blank, axis=1)
        shifted = jnp.concatenate(blank + pieces, axis=1)
        factor = scale_ref[e][:1]
        gate = factor * lax.dot_general(
            wg[slot, :, :, :wide].reshape(2 * units, wide),
            rows_in,
            NT,
            preferred_element_type=jnp.float32,
        )
        up = factor * lax.dot_general(
            wg[slot, :, :, 2 * width - wide :].reshape(2 * units, wide),
            shifted,
            NT,
            preferred_element_type=jnp.float32,
        )
        active = gate * jax.nn.sigmoid(1.702 * gate) * (up + 1.0)
        unit_rows[...] = jnp.concatenate(
            [active, jnp.zeros((2 * units, LANES - cap), jnp.float32)], axis=1
        )
        stacked = jnp.concatenate(
            [unit_rows[pl.ds(u, units, stride=2), :] for u in range(2)]
            + [jnp.zeros((packed - 2 * units, LANES), jnp.float32)],
            axis=0,
        )
        act_all[h, e] = jnp.transpose(stacked)[:cap].astype(jnp.bfloat16)
        act_x(e).start()
        act_core(h, e).start()

        @pl.when(e + slots < local_experts)
        def _():
            wg_copy(e + slots, slot).start()

        @pl.when(e >= 2)
        def _():
            act_arrived(h ^ 2, e - 2)
            act_core(h ^ 2, e - 2).start()

    by_token = token_ref[...]
    logits = logits_ref[...] * square_ref[:, :1]
    experts = logits.shape[1]
    expert_lane = lax.broadcasted_iota(jnp.int32, (all_rows, experts), 1).astype(jnp.float32)
    named = jnp.zeros((all_rows, experts), jnp.bool_)
    for k in range(topk):
        named = named | (expert_lane == by_token[:, k : k + 1])
    top = jnp.max(jnp.where(named, logits, -1e30), axis=1, keepdims=True)
    weight = jnp.where(named, jnp.exp(logits - top), 0.0)
    mix = weight / jnp.sum(weight, axis=1, keepdims=True)
    mix = jnp.concatenate([mix, jnp.zeros((all_rows, LANES - experts), jnp.float32)], axis=1)
    mix = pltpu.roll(mix, lax.rem(LANES - c * local_experts, LANES), 1)
    slot_lane = lax.broadcasted_iota(jnp.int32, (all_rows, LANES), 1).astype(jnp.float32)
    for e in range(local_experts):
        spread[:, e * LANES : (e + 1) * LANES] = jnp.where(
            slot_lane == by_token[:, 8 + e : 9 + e], mix[:, e : e + 1], 0.0
        ).astype(jnp.bfloat16)

    for e in range(local_experts - 2, local_experts):
        act_arrived(h ^ 2, e)
        act_core(h ^ 2, e).start()

    @pl.loop(0, local_experts)
    def _(e):
        wd_copy(e).wait()
        act_arrived(h ^ 1, e)
        act_arrived(h ^ 3, e)
        total = None
        for u in range(2):
            hidden = jnp.concatenate(
                [act_all[shard, e][:, u * units : (u + 1) * units] for shard in range(4)], axis=1
            )
            piece = lax.dot_general(
                hidden, wd[2 * e + u], NN, preferred_element_type=jnp.float32
            )
            total = piece if total is None else total + piece
        parts[pl.ds(pl.multiple_of(e * LANES, LANES), cap), :] = jnp.concatenate(
            [total, jnp.zeros((cap, pad_cols - cols), jnp.float32)], axis=1
        ).astype(jnp.bfloat16)

    def rs_copy(src, dst):
        return remote(rs_out.at[dst], rs_in.at[src], rs_send.at[dst], rs_recv.at[src], (dst, h, r))

    def combined(block):
        return lax.dot_general(
            spread[pl.ds(pl.multiple_of(block * rows, rows), rows), :],
            parts[...],
            NN,
            preferred_element_type=jnp.float32,
        )

    outer = (c == 0) | (c == ctxs - 1)
    far = ctxs - 1 - c
    relay_dst = jnp.where(c == 0, 1, 2)
    end_dst = jnp.where(c == 1, 3, 0)
    relay_copy = remote(
        rs_out.at[far], relay_in, rs_send.at[far], relay_recv.at[0], (relay_dst, h, r)
    )

    @pl.when(outer)
    def _():
        rs_out[far] = combined(far).astype(jnp.bfloat16)
        relay_copy.start()
        for dst in (ctxs - 1 - relay_dst, relay_dst):
            rs_out[dst] = combined(dst).astype(jnp.bfloat16)
            rs_copy(c, dst).start()

    @pl.when(jnp.logical_not(outer))
    def _():
        for dst in (ctxs - 1 - c, ctxs - 1 - end_dst):
            rs_out[dst] = combined(dst).astype(jnp.bfloat16)
            rs_copy(c, dst).start()
        ends = combined(end_dst)
        relay_copy.wait_recv()
        rs_out[end_dst] = (ends + relay_in[...].astype(jnp.float32)).astype(jnp.bfloat16)
        rs_copy(c, end_dst).start()

    keep[0] = combined(c) + h_all[h, c].astype(jnp.float32)
    for src in range(ctxs):
        sends_here = (src != c) & jnp.logical_not(outer & (src == far))

        @pl.when(sends_here)
        def _():
            rs_copy(src, c).wait_recv()
            keep[0] += rs_in[src].astype(jnp.float32)

    total = keep[0]
    out_ref[...] = total[:, :cols].astype(jnp.bfloat16).reshape(out_ref.shape)

    for dst in range(ctxs):

        @pl.when(dst > c)
        def _():
            kv_copy(c, dst).wait_send()

        @pl.when(dst != c)
        def _():
            ids_copy(c, dst).wait_send()
            for s in range(seqs):
                att_copy(c, dst, s).wait_send()
            rs_copy(c, dst).wait_send()

    @pl.when(c != h)
    def _():
        stream_copy.wait_send()

    for s in range(seqs):
        x_copy(s).wait_send()
        core_copy(s).wait_send()
        for block in range(ctxs):
            h_x(block, s).wait_send()
            h_core(block, h, s).wait_send()
            h_core(block, h ^ 2, s).wait_send()

            @pl.when((c < ctxs - 1) & (block <= c))
            def _():
                h_right(block, s).wait_send()

            @pl.when((c > 0) & (block >= c))
            def _():
                h_left(block, s).wait_send()

    for e in range(local_experts):
        act_x(e).wait_send()
        act_core(h, e).wait_send()
        act_core(h ^ 2, e).wait_send()


def layer_call(queries, keyvals, sinks, stream, out_weight, gain, router, ids, w_gate_up, w_down):
    seqs, tokens, q_cols = queries.shape
    cols = stream.shape[2]
    ctxs = lax.axis_size("ctx")
    rows = seqs * tokens
    width = gain.shape[0]
    halves, units, wide_w = w_gate_up.shape
    local_experts = halves // 2
    all_rows = ctxs * rows
    cap = all_rows * 3 // 16
    pad_cols = pl.cdiv(cols, LANES) * LANES
    packed = pl.cdiv(2 * units, LANES) * LANES
    slots = min(4, local_experts)
    sizes = (seqs, tokens, rows, ctxs, width, cols, cap, local_experts, units, slots)
    bf16, f32 = jnp.bfloat16, jnp.float32
    dma = pltpu.SemaphoreType.DMA
    vmem = pl.BlockSpec(memory_space=pltpu.VMEM)
    hbm = pl.BlockSpec(memory_space=pl.ANY)
    return pl.pallas_call(
        functools.partial(layer_kernel, sizes),
        out_shape=jax.ShapeDtypeStruct((seqs, tokens, cols), bf16),
        in_specs=[hbm, hbm, vmem, pl.BlockSpec(memory_space=pltpu.SMEM)] + [hbm] * 6,
        out_specs=vmem,
        scratch_shapes=[
            pltpu.VMEM(queries.shape, bf16),
            pltpu.VMEM(gain.shape, f32),
            pltpu.VMEM((ctxs, 8, pad_cols), f32),
            pltpu.VMEM((ctxs, seqs, tokens, keyvals.shape[3]), bf16),
            pltpu.VMEM((ctxs, 8, LANES), f32),
            pltpu.VMEM((seqs, tokens, cols), bf16),
            pltpu.VMEM(out_weight.shape[::-1], bf16),
            pltpu.VMEM(router.shape[::-1], bf16),
            pltpu.VMEM((ctxs, router.shape[1], pad_cols), bf16),
            pltpu.VMEM((slots, units, 2, wide_w), bf16),
            pltpu.VMEM(w_down.shape, bf16),
            pltpu.VMEM((ctxs, rows, q_cols), bf16),
            pltpu.VMEM((seqs, 2 * tokens, pad_cols), bf16),
            pltpu.VMEM((seqs, 2 * tokens, pad_cols), bf16),
            pltpu.VMEM((seqs, 2 * tokens, pad_cols), f32),
            pltpu.VMEM((seqs, tokens, pad_cols), bf16),
            pltpu.VMEM((seqs, tokens, pad_cols), bf16),
            pltpu.VMEM((ctxs, 4, rows, pad_cols), bf16),
            pltpu.VMEM((all_rows, pad_cols), bf16),
            pltpu.VMEM((all_rows, LANES), f32),
            pltpu.VMEM((all_rows, router.shape[1]), f32),
            pltpu.VMEM((all_rows, LANES), f32),
            pltpu.VMEM((local_experts * cap, all_rows), bf16),
            pltpu.VMEM((all_rows, local_experts * LANES), bf16),
            pltpu.VMEM((ctxs, local_experts * cap, pad_cols), bf16),
            pltpu.VMEM((local_experts, 8, cap), f32),
            pltpu.VMEM((2 * units, LANES), f32),
            pltpu.VMEM((4, local_experts, cap, packed), bf16),
            pltpu.VMEM((local_experts * LANES, pad_cols), bf16),
            pltpu.VMEM((ctxs, rows, pad_cols), bf16),
            pltpu.VMEM((ctxs, rows, pad_cols), bf16),
            pltpu.VMEM((rows, pad_cols), bf16),
            dma((6,)),
            dma((slots,)),
            dma((local_experts,)),
            dma((ctxs,)),
            dma((ctxs,)),
            dma((ctxs,)),
            dma((ctxs,)),
            dma((1,)),
            dma((1,)),
            dma((ctxs, seqs)),
            dma((ctxs, seqs)),
            dma((seqs,)),
            dma((seqs,)),
            dma((seqs,)),
            dma((seqs,)),
            dma((5, ctxs, seqs)),
            dma((ctxs, 4, seqs)),
            dma((3, local_experts)),
            dma((4, local_experts)),
            dma((ctxs,)),
            dma((ctxs,)),
            dma((1,)),
        ],
        compiler_params=pltpu.CompilerParams(
            vmem_limit_bytes=67043328, collective_id=0, has_side_effects=True
        ),
    )(
        queries,
        keyvals.reshape(seqs, tokens, keyvals.shape[3]),
        jnp.transpose(ids, (0, 2, 1)),
        sinks,
        gain,
        stream,
        out_weight.T,
        router.T,
        jnp.transpose(w_gate_up, (1, 0, 2)),
        w_down,
    )


def one_chip_row(queries, keyvals, stream, out_weight, router, ids, w_gate_up):
    ctxs, heads = lax.axis_size("ctx"), lax.axis_size("head")
    rows = queries.shape[0] * queries.shape[1]
    return (
        ctxs == heads == 4
        and rows == LANES
        and keyvals.shape[2] == 1
        and keyvals.shape[3] == LANES
        and out_weight.shape[1] == stream.shape[2]
        and w_gate_up.shape[0] == 16
        and ids.shape[2] <= 8
        and router.shape[1] <= LANES
    )


def on_device(
    queries, keyvals, sinks, stream, out_weight, norm_gain, router, expert_ids, w_gate_up, w_down
):
    if one_chip_row(queries, keyvals, stream, out_weight, router, expert_ids, w_gate_up):
        return layer_call(
            queries,
            keyvals,
            sinks,
            stream,
            out_weight,
            norm_gain,
            router,
            expert_ids,
            w_gate_up,
            w_down,
        )
    ctx_count = lax.axis_size("ctx")
    local_seqs = queries.shape[0]
    tokens = queries.shape[1]
    row_count = local_seqs * tokens
    kv_local = keyvals.shape[2]
    head_dim = keyvals.shape[3] // 2
    q_local = queries.shape[2] // head_dim
    query_group_size = q_local // kv_local
    wide_rows = query_group_size * tokens
    col_width = stream.shape[2]
    first_pos = lax.axis_index("ctx") * tokens
    last_pos = first_pos + tokens - 1
    score_scale = head_dim ** (-0.5)
    scaled_queries = queries * jnp.asarray(score_scale, jnp.bfloat16)
    query_grid = scaled_queries.reshape(local_seqs, tokens, kv_local, query_group_size, head_dim)
    query_wide = jnp.transpose(query_grid, (0, 2, 3, 1, 4)).reshape(
        local_seqs, kv_local, wide_rows, head_dim
    )
    positions = first_pos + jnp.tile(jnp.arange(tokens), query_group_size)
    sink_rows = jnp.repeat(sinks.reshape(kv_local, query_group_size), tokens, axis=1)
    sink_grid = jnp.broadcast_to(sink_rows[None], (local_seqs, kv_local, wide_rows))
    start_state = (
        sink_grid,
        jnp.ones_like(sink_grid),
        jnp.zeros((local_seqs, kv_local, head_dim, wide_rows), jnp.float32),
    )

    def attend_block(running, shard_piece):
        peak_old, denom_old, accum_old = running
        key_block = shard_piece[..., :head_dim]
        value_block = shard_piece[..., head_dim:]
        scores = jnp.einsum(
            "skmd,snkd->sknm", query_wide, key_block, preferred_element_type=jnp.float32
        )
        key_pos = jnp.arange(shard_piece.shape[1])
        visible = key_pos[:, None] <= positions[None, :]
        masked = jnp.where(visible[None, None], scores, -jnp.inf)
        peak_new = jnp.maximum(peak_old, jnp.max(masked, axis=2))
        exp_terms = jnp.exp(masked - peak_new[:, :, None, :])
        factor = jnp.exp(peak_old - peak_new)
        denom_new = denom_old * factor + jnp.sum(exp_terms, axis=2)
        accum_new = accum_old * factor[:, :, None, :] + jnp.einsum(
            "sknm,snkd->skdm",
            exp_terms.astype(jnp.bfloat16),
            value_block,
            preferred_element_type=jnp.float32,
        )
        return (peak_new, denom_new, accum_new)

    shard_piece = lax.all_gather(keyvals, "ctx", axis=1, tiled=True)

    def keep_state(state_in):
        return state_in

    def update_state(state_in):
        return attend_block(state_in, shard_piece)

    peak_fin, denom_fin, accum_fin = lax.cond(
        jnp.int32(0) > last_pos, keep_state, update_state, start_state
    )
    normalized = (accum_fin / denom_fin[:, :, None, :]).reshape(
        local_seqs, kv_local, head_dim, query_group_size, tokens
    )
    attended = (
        jnp.transpose(normalized, (0, 4, 1, 3, 2))
        .reshape(row_count, q_local * head_dim)
        .astype(jnp.bfloat16)
    )
    token_ids = lax.all_gather(
        expert_ids.reshape(row_count, expert_ids.shape[2]).T, "ctx", axis=1, tiled=True
    )
    all_rows = ctx_count * row_count
    halves = w_gate_up.shape[0]
    units = w_gate_up.shape[1]
    token_block = min(all_rows, 8 * tokens)
    cap = token_block // tokens * (3 * tokens // 16)
    row_expert = (lax.axis_index("ctx") * halves + jnp.arange(halves)) // 2
    named = jnp.any(token_ids[:, None, :] == row_expert[None, :, None], axis=0)
    counted = named.astype(jnp.int32).reshape(halves, all_rows // token_block, token_block)
    rank = jnp.cumsum(counted, axis=2) - 1
    slots = jnp.where(named, rank.reshape(halves, all_rows), -1).reshape(halves, 1, all_rows)
    width = norm_gain.shape[0]
    head_count = lax.axis_size("head")
    swapped = ctx_count == head_count and out_weight.shape[1] == col_width
    if swapped:
        pairs = [
            (first * head_count + second, second * head_count + first)
            for first in range(ctx_count)
            for second in range(head_count)
        ]
        turned = lax.ppermute(
            stream.reshape(row_count, col_width), ("ctx", "head"), perm=pairs
        )
        every_row = lax.all_gather(attended, "ctx", axis=0, tiled=True)
        partial_proj = jnp.dot(every_row, out_weight, preferred_element_type=jnp.float32)
        summed = lax.psum_scatter(
            partial_proj.astype(jnp.bfloat16), "head", scatter_dimension=0, tiled=True
        )
        turned_state = summed.astype(jnp.float32) + turned.astype(jnp.float32)
        every_state = lax.all_gather(
            turned_state.astype(jnp.bfloat16), ("head", "ctx"), axis=0, tiled=False
        )
    else:
        partial_proj = jnp.dot(attended, lax.all_gather(out_weight, "ctx", axis=1, tiled=True), preferred_element_type=jnp.float32)
        own_stream = stream.reshape(row_count, col_width).astype(jnp.float32)
        summed = lax.psum_scatter(
            partial_proj.astype(jnp.bfloat16), "head", scatter_dimension=1, tiled=True
        )
        own_state = (summed.astype(jnp.float32) + own_stream).astype(jnp.bfloat16)
        every_state = lax.all_gather(own_state, ("ctx", "head"), axis=0, tiled=False)
    every_state = every_state.reshape(ctx_count, width // col_width, row_count, col_width)
    expert_count = router.shape[1]
    unit_rows = jnp.transpose(w_gate_up, (1, 0, 2)).reshape(units * halves, w_gate_up.shape[2])
    router_rows = jnp.pad(router.T, ((0, 0), (0, -width % LANES)))
    gain = norm_gain.reshape(width // col_width, 1, col_width)
    active, logits = gate_up_call(
        every_state, gain, router_rows, unit_rows, slots, units, token_block, cap
    )
    member = jnp.any(token_ids[:, None, :] == jnp.arange(expert_count)[None, :, None], axis=0)
    masked = jnp.where(member, logits, -jnp.inf)
    mix_all = jax.nn.softmax(masked, axis=0)
    chosen_rows = (row_expert[:, None] == jnp.arange(expert_count)[None, :]).astype(jnp.float32)
    mix_rows = jnp.dot(chosen_rows, mix_all, precision=lax.Precision.HIGHEST)
    mix_rows = mix_rows.reshape(halves, 1, all_rows)
    every_active = lax.all_gather(active.reshape(-1, units), "head", axis=0, tiled=True)
    every_active = every_active.reshape(width // col_width, *active.shape)
    partial_out = down_call(every_active, w_down, slots, mix_rows, token_block)
    combined = lax.psum_scatter(partial_out, "ctx", scatter_dimension=0, tiled=True)
    if swapped:
        own_state = every_state[lax.axis_index("ctx"), lax.axis_index("head")]
    layer_out = (own_state.astype(jnp.float32) + combined.astype(jnp.float32)).astype(jnp.bfloat16)
    return layer_out.reshape(local_seqs, tokens, col_width)


def solution(mesh):
    placed = (
        P("rep", "ctx", "head"),
        P("rep", "ctx", "head", None),
        P("head"),
        P("rep", "ctx", "head"),
        P("head", "ctx"),
        P(),
        P(),
        P("rep", "ctx", None),
        P("ctx", "head", None),
        P("ctx", None, "head"),
    )
    return jax.shard_map(
        on_device, mesh=mesh, in_specs=placed, out_specs=P("rep", "ctx", "head"), check_vma=False
    )
```

```python
import functools

import jax
import jax.numpy as jnp
from jax import lax
from jax.experimental import pallas as pl
from jax.experimental.pallas import tpu as pltpu
from jax.sharding import PartitionSpec as P


NT = (((1,), (1,)), ((), ()))
TN = (((0,), (0,)), ((), ()))
LANES = 128


def one_hot_rows(slots, cap, value):
    rows = lax.broadcasted_iota(jnp.int32, (cap, slots.shape[1]), 0)
    return jnp.where(rows == slots, value, 0.0).astype(jnp.bfloat16)


def gate_up_kernel(
    halves,
    units,
    state_ref,
    gain_ref,
    router_ref,
    w_ref,
    slot_ref,
    out_ref,
    logits_ref,
    act_ref,
    xg_ref,
    xu_ref,
):
    step = pl.program_id(1)
    groups, shards, group_rows, cols = state_ref.shape

    @pl.when(step == 0)
    def _():
        for group in range(groups):
            pieces = [state_ref[group, shard].astype(jnp.float32) for shard in range(shards)]
            square = sum(jnp.sum(piece * piece, axis=1, keepdims=True) for piece in pieces)
            inverse = lax.rsqrt(square / (shards * cols) + 1e-05)
            scaled = [
                (piece * inverse * gain_ref[shard]).astype(jnp.bfloat16)
                for shard, piece in enumerate(pieces)
            ]
            extra = xg_ref.shape[1] - shards * cols
            blank = [jnp.zeros((group_rows, extra), jnp.bfloat16)] if extra else []
            here = slice(group * group_rows, (group + 1) * group_rows)
            xg_ref[here, :] = jnp.concatenate(scaled + blank, axis=1)
            xu_ref[here, :] = jnp.concatenate(blank + scaled, axis=1)
        logits_ref[...] = lax.dot_general(
            router_ref[...], xg_ref[...], NT, preferred_element_type=jnp.float32
        )

    rows, wide = w_ref.shape[0], xg_ref.shape[1]
    gate = lax.dot_general(w_ref[:, :wide], xg_ref[...], NT, preferred_element_type=jnp.float32)
    up = lax.dot_general(
        w_ref[:, w_ref.shape[1] - wide :], xu_ref[...], NT, preferred_element_type=jnp.float32
    )
    active = gate * jax.nn.sigmoid(1.702 * gate) * (up + 1.0)
    slabs = act_ref.shape[0]
    for slab in range(slabs):
        act_ref[slab, pl.ds(step * rows, rows), :] = active[:, slab * LANES : (slab + 1) * LANES]

    @pl.when(step == pl.num_programs(1) - 1)
    def _():
        for row in range(halves):
            wanted = pl.ds(row, units, stride=halves) if halves > 1 else pl.ds(0, units)
            picked = jnp.concatenate([act_ref[slab, wanted, :] for slab in range(slabs)], axis=1)
            spread = one_hot_rows(slot_ref[row], out_ref.shape[2], 1.0)
            out_ref[row, 0] = lax.dot_general(
                spread, picked.astype(jnp.bfloat16), NT, preferred_element_type=jnp.float32
            ).astype(jnp.bfloat16)


def gate_up_call(state, gain, router, weights, slots, units, token_block, cap):
    halves = slots.shape[0]
    sources, shards, group_rows, cols = state.shape
    groups = token_block // group_rows
    blocks = sources // groups
    experts, wide = router.shape
    wide_w = weights.shape[1]
    sizes = [
        size
        for size in range(1, units + 1)
        if units % size == 0
        and (size == units or (size * halves) % 16 == 0)
        and size * halves * wide_w * 2 <= 4 << 20
    ]
    size = sizes[-1]
    return pl.pallas_call(
        functools.partial(gate_up_kernel, halves, units),
        grid=(blocks, units // size),
        out_shape=(
            jax.ShapeDtypeStruct((halves, blocks, cap, units), jnp.bfloat16),
            jax.ShapeDtypeStruct((experts, blocks * token_block), jnp.float32),
        ),
        in_specs=[
            pl.BlockSpec((groups, shards, group_rows, cols), lambda i, j: (i, 0, 0, 0)),
            pl.BlockSpec((shards, 1, cols), lambda i, j: (0, 0, 0)),
            pl.BlockSpec((experts, wide), lambda i, j: (0, 0)),
            pl.BlockSpec((size * halves, wide_w), lambda i, j: (j, 0)),
            pl.BlockSpec((halves, 1, token_block), lambda i, j: (0, 0, i)),
        ],
        out_specs=(
            pl.BlockSpec((halves, 1, cap, units), lambda i, j: (0, i, 0, 0)),
            pl.BlockSpec((experts, token_block), lambda i, j: (0, i)),
        ),
        scratch_shapes=[
            pltpu.VMEM((token_block // LANES, units * halves, LANES), jnp.float32),
            pltpu.VMEM((token_block, wide), jnp.bfloat16),
            pltpu.VMEM((token_block, wide), jnp.bfloat16),
        ],
        compiler_params=pltpu.CompilerParams(vmem_limit_bytes=56 << 20),
    )(state, gain, router, weights, slots)


def down_kernel(act_ref, w_ref, slot_ref, mix_ref, out_ref, total_ref):
    step = pl.program_id(1)
    part = None
    for row in range(w_ref.shape[0]):
        pieces = [act_ref[shard, row, 0] for shard in range(act_ref.shape[0])]
        hidden = jnp.concatenate(pieces, axis=1)
        piece = jnp.dot(hidden, w_ref[row], preferred_element_type=jnp.float32)
        part = piece if part is None else part + piece
    spread = one_hot_rows(slot_ref[0], act_ref.shape[3], mix_ref[0])
    added = lax.dot_general(
        spread, part.astype(jnp.bfloat16), TN, preferred_element_type=jnp.float32
    )

    @pl.when(step == 0)
    def _():
        total_ref[...] = added

    @pl.when(step != 0)
    def _():
        total_ref[...] += added

    @pl.when(step == pl.num_programs(1) - 1)
    def _():
        out_ref[...] = total_ref[...].astype(jnp.bfloat16)


def down_call(act, weights, slots, mix, token_block):
    shards, halves, blocks, cap, units = act.shape
    hidden, cols = weights.shape[1:]
    pair = 2 if halves % 2 == 0 else 1
    return pl.pallas_call(
        down_kernel,
        grid=(blocks, halves // pair),
        out_shape=jax.ShapeDtypeStruct((blocks * token_block, cols), jnp.bfloat16),
        in_specs=[
            pl.BlockSpec((shards, pair, 1, cap, units), lambda i, r: (0, r, i, 0, 0)),
            pl.BlockSpec((pair, hidden, cols), lambda i, r: (r, 0, 0)),
            pl.BlockSpec((1, 1, token_block), lambda i, r: (r * pair, 0, i)),
            pl.BlockSpec((1, 1, token_block), lambda i, r: (r * pair, 0, i)),
        ],
        out_specs=pl.BlockSpec((token_block, cols), lambda i, r: (i, 0)),
        scratch_shapes=[pltpu.VMEM((token_block, cols), jnp.float32)],
        compiler_params=pltpu.CompilerParams(vmem_limit_bytes=48 << 20),
    )(act, weights, slots, mix)


MESH = pl.DeviceIdType.MESH
NN = (((1,), (0,)), ((), ()))


def layer_kernel(
    sizes,
    q_hbm,
    kv_hbm,
    ids_ref,
    sink_ref,
    gain_hbm,
    stream_hbm,
    ow_hbm,
    router_hbm,
    wg_hbm,
    wd_hbm,
    out_ref,
    q_ref,
    gain_ref,
    gains,
    kv_all,
    ids_all,
    stream_in,
    ow,
    router,
    routers,
    wg,
    wd,
    att_all,
    core_out,
    core_in,
    keep,
    x_out,
    x_in,
    h_all,
    y_ref,
    square_ref,
    logits_ref,
    token_ref,
    pick,
    spread,
    xg,
    scale_ref,
    unit_rows,
    act_all,
    parts,
    rs_out,
    rs_in,
    relay_in,
    hidden_ref,
    total_ref,
    local_sem,
    wg_sem,
    wd_sem,
    kv_send,
    kv_recv,
    ids_send,
    ids_recv,
    stream_send,
    stream_recv,
    att_send,
    att_recv,
    core_send,
    core_recv,
    x_send,
    x_recv,
    h_send,
    h_recv,
    act_send,
    act_recv,
    rs_send,
    rs_recv,
    relay_recv,
    onward_send,
):
    seqs, tokens, rows, ctxs, width, cols, cap, local_experts, units, slots = sizes
    c, h, r = lax.axis_index("ctx"), lax.axis_index("head"), lax.axis_index("rep")
    all_rows = ctxs * rows
    wide = pl.cdiv(width, LANES) * LANES
    pad_cols = h_all.shape[3]
    core_dev, x_dev = (c, h ^ 1, r), (c, h ^ 2, r)
    partner = (h, c, r)

    def remote(src, dst, send, recv, device):
        return pltpu.make_async_remote_copy(
            src_ref=src,
            dst_ref=dst,
            send_sem=send,
            recv_sem=recv,
            device_id=device,
            device_id_type=MESH,
        )

    ow_copy = pltpu.make_async_copy(ow_hbm, ow, local_sem.at[0])
    router_copy = pltpu.make_async_copy(router_hbm, router, local_sem.at[1])
    q_copy = pltpu.make_async_copy(q_hbm, q_ref, local_sem.at[3])
    kv_local = pltpu.make_async_copy(kv_hbm, kv_all.at[c], local_sem.at[4])
    gain_copy = pltpu.make_async_copy(gain_hbm, gain_ref, local_sem.at[5])

    def wg_copy(e, slot):
        return pltpu.make_async_copy(
            wg_hbm.at[:, pl.ds(2 * e, 2), :], wg.at[slot], wg_sem.at[slot]
        )

    def wd_copy(e):
        return pltpu.make_async_copy(
            wd_hbm.at[pl.ds(2 * e, 2)], wd.at[pl.ds(2 * e, 2)], wd_sem.at[e]
        )

    barrier = pltpu.get_barrier_semaphore()
    for step in range(1, ctxs):
        pl.semaphore_signal(
            barrier, inc=1, device_id=(lax.rem(c + step, ctxs), h, r), device_id_type=MESH
        )
    pl.semaphore_signal(barrier, inc=1, device_id=core_dev, device_id_type=MESH)
    pl.semaphore_signal(barrier, inc=1, device_id=x_dev, device_id_type=MESH)

    @pl.when(c != h)
    def _():
        pl.semaphore_signal(barrier, inc=1, device_id=partner, device_id_type=MESH)

    kv_local.start()
    q_copy.start()
    gain_copy.start()
    router_copy.start()
    ow_copy.start()
    for e in range(min(slots, local_experts)):
        wg_copy(e, e).start()
    for e in range(local_experts):
        wd_copy(e).start()
    topk = ids_ref.shape[1]
    own_ids = jnp.concatenate([ids_ref[s] for s in range(seqs)], axis=1).astype(jnp.float32)
    ids_all[c] = jnp.concatenate(
        [own_ids, jnp.full((8 - topk, rows), -1.0, jnp.float32)], axis=0
    )
    for other in range(ctxs):

        @pl.when(other > c)
        def _():
            kv_all[other] = jnp.zeros(kv_all.shape[1:], jnp.bfloat16)

    parts[...] = jnp.zeros(parts.shape, jnp.bfloat16)
    pl.semaphore_wait(barrier, ctxs + 1 + (c != h).astype(jnp.int32))

    def kv_copy(src, dst):
        return remote(kv_hbm, kv_all.at[src], kv_send.at[dst], kv_recv.at[src], (dst, h, r))

    def ids_copy(src, dst):
        return remote(
            ids_all.at[src], ids_all.at[src], ids_send.at[dst], ids_recv.at[src], (dst, h, r)
        )

    def att_copy(src, dst, s):
        part = att_all.at[src, pl.ds(s * tokens, tokens)]
        return remote(part, part, att_send.at[dst, s], att_recv.at[src, s], (dst, h, r))

    def att_onward(block, s):
        part = att_all.at[block, pl.ds(s * tokens, tokens)]
        end = (ctxs - 1 - block, h, r)
        return remote(part, part, onward_send.at[s], att_recv.at[block, s], end)

    for dst in range(ctxs):

        @pl.when(dst > c)
        def _():
            kv_copy(c, dst).start()

    stream_copy = remote(
        stream_hbm, stream_in, stream_send.at[0], stream_recv.at[0], partner
    )
    stream_local = pltpu.make_async_copy(stream_hbm, stream_in, local_sem.at[2])

    for dst in range(ctxs):

        @pl.when(dst != c)
        def _():
            ids_copy(c, dst).start()

    kv_local.wait()
    q_copy.wait()
    for src in range(ctxs):

        @pl.when(src < c)
        def _():
            kv_copy(src, c).wait_recv()

    pairs = q_ref.shape[2] // LANES
    half = LANES // 2
    keys = ctxs * tokens
    group = pairs * tokens
    low_k = lax.broadcasted_iota(jnp.int32, (keys, LANES), 1) < half
    low_q = lax.broadcasted_iota(jnp.int32, (group, LANES), 1) < half
    key_pos = lax.broadcasted_iota(jnp.int32, (group, keys), 1)
    row_pos = lax.rem(lax.broadcasted_iota(jnp.int32, (group, keys), 0), tokens)
    visible = key_pos <= row_pos + c * tokens
    for s in range(seqs):
        kv = jnp.concatenate([kv_all[src, s] for src in range(ctxs)], axis=0).astype(jnp.float32)
        turned = pltpu.roll(kv, half, 1)
        key_sides = [jnp.where(low_k, kv, 0.0), jnp.where(low_k, 0.0, turned)]
        value_sides = [jnp.where(low_k, turned, 0.0), jnp.where(low_k, 0.0, kv)]
        q = jnp.concatenate(
            [q_ref[s, :, p * LANES : (p + 1) * LANES] for p in range(pairs)], axis=0
        )
        acc, totals = None, []
        for side in range(2):
            sink = jnp.concatenate(
                [
                    jnp.full((tokens, 1), sink_ref[2 * p + side], jnp.float32)
                    for p in range(pairs)
                ],
                axis=0,
            )
            scores = lax.dot_general(
                q, key_sides[side].astype(jnp.bfloat16), NT, preferred_element_type=jnp.float32
            ) * (half ** (-0.5))
            scores = jnp.where(visible, scores, -1e30)
            peak = jnp.maximum(sink, jnp.max(scores, axis=1, keepdims=True))
            terms = jnp.where(visible, jnp.exp(scores - peak), 0.0)
            totals.append(jnp.exp(sink - peak) + jnp.sum(terms, axis=1, keepdims=True))
            piece = lax.dot_general(
                terms.astype(jnp.bfloat16),
                value_sides[side].astype(jnp.bfloat16),
                NN,
                preferred_element_type=jnp.float32,
            )
            acc = piece if acc is None else acc + piece
        attended = (acc / jnp.where(low_q, totals[0], totals[1])).astype(jnp.bfloat16)
        for p in range(pairs):
            att_all[c, s * tokens : (s + 1) * tokens, p * LANES : (p + 1) * LANES] = attended[
                p * tokens : (p + 1) * tokens
            ]
        for dst in range(ctxs):

            @pl.when((dst != c) & (lax.abs(dst - c) < ctxs - 1))
            def _():
                att_copy(c, dst, s).start()

    @pl.when(c != h)
    def _():
        stream_copy.start()

    @pl.when(c == h)
    def _():
        stream_local.start()

    for src in range(ctxs):

        @pl.when(src != c)
        def _():
            ids_copy(src, c).wait_recv()

    ids_row = jnp.concatenate([ids_all[src] for src in range(ctxs)], axis=1)
    mine = (
        lax.broadcasted_iota(jnp.int32, (local_experts, all_rows), 0) + c * local_experts
    ).astype(jnp.float32)
    member = jnp.zeros((local_experts, all_rows), jnp.bool_)
    for k in range(topk):
        member = member | (mine == ids_row[k : k + 1])
    before = lax.broadcasted_iota(jnp.int32, (all_rows, all_rows), 0) <= lax.broadcasted_iota(
        jnp.int32, (all_rows, all_rows), 1
    )
    rank = lax.dot_general(
        jnp.where(member, 1.0, 0.0).astype(jnp.bfloat16),
        jnp.where(before, 1.0, 0.0).astype(jnp.bfloat16),
        NN,
        preferred_element_type=jnp.float32,
    )
    slot_row = jnp.where(member, rank - 1.0, -1.0)
    slot_rows = lax.broadcasted_iota(jnp.int32, (cap, all_rows), 0).astype(jnp.float32)
    for e in range(local_experts):
        pick[e * cap : (e + 1) * cap, :] = jnp.where(
            slot_rows == slot_row[e : e + 1], 1.0, 0.0
        ).astype(jnp.bfloat16)
    both = jnp.concatenate(
        [ids_row, slot_row, jnp.zeros((LANES - 8 - local_experts, all_rows), jnp.float32)], axis=0
    )
    token_ref[...] = jnp.transpose(both)
    gain_copy.wait()
    router_copy.wait()
    gain = gain_ref[...].reshape(1, width)
    for block in range(ctxs):
        here = slice(block * cols, (block + 1) * cols)
        gains[block] = jnp.concatenate(
            [jnp.broadcast_to(gain[:, here], (8, cols)), jnp.zeros((8, pad_cols - cols), jnp.float32)],
            axis=1,
        )
        routers[block] = jnp.concatenate(
            [
                router[:, here],
                jnp.zeros((router.shape[0], pad_cols - cols), jnp.bfloat16),
            ],
            axis=1,
        )

    ow_copy.wait()
    side, core = h // 2, lax.rem(h, 2)

    def widened(values):
        extra = jnp.zeros((values.shape[0], pad_cols - cols), jnp.float32)
        return jnp.concatenate([values, extra], axis=1)

    def projected(blocks, s):
        stacked = jnp.concatenate(
            [att_all[block, s * tokens : (s + 1) * tokens] for block in blocks], axis=0
        )
        return widened(
            lax.dot_general(stacked, ow[...], NT, preferred_element_type=jnp.float32)
        )

    def core_copy(s):
        return remote(core_out.at[s], core_in.at[s], core_send.at[s], core_recv.at[s], core_dev)

    def x_copy(s):
        return remote(x_out.at[s], x_in.at[s], x_send.at[s], x_recv.at[s], x_dev)

    for s in range(seqs):
        for block in (0, ctxs - 1) + tuple(range(1, ctxs - 1)):

            @pl.when(block != c)
            def _():
                att_copy(block, c, s).wait_recv()

            if block in (0, ctxs - 1):

                @pl.when(c == lax.abs(block - (ctxs - 2)))
                def _():
                    att_onward(block, s).start()

        across = (1 - side, side)
        core_out[s] = projected([2 * to + 1 - core for to in across], s).astype(jnp.bfloat16)
        core_copy(s).start()
        keep[s] = projected([2 * to + core for to in across], s)
        core_copy(s).wait_recv()
        x_out[s] = (keep[s, :tokens] + core_in[s, :tokens].astype(jnp.float32)).astype(
            jnp.bfloat16
        )
        x_copy(s).start()

    @pl.when(c != h)
    def _():
        stream_copy.wait_recv()

    @pl.when(c == h)
    def _():
        stream_local.wait()

    def h_copy(way, block, row, s, device):
        part = h_all.at[block, row, pl.ds(s * tokens, tokens)]
        return remote(part, part, h_send.at[way, block, s], h_recv.at[block, row, s], device)

    def h_core(block, row, s):
        return h_copy(jnp.where(row == h, 0, 1), block, row, s, core_dev)

    def h_x(block, s):
        return h_copy(2, block, h, s, x_dev)

    def h_right(block, s):
        return h_copy(3, block, h, s, (jnp.minimum(c + 1, ctxs - 1), h, r))

    def h_left(block, s):
        return h_copy(4, block, h, s, (jnp.maximum(c - 1, 0), h, r))

    def arrived(block, row, s):
        h_copy(0, block, row, s, core_dev).wait_recv()

    for s in range(seqs):
        kept = (
            keep[s, tokens:]
            + core_in[s, tokens:].astype(jnp.float32)
            + widened(stream_in[s].astype(jnp.float32))
        )
        x_copy(s).wait_recv()
        h_all[c, h, s * tokens : (s + 1) * tokens] = (
            kept + x_in[s].astype(jnp.float32)
        ).astype(jnp.bfloat16)
        h_x(c, s).start()

        @pl.when(c < ctxs - 1)
        def _():
            h_right(c, s).start()

        @pl.when(c > 0)
        def _():
            h_left(c, s).start()

        h_core(c, h, s).start()

    square_ref[...] = jnp.zeros(square_ref.shape, jnp.float32)
    logits_ref[...] = jnp.zeros(logits_ref.shape, jnp.float32)

    def take(block):
        for s in range(seqs):
            arrived(block, h ^ 1, s)
            arrived(block, h ^ 3, s)
        for row in range(ctxs):
            here = slice(row * rows, (row + 1) * rows)
            piece = h_all[block, row].astype(jnp.float32)
            y_ref[here, :] = (piece * gains[block][:1]).astype(jnp.bfloat16)
            square = piece * piece
            square_ref[here, :] += sum(
                square[:, i : i + LANES] for i in range(0, pad_cols, LANES)
            )
        xg[block] = lax.dot_general(
            pick[...], y_ref[...], NN, preferred_element_type=jnp.float32
        ).astype(jnp.bfloat16)
        logits_ref[...] += lax.dot_general(
            y_ref[...], routers[block], NT, preferred_element_type=jnp.float32
        )

    for d in range(1, ctxs + 1):
        for s in range(seqs):

            @pl.when(c - d >= 0)
            def _():
                arrived(c - d, h, s)

                @pl.when(c < ctxs - 1)
                def _():
                    h_right(c - d, s).start()

                h_x(c - d, s).start()
                h_core(c - d, h, s).start()

            @pl.when(c + d < ctxs)
            def _():
                arrived(c + d, h, s)

                @pl.when(c > 0)
                def _():
                    h_left(c + d, s).start()

                h_x(c + d, s).start()
                h_core(c + d, h, s).start()

            @pl.when(c - (d - 1) >= 0)
            def _():
                arrived(c - (d - 1), h ^ 2, s)
                h_core(c - (d - 1), h ^ 2, s).start()

            if d > 1:

                @pl.when(c + (d - 1) < ctxs)
                def _():
                    arrived(c + (d - 1), h ^ 2, s)
                    h_core(c + (d - 1), h ^ 2, s).start()

        @pl.when(c - (d - 1) >= 0)
        def _():
            take(c - (d - 1))

        if d > 1:

            @pl.when(c + (d - 1) < ctxs)
            def _():
                take(c + (d - 1))

    inverse = lax.rsqrt(jnp.sum(square_ref[...], axis=1, keepdims=True) / width + 1e-05)
    square_ref[...] = jnp.broadcast_to(inverse, square_ref.shape)
    inverse_row = jnp.transpose(square_ref[...])[:1]
    first = inverse_row.astype(jnp.bfloat16)
    rest = inverse_row - first.astype(jnp.float32)
    second = rest.astype(jnp.bfloat16)
    third = (rest - second.astype(jnp.float32)).astype(jnp.bfloat16)
    in_parts = jnp.concatenate(
        [part.astype(jnp.float32) for part in (first, second, third)]
        + [jnp.zeros((5, all_rows), jnp.float32)],
        axis=0,
    ).astype(jnp.bfloat16)
    for e in range(local_experts):
        found = lax.dot_general(
            in_parts, pick[e * cap : (e + 1) * cap, :], NT, preferred_element_type=jnp.float32
        )
        scale_ref[e] = jnp.broadcast_to(jnp.sum(found, axis=0, keepdims=True), (8, cap))

    def act_core(shard, e):
        return remote(
            act_all.at[shard, e],
            act_all.at[shard, e],
            act_send.at[jnp.where(shard == h, 0, 1), e],
            act_recv.at[shard, e],
            core_dev,
        )

    def act_x(e):
        return remote(
            act_all.at[h, e], act_all.at[h, e], act_send.at[2, e], act_recv.at[h, e], x_dev
        )

    def act_arrived(shard, e):
        remote(
            act_all.at[shard, e],
            act_all.at[shard, e],
            act_send.at[0, e],
            act_recv.at[shard, e],
            core_dev,
        ).wait_recv()

    lead = wide - width
    packed = act_all.shape[3]

    def activated(e, slot):
        pieces = [
            xg[block, pl.ds(pl.multiple_of(e * cap, cap), cap), :][:, :cols]
            for block in range(ctxs)
        ]
        blank = [jnp.zeros((cap, lead), jnp.bfloat16)]
        rows_in = jnp.concatenate(pieces + blank, axis=1)
        shifted = jnp.concatenate(blank + pieces, axis=1)
        factor = scale_ref[e][:1]
        gate = factor * lax.dot_general(
            wg[slot, :, :, :wide].reshape(2 * units, wide),
            rows_in,
            NT,
            preferred_element_type=jnp.float32,
        )
        up = factor * lax.dot_general(
            wg[slot, :, :, 2 * width - wide :].reshape(2 * units, wide),
            shifted,
            NT,
            preferred_element_type=jnp.float32,
        )
        return gate * jax.nn.sigmoid(1.702 * gate) * (up + 1.0)

    def hand_out(e, i, active):
        unit_rows[i] = jnp.concatenate(
            [active, jnp.zeros((2 * units, LANES - cap), jnp.float32)], axis=1
        )
        stacked = jnp.concatenate(
            [unit_rows[i, pl.ds(u, units, stride=2), :] for u in range(2)]
            + [jnp.zeros((packed - 2 * units, LANES), jnp.float32)],
            axis=0,
        )
        act_all[h, e] = jnp.transpose(stacked)[:cap].astype(jnp.bfloat16)
        act_x(e).start()
        act_core(h, e).start()

    @pl.loop(0, local_experts // 2)
    def _(pair):
        both = [(2 * pair + i, lax.rem(2 * pair + i, slots)) for i in range(2)]
        for e, slot in both:
            wg_copy(e, slot).wait()
        results = [activated(e, slot) for e, slot in both]
        for i, (e, slot) in enumerate(both):
            hand_out(e, i, results[i])

            @pl.when(e + slots < local_experts)
            def _():
                wg_copy(e + slots, slot).start()

        @pl.when(pair >= 1)
        def _():
            for e, slot in both:
                act_arrived(h ^ 2, e - 2)
                act_core(h ^ 2, e - 2).start()

    by_token = token_ref[...]
    logits = logits_ref[...] * square_ref[:, :1]
    experts = logits.shape[1]
    expert_lane = lax.broadcasted_iota(jnp.int32, (all_rows, experts), 1).astype(jnp.float32)
    named = jnp.zeros((all_rows, experts), jnp.bool_)
    for k in range(topk):
        named = named | (expert_lane == by_token[:, k : k + 1])
    top = jnp.max(jnp.where(named, logits, -1e30), axis=1, keepdims=True)
    weight = jnp.where(named, jnp.exp(logits - top), 0.0)
    mix = weight / jnp.sum(weight, axis=1, keepdims=True)
    mix = jnp.concatenate([mix, jnp.zeros((all_rows, LANES - experts), jnp.float32)], axis=1)
    mix = pltpu.roll(mix, lax.rem(LANES - c * local_experts, LANES), 1)
    slot_lane = lax.broadcasted_iota(jnp.int32, (all_rows, LANES), 1).astype(jnp.float32)
    for e in range(local_experts):
        spread[:, e * LANES : (e + 1) * LANES] = jnp.where(
            slot_lane == by_token[:, 8 + e : 9 + e], mix[:, e : e + 1], 0.0
        ).astype(jnp.bfloat16)

    for e in range(local_experts - 2, local_experts):
        act_arrived(h ^ 2, e)
        act_core(h ^ 2, e).start()

    def rs_copy(src, dst, j):
        return remote(
            rs_out.at[dst, j], rs_in.at[src, j], rs_send.at[dst, j], rs_recv.at[src, j], (dst, h, r)
        )

    def combined(block, j):
        return lax.dot_general(
            spread[pl.ds(pl.multiple_of(block * rows, rows), rows), :],
            parts[j],
            NN,
            preferred_element_type=jnp.float32,
        )

    outer = (c == 0) | (c == ctxs - 1)
    far = ctxs - 1 - c
    relay_dst = jnp.where(c == 0, 1, 2)
    end_dst = jnp.where(c == 1, 3, 0)

    def relay_copy(j):
        return remote(
            rs_out.at[far, j],
            relay_in.at[j],
            rs_send.at[far, j],
            relay_recv.at[j],
            (relay_dst, h, r),
        )

    chunk = parts.shape[2]
    chunks = parts.shape[0]
    for j in range(chunks):
        first_col = j * chunk
        last_col = min(cols, first_col + chunk)

        @pl.loop(0, local_experts)
        def _(e):
            if j == 0:
                wd_copy(e).wait()
                act_arrived(h ^ 1, e)
                act_arrived(h ^ 3, e)
                for u in range(2):
                    hidden_ref[2 * e + u] = jnp.concatenate(
                        [act_all[shard, e][:, u * units : (u + 1) * units] for shard in range(4)],
                        axis=1,
                    )
            total = None
            for u in range(2):
                piece = lax.dot_general(
                    hidden_ref[2 * e + u],
                    wd[2 * e + u, :, first_col:last_col],
                    NN,
                    preferred_element_type=jnp.float32,
                )
                total = piece if total is None else total + piece
            if last_col - first_col < chunk:
                extra = jnp.zeros((cap, chunk - (last_col - first_col)), jnp.float32)
                total = jnp.concatenate([total, extra], axis=1)
            parts[j, pl.ds(pl.multiple_of(e * LANES, LANES), cap), :] = total.astype(jnp.bfloat16)

        @pl.when(outer)
        def _():
            rs_out[far, j] = combined(far, j).astype(jnp.bfloat16)
            relay_copy(j).start()
            for dst in (ctxs - 1 - relay_dst, relay_dst):
                rs_out[dst, j] = combined(dst, j).astype(jnp.bfloat16)
                rs_copy(c, dst, j).start()

        @pl.when(jnp.logical_not(outer))
        def _():
            for dst in (ctxs - 1 - c, ctxs - 1 - end_dst):
                rs_out[dst, j] = combined(dst, j).astype(jnp.bfloat16)
                rs_copy(c, dst, j).start()

    @pl.when(jnp.logical_not(outer))
    def _():
        for j in range(chunks):
            ends = combined(end_dst, j)
            relay_copy(j).wait_recv()
            rs_out[end_dst, j] = (ends + relay_in[j].astype(jnp.float32)).astype(jnp.bfloat16)
            rs_copy(c, end_dst, j).start()

    own = h_all[h, c].astype(jnp.float32)
    for j in range(chunks):
        here = slice(j * chunk, (j + 1) * chunk)
        total_ref[:, here] = combined(c, j) + own[:, here]
    for j in range(chunks):
        here = slice(j * chunk, (j + 1) * chunk)
        for src in (1, 2, 0, 3):
            sends_here = (src != c) & jnp.logical_not(outer & (src == far))

            @pl.when(sends_here)
            def _():
                rs_copy(src, c, j).wait_recv()
                total_ref[:, here] += rs_in[src, j].astype(jnp.float32)

    total = total_ref[...]
    out_ref[...] = total[:, :cols].astype(jnp.bfloat16).reshape(out_ref.shape)

    for dst in range(ctxs):

        @pl.when(dst > c)
        def _():
            kv_copy(c, dst).wait_send()

        @pl.when(dst != c)
        def _():
            ids_copy(c, dst).wait_send()
            for j in range(chunks):
                rs_copy(c, dst, j).wait_send()

        @pl.when((dst != c) & (lax.abs(dst - c) < ctxs - 1))
        def _():
            for s in range(seqs):
                att_copy(c, dst, s).wait_send()

    @pl.when((c == 1) | (c == ctxs - 2))
    def _():
        for s in range(seqs):
            att_onward(jnp.where(c == 1, ctxs - 1, 0), s).wait_send()

    @pl.when(c != h)
    def _():
        stream_copy.wait_send()

    for s in range(seqs):
        x_copy(s).wait_send()
        core_copy(s).wait_send()
        for block in range(ctxs):
            h_x(block, s).wait_send()
            h_core(block, h, s).wait_send()
            h_core(block, h ^ 2, s).wait_send()

            @pl.when((c < ctxs - 1) & (block <= c))
            def _():
                h_right(block, s).wait_send()

            @pl.when((c > 0) & (block >= c))
            def _():
                h_left(block, s).wait_send()

    for e in range(local_experts):
        act_x(e).wait_send()
        act_core(h, e).wait_send()
        act_core(h ^ 2, e).wait_send()


def layer_call(queries, keyvals, sinks, stream, out_weight, gain, router, ids, w_gate_up, w_down):
    seqs, tokens, q_cols = queries.shape
    cols = stream.shape[2]
    ctxs = lax.axis_size("ctx")
    rows = seqs * tokens
    width = gain.shape[0]
    halves, units, wide_w = w_gate_up.shape
    local_experts = halves // 2
    all_rows = ctxs * rows
    cap = all_rows * 3 // 16
    pad_cols = pl.cdiv(cols, 2 * LANES) * 2 * LANES
    packed = pl.cdiv(2 * units, LANES) * LANES
    slots = min(4, local_experts)
    chunk = 2 * LANES
    chunks = pl.cdiv(cols, chunk)
    sizes = (seqs, tokens, rows, ctxs, width, cols, cap, local_experts, units, slots)
    bf16, f32 = jnp.bfloat16, jnp.float32
    dma = pltpu.SemaphoreType.DMA
    vmem = pl.BlockSpec(memory_space=pltpu.VMEM)
    hbm = pl.BlockSpec(memory_space=pl.ANY)
    return pl.pallas_call(
        functools.partial(layer_kernel, sizes),
        out_shape=jax.ShapeDtypeStruct((seqs, tokens, cols), bf16),
        in_specs=[hbm, hbm, vmem, pl.BlockSpec(memory_space=pltpu.SMEM)] + [hbm] * 6,
        out_specs=vmem,
        scratch_shapes=[
            pltpu.VMEM(queries.shape, bf16),
            pltpu.VMEM(gain.shape, f32),
            pltpu.VMEM((ctxs, 8, pad_cols), f32),
            pltpu.VMEM((ctxs, seqs, tokens, keyvals.shape[3]), bf16),
            pltpu.VMEM((ctxs, 8, LANES), f32),
            pltpu.VMEM((seqs, tokens, cols), bf16),
            pltpu.VMEM(out_weight.shape[::-1], bf16),
            pltpu.VMEM(router.shape[::-1], bf16),
            pltpu.VMEM((ctxs, router.shape[1], pad_cols), bf16),
            pltpu.VMEM((slots, units, 2, wide_w), bf16),
            pltpu.VMEM(w_down.shape, bf16),
            pltpu.VMEM((ctxs, rows, q_cols), bf16),
            pltpu.VMEM((seqs, 2 * tokens, pad_cols), bf16),
            pltpu.VMEM((seqs, 2 * tokens, pad_cols), bf16),
            pltpu.VMEM((seqs, 2 * tokens, pad_cols), f32),
            pltpu.VMEM((seqs, tokens, pad_cols), bf16),
            pltpu.VMEM((seqs, tokens, pad_cols), bf16),
            pltpu.VMEM((ctxs, 4, rows, pad_cols), bf16),
            pltpu.VMEM((all_rows, pad_cols), bf16),
            pltpu.VMEM((all_rows, LANES), f32),
            pltpu.VMEM((all_rows, router.shape[1]), f32),
            pltpu.VMEM((all_rows, LANES), f32),
            pltpu.VMEM((local_experts * cap, all_rows), bf16),
            pltpu.VMEM((all_rows, local_experts * LANES), bf16),
            pltpu.VMEM((ctxs, local_experts * cap, pad_cols), bf16),
            pltpu.VMEM((local_experts, 8, cap), f32),
            pltpu.VMEM((2, 2 * units, LANES), f32),
            pltpu.VMEM((4, local_experts, cap, packed), bf16),
            pltpu.VMEM((chunks, local_experts * LANES, chunk), bf16),
            pltpu.VMEM((ctxs, chunks, rows, chunk), bf16),
            pltpu.VMEM((ctxs, chunks, rows, chunk), bf16),
            pltpu.VMEM((chunks, rows, chunk), bf16),
            pltpu.VMEM((halves, cap, w_down.shape[1]), bf16),
            pltpu.VMEM((rows, chunks * chunk), f32),
            dma((6,)),
            dma((slots,)),
            dma((local_experts,)),
            dma((ctxs,)),
            dma((ctxs,)),
            dma((ctxs,)),
            dma((ctxs,)),
            dma((1,)),
            dma((1,)),
            dma((ctxs, seqs)),
            dma((ctxs, seqs)),
            dma((seqs,)),
            dma((seqs,)),
            dma((seqs,)),
            dma((seqs,)),
            dma((5, ctxs, seqs)),
            dma((ctxs, 4, seqs)),
            dma((3, local_experts)),
            dma((4, local_experts)),
            dma((ctxs, chunks)),
            dma((ctxs, chunks)),
            dma((chunks,)),
            dma((seqs,)),
        ],
        compiler_params=pltpu.CompilerParams(
            vmem_limit_bytes=67043328, collective_id=0, has_side_effects=True
        ),
    )(
        queries,
        keyvals.reshape(seqs, tokens, keyvals.shape[3]),
        jnp.transpose(ids, (0, 2, 1)),
        sinks,
        gain,
        stream,
        out_weight.T,
        router.T,
        jnp.transpose(w_gate_up, (1, 0, 2)),
        w_down,
    )


def one_chip_row(queries, keyvals, stream, out_weight, router, ids, w_gate_up):
    ctxs, heads = lax.axis_size("ctx"), lax.axis_size("head")
    rows = queries.shape[0] * queries.shape[1]
    return (
        ctxs == heads == 4
        and rows == LANES
        and keyvals.shape[2] == 1
        and keyvals.shape[3] == LANES
        and out_weight.shape[1] == stream.shape[2]
        and w_gate_up.shape[0] == 16
        and ids.shape[2] <= 8
        and router.shape[1] <= LANES
    )


def on_device(
    queries, keyvals, sinks, stream, out_weight, norm_gain, router, expert_ids, w_gate_up, w_down
):
    if one_chip_row(queries, keyvals, stream, out_weight, router, expert_ids, w_gate_up):
        return layer_call(
            queries,
            keyvals,
            sinks,
            stream,
            out_weight,
            norm_gain,
            router,
            expert_ids,
            w_gate_up,
            w_down,
        )
    ctx_count = lax.axis_size("ctx")
    local_seqs = queries.shape[0]
    tokens = queries.shape[1]
    row_count = local_seqs * tokens
    kv_local = keyvals.shape[2]
    head_dim = keyvals.shape[3] // 2
    q_local = queries.shape[2] // head_dim
    query_group_size = q_local // kv_local
    wide_rows = query_group_size * tokens
    col_width = stream.shape[2]
    first_pos = lax.axis_index("ctx") * tokens
    last_pos = first_pos + tokens - 1
    score_scale = head_dim ** (-0.5)
    scaled_queries = queries * jnp.asarray(score_scale, jnp.bfloat16)
    query_grid = scaled_queries.reshape(local_seqs, tokens, kv_local, query_group_size, head_dim)
    query_wide = jnp.transpose(query_grid, (0, 2, 3, 1, 4)).reshape(
        local_seqs, kv_local, wide_rows, head_dim
    )
    positions = first_pos + jnp.tile(jnp.arange(tokens), query_group_size)
    sink_rows = jnp.repeat(sinks.reshape(kv_local, query_group_size), tokens, axis=1)
    sink_grid = jnp.broadcast_to(sink_rows[None], (local_seqs, kv_local, wide_rows))
    start_state = (
        sink_grid,
        jnp.ones_like(sink_grid),
        jnp.zeros((local_seqs, kv_local, head_dim, wide_rows), jnp.float32),
    )

    def attend_block(running, shard_piece):
        peak_old, denom_old, accum_old = running
        key_block = shard_piece[..., :head_dim]
        value_block = shard_piece[..., head_dim:]
        scores = jnp.einsum(
            "skmd,snkd->sknm", query_wide, key_block, preferred_element_type=jnp.float32
        )
        key_pos = jnp.arange(shard_piece.shape[1])
        visible = key_pos[:, None] <= positions[None, :]
        masked = jnp.where(visible[None, None], scores, -jnp.inf)
        peak_new = jnp.maximum(peak_old, jnp.max(masked, axis=2))
        exp_terms = jnp.exp(masked - peak_new[:, :, None, :])
        factor = jnp.exp(peak_old - peak_new)
        denom_new = denom_old * factor + jnp.sum(exp_terms, axis=2)
        accum_new = accum_old * factor[:, :, None, :] + jnp.einsum(
            "sknm,snkd->skdm",
            exp_terms.astype(jnp.bfloat16),
            value_block,
            preferred_element_type=jnp.float32,
        )
        return (peak_new, denom_new, accum_new)

    shard_piece = lax.all_gather(keyvals, "ctx", axis=1, tiled=True)

    def keep_state(state_in):
        return state_in

    def update_state(state_in):
        return attend_block(state_in, shard_piece)

    peak_fin, denom_fin, accum_fin = lax.cond(
        jnp.int32(0) > last_pos, keep_state, update_state, start_state
    )
    normalized = (accum_fin / denom_fin[:, :, None, :]).reshape(
        local_seqs, kv_local, head_dim, query_group_size, tokens
    )
    attended = (
        jnp.transpose(normalized, (0, 4, 1, 3, 2))
        .reshape(row_count, q_local * head_dim)
        .astype(jnp.bfloat16)
    )
    token_ids = lax.all_gather(
        expert_ids.reshape(row_count, expert_ids.shape[2]).T, "ctx", axis=1, tiled=True
    )
    all_rows = ctx_count * row_count
    halves = w_gate_up.shape[0]
    units = w_gate_up.shape[1]
    token_block = min(all_rows, 8 * tokens)
    cap = token_block // tokens * (3 * tokens // 16)
    row_expert = (lax.axis_index("ctx") * halves + jnp.arange(halves)) // 2
    named = jnp.any(token_ids[:, None, :] == row_expert[None, :, None], axis=0)
    counted = named.astype(jnp.int32).reshape(halves, all_rows // token_block, token_block)
    rank = jnp.cumsum(counted, axis=2) - 1
    slots = jnp.where(named, rank.reshape(halves, all_rows), -1).reshape(halves, 1, all_rows)
    width = norm_gain.shape[0]
    head_count = lax.axis_size("head")
    swapped = ctx_count == head_count and out_weight.shape[1] == col_width
    if swapped:
        pairs = [
            (first * head_count + second, second * head_count + first)
            for first in range(ctx_count)
            for second in range(head_count)
        ]
        turned = lax.ppermute(
            stream.reshape(row_count, col_width), ("ctx", "head"), perm=pairs
        )
        every_row = lax.all_gather(attended, "ctx", axis=0, tiled=True)
        partial_proj = jnp.dot(every_row, out_weight, preferred_element_type=jnp.float32)
        summed = lax.psum_scatter(
            partial_proj.astype(jnp.bfloat16), "head", scatter_dimension=0, tiled=True
        )
        turned_state = summed.astype(jnp.float32) + turned.astype(jnp.float32)
        every_state = lax.all_gather(
            turned_state.astype(jnp.bfloat16), ("head", "ctx"), axis=0, tiled=False
        )
    else:
        partial_proj = jnp.dot(attended, lax.all_gather(out_weight, "ctx", axis=1, tiled=True), preferred_element_type=jnp.float32)
        own_stream = stream.reshape(row_count, col_width).astype(jnp.float32)
        summed = lax.psum_scatter(
            partial_proj.astype(jnp.bfloat16), "head", scatter_dimension=1, tiled=True
        )
        own_state = (summed.astype(jnp.float32) + own_stream).astype(jnp.bfloat16)
        every_state = lax.all_gather(own_state, ("ctx", "head"), axis=0, tiled=False)
    every_state = every_state.reshape(ctx_count, width // col_width, row_count, col_width)
    expert_count = router.shape[1]
    unit_rows = jnp.transpose(w_gate_up, (1, 0, 2)).reshape(units * halves, w_gate_up.shape[2])
    router_rows = jnp.pad(router.T, ((0, 0), (0, -width % LANES)))
    gain = norm_gain.reshape(width // col_width, 1, col_width)
    active, logits = gate_up_call(
        every_state, gain, router_rows, unit_rows, slots, units, token_block, cap
    )
    member = jnp.any(token_ids[:, None, :] == jnp.arange(expert_count)[None, :, None], axis=0)
    masked = jnp.where(member, logits, -jnp.inf)
    mix_all = jax.nn.softmax(masked, axis=0)
    chosen_rows = (row_expert[:, None] == jnp.arange(expert_count)[None, :]).astype(jnp.float32)
    mix_rows = jnp.dot(chosen_rows, mix_all, precision=lax.Precision.HIGHEST)
    mix_rows = mix_rows.reshape(halves, 1, all_rows)
    every_active = lax.all_gather(active.reshape(-1, units), "head", axis=0, tiled=True)
    every_active = every_active.reshape(width // col_width, *active.shape)
    partial_out = down_call(every_active, w_down, slots, mix_rows, token_block)
    combined = lax.psum_scatter(partial_out, "ctx", scatter_dimension=0, tiled=True)
    if swapped:
        own_state = every_state[lax.axis_index("ctx"), lax.axis_index("head")]
    layer_out = (own_state.astype(jnp.float32) + combined.astype(jnp.float32)).astype(jnp.bfloat16)
    return layer_out.reshape(local_seqs, tokens, col_width)


def solution(mesh):
    placed = (
        P("rep", "ctx", "head"),
        P("rep", "ctx", "head", None),
        P("head"),
        P("rep", "ctx", "head"),
        P("head", "ctx"),
        P(),
        P(),
        P("rep", "ctx", None),
        P("ctx", "head", None),
        P("ctx", None, "head"),
    )
    return jax.shard_map(
        on_device, mesh=mesh, in_specs=placed, out_specs=P("rep", "ctx", "head"), check_vma=False
    )
```

```python
import functools

import jax
import jax.numpy as jnp
from jax import lax
from jax.experimental import pallas as pl
from jax.experimental.pallas import tpu as pltpu
from jax.sharding import PartitionSpec as P


NT = (((1,), (1,)), ((), ()))
TN = (((0,), (0,)), ((), ()))
LANES = 128


def one_hot_rows(slots, cap, value):
    rows = lax.broadcasted_iota(jnp.int32, (cap, slots.shape[1]), 0)
    return jnp.where(rows == slots, value, 0.0).astype(jnp.bfloat16)


def gate_up_kernel(
    halves,
    units,
    state_ref,
    gain_ref,
    router_ref,
    w_ref,
    slot_ref,
    out_ref,
    logits_ref,
    act_ref,
    xg_ref,
    xu_ref,
):
    step = pl.program_id(1)
    groups, shards, group_rows, cols = state_ref.shape

    @pl.when(step == 0)
    def _():
        for group in range(groups):
            pieces = [state_ref[group, shard].astype(jnp.float32) for shard in range(shards)]
            square = sum(jnp.sum(piece * piece, axis=1, keepdims=True) for piece in pieces)
            inverse = lax.rsqrt(square / (shards * cols) + 1e-05)
            scaled = [
                (piece * inverse * gain_ref[shard]).astype(jnp.bfloat16)
                for shard, piece in enumerate(pieces)
            ]
            extra = xg_ref.shape[1] - shards * cols
            blank = [jnp.zeros((group_rows, extra), jnp.bfloat16)] if extra else []
            here = slice(group * group_rows, (group + 1) * group_rows)
            xg_ref[here, :] = jnp.concatenate(scaled + blank, axis=1)
            xu_ref[here, :] = jnp.concatenate(blank + scaled, axis=1)
        logits_ref[...] = lax.dot_general(
            router_ref[...], xg_ref[...], NT, preferred_element_type=jnp.float32
        )

    rows, wide = w_ref.shape[0], xg_ref.shape[1]
    gate = lax.dot_general(w_ref[:, :wide], xg_ref[...], NT, preferred_element_type=jnp.float32)
    up = lax.dot_general(
        w_ref[:, w_ref.shape[1] - wide :], xu_ref[...], NT, preferred_element_type=jnp.float32
    )
    active = gate * jax.nn.sigmoid(1.702 * gate) * (up + 1.0)
    slabs = act_ref.shape[0]
    for slab in range(slabs):
        act_ref[slab, pl.ds(step * rows, rows), :] = active[:, slab * LANES : (slab + 1) * LANES]

    @pl.when(step == pl.num_programs(1) - 1)
    def _():
        for row in range(halves):
            wanted = pl.ds(row, units, stride=halves) if halves > 1 else pl.ds(0, units)
            picked = jnp.concatenate([act_ref[slab, wanted, :] for slab in range(slabs)], axis=1)
            spread = one_hot_rows(slot_ref[row], out_ref.shape[2], 1.0)
            out_ref[row, 0] = lax.dot_general(
                spread, picked.astype(jnp.bfloat16), NT, preferred_element_type=jnp.float32
            ).astype(jnp.bfloat16)


def gate_up_call(state, gain, router, weights, slots, units, token_block, cap):
    halves = slots.shape[0]
    sources, shards, group_rows, cols = state.shape
    groups = token_block // group_rows
    blocks = sources // groups
    experts, wide = router.shape
    wide_w = weights.shape[1]
    sizes = [
        size
        for size in range(1, units + 1)
        if units % size == 0
        and (size == units or (size * halves) % 16 == 0)
        and size * halves * wide_w * 2 <= 4 << 20
    ]
    size = sizes[-1]
    return pl.pallas_call(
        functools.partial(gate_up_kernel, halves, units),
        grid=(blocks, units // size),
        out_shape=(
            jax.ShapeDtypeStruct((halves, blocks, cap, units), jnp.bfloat16),
            jax.ShapeDtypeStruct((experts, blocks * token_block), jnp.float32),
        ),
        in_specs=[
            pl.BlockSpec((groups, shards, group_rows, cols), lambda i, j: (i, 0, 0, 0)),
            pl.BlockSpec((shards, 1, cols), lambda i, j: (0, 0, 0)),
            pl.BlockSpec((experts, wide), lambda i, j: (0, 0)),
            pl.BlockSpec((size * halves, wide_w), lambda i, j: (j, 0)),
            pl.BlockSpec((halves, 1, token_block), lambda i, j: (0, 0, i)),
        ],
        out_specs=(
            pl.BlockSpec((halves, 1, cap, units), lambda i, j: (0, i, 0, 0)),
            pl.BlockSpec((experts, token_block), lambda i, j: (0, i)),
        ),
        scratch_shapes=[
            pltpu.VMEM((token_block // LANES, units * halves, LANES), jnp.float32),
            pltpu.VMEM((token_block, wide), jnp.bfloat16),
            pltpu.VMEM((token_block, wide), jnp.bfloat16),
        ],
        compiler_params=pltpu.CompilerParams(vmem_limit_bytes=56 << 20),
    )(state, gain, router, weights, slots)


def down_kernel(act_ref, w_ref, slot_ref, mix_ref, out_ref, total_ref):
    step = pl.program_id(1)
    part = None
    for row in range(w_ref.shape[0]):
        pieces = [act_ref[shard, row, 0] for shard in range(act_ref.shape[0])]
        hidden = jnp.concatenate(pieces, axis=1)
        piece = jnp.dot(hidden, w_ref[row], preferred_element_type=jnp.float32)
        part = piece if part is None else part + piece
    spread = one_hot_rows(slot_ref[0], act_ref.shape[3], mix_ref[0])
    added = lax.dot_general(
        spread, part.astype(jnp.bfloat16), TN, preferred_element_type=jnp.float32
    )

    @pl.when(step == 0)
    def _():
        total_ref[...] = added

    @pl.when(step != 0)
    def _():
        total_ref[...] += added

    @pl.when(step == pl.num_programs(1) - 1)
    def _():
        out_ref[...] = total_ref[...].astype(jnp.bfloat16)


def down_call(act, weights, slots, mix, token_block):
    shards, halves, blocks, cap, units = act.shape
    hidden, cols = weights.shape[1:]
    pair = 2 if halves % 2 == 0 else 1
    return pl.pallas_call(
        down_kernel,
        grid=(blocks, halves // pair),
        out_shape=jax.ShapeDtypeStruct((blocks * token_block, cols), jnp.bfloat16),
        in_specs=[
            pl.BlockSpec((shards, pair, 1, cap, units), lambda i, r: (0, r, i, 0, 0)),
            pl.BlockSpec((pair, hidden, cols), lambda i, r: (r, 0, 0)),
            pl.BlockSpec((1, 1, token_block), lambda i, r: (r * pair, 0, i)),
            pl.BlockSpec((1, 1, token_block), lambda i, r: (r * pair, 0, i)),
        ],
        out_specs=pl.BlockSpec((token_block, cols), lambda i, r: (i, 0)),
        scratch_shapes=[pltpu.VMEM((token_block, cols), jnp.float32)],
        compiler_params=pltpu.CompilerParams(vmem_limit_bytes=48 << 20),
    )(act, weights, slots, mix)


MESH = pl.DeviceIdType.MESH
NN = (((1,), (0,)), ((), ()))


def layer_kernel(
    sizes,
    q_hbm,
    kv_hbm,
    ids_ref,
    sink_ref,
    gain_hbm,
    stream_hbm,
    ow_hbm,
    router_hbm,
    wg_hbm,
    wd_hbm,
    out_ref,
    q_ref,
    gain_ref,
    gains,
    kv_all,
    ids_all,
    stream_in,
    ow,
    router,
    routers,
    wg,
    wd,
    att_all,
    core_out,
    core_in,
    keep,
    x_out,
    x_in,
    h_all,
    y_ref,
    square_ref,
    logits_ref,
    token_ref,
    pick,
    spread,
    xg,
    scale_ref,
    unit_rows,
    act_all,
    parts,
    rs_out,
    rs_in,
    relay_in,
    hidden_ref,
    total_ref,
    local_sem,
    wg_sem,
    wd_sem,
    kv_send,
    kv_recv,
    ids_send,
    ids_recv,
    stream_send,
    stream_recv,
    att_send,
    att_recv,
    core_send,
    core_recv,
    x_send,
    x_recv,
    h_send,
    h_recv,
    act_send,
    act_recv,
    rs_send,
    rs_recv,
    relay_recv,
    onward_send,
):
    seqs, tokens, rows, ctxs, width, cols, cap, local_experts, units, slots = sizes
    c, h, r = lax.axis_index("ctx"), lax.axis_index("head"), lax.axis_index("rep")
    all_rows = ctxs * rows
    wide = pl.cdiv(width, LANES) * LANES
    pad_cols = h_all.shape[3]
    core_dev, x_dev = (c, h ^ 1, r), (c, h ^ 2, r)
    partner = (h, c, r)

    def remote(src, dst, send, recv, device):
        return pltpu.make_async_remote_copy(
            src_ref=src,
            dst_ref=dst,
            send_sem=send,
            recv_sem=recv,
            device_id=device,
            device_id_type=MESH,
        )

    ow_copy = pltpu.make_async_copy(ow_hbm, ow, local_sem.at[0])
    router_copy = pltpu.make_async_copy(router_hbm, router, local_sem.at[1])
    q_copy = pltpu.make_async_copy(q_hbm, q_ref, local_sem.at[3])
    kv_local = pltpu.make_async_copy(kv_hbm, kv_all.at[c], local_sem.at[4])
    gain_copy = pltpu.make_async_copy(gain_hbm, gain_ref, local_sem.at[5])

    def wg_copy(e, slot):
        return pltpu.make_async_copy(
            wg_hbm.at[:, pl.ds(2 * e, 2), :], wg.at[slot], wg_sem.at[slot]
        )

    def wd_copy(e):
        return pltpu.make_async_copy(
            wd_hbm.at[pl.ds(2 * e, 2)], wd.at[pl.ds(2 * e, 2)], wd_sem.at[e]
        )

    barrier = pltpu.get_barrier_semaphore()
    for step in range(1, ctxs):
        pl.semaphore_signal(
            barrier, inc=1, device_id=(lax.rem(c + step, ctxs), h, r), device_id_type=MESH
        )
    pl.semaphore_signal(barrier, inc=1, device_id=core_dev, device_id_type=MESH)
    pl.semaphore_signal(barrier, inc=1, device_id=x_dev, device_id_type=MESH)

    @pl.when(c != h)
    def _():
        pl.semaphore_signal(barrier, inc=1, device_id=partner, device_id_type=MESH)

    kv_local.start()
    q_copy.start()
    gain_copy.start()
    router_copy.start()
    ow_copy.start()
    for e in range(min(slots, local_experts)):
        wg_copy(e, e).start()
    for e in range(local_experts):
        wd_copy(e).start()
    topk = ids_ref.shape[1]
    own_ids = jnp.concatenate([ids_ref[s] for s in range(seqs)], axis=1).astype(jnp.float32)
    ids_all[c] = jnp.concatenate(
        [own_ids, jnp.full((8 - topk, rows), -1.0, jnp.float32)], axis=0
    )
    for other in range(ctxs):

        @pl.when(other > c)
        def _():
            kv_all[other] = jnp.zeros(kv_all.shape[1:], jnp.bfloat16)

    parts[...] = jnp.zeros(parts.shape, jnp.bfloat16)
    pl.semaphore_wait(barrier, ctxs + 1 + (c != h).astype(jnp.int32))

    def kv_copy(src, dst):
        return remote(kv_hbm, kv_all.at[src], kv_send.at[dst], kv_recv.at[src], (dst, h, r))

    def ids_copy(src, dst):
        return remote(
            ids_all.at[src], ids_all.at[src], ids_send.at[dst], ids_recv.at[src], (dst, h, r)
        )

    def att_copy(src, dst, s):
        part = att_all.at[src, pl.ds(s * tokens, tokens)]
        return remote(part, part, att_send.at[dst, s], att_recv.at[src, s], (dst, h, r))

    def att_onward(block, s):
        part = att_all.at[block, pl.ds(s * tokens, tokens)]
        end = (ctxs - 1 - block, h, r)
        return remote(part, part, onward_send.at[s], att_recv.at[block, s], end)

    for dst in range(ctxs):

        @pl.when(dst > c)
        def _():
            kv_copy(c, dst).start()

    stream_copy = remote(
        stream_hbm, stream_in, stream_send.at[0], stream_recv.at[0], partner
    )
    stream_local = pltpu.make_async_copy(stream_hbm, stream_in, local_sem.at[2])

    @pl.when(c != h)
    def _():
        stream_copy.start()

    @pl.when(c == h)
    def _():
        stream_local.start()

    for dst in range(ctxs):

        @pl.when(dst != c)
        def _():
            ids_copy(c, dst).start()

    kv_local.wait()
    q_copy.wait()
    for src in range(ctxs):

        @pl.when(src < c)
        def _():
            kv_copy(src, c).wait_recv()

    pairs = q_ref.shape[2] // LANES
    half = LANES // 2
    keys = ctxs * tokens
    group = pairs * tokens
    low_k = lax.broadcasted_iota(jnp.int32, (keys, LANES), 1) < half
    low_q = lax.broadcasted_iota(jnp.int32, (group, LANES), 1) < half
    key_pos = lax.broadcasted_iota(jnp.int32, (group, keys), 1)
    row_pos = lax.rem(lax.broadcasted_iota(jnp.int32, (group, keys), 0), tokens)
    visible = key_pos <= row_pos + c * tokens
    for s in range(seqs):
        kv = jnp.concatenate([kv_all[src, s] for src in range(ctxs)], axis=0).astype(jnp.float32)
        turned = pltpu.roll(kv, half, 1)
        key_sides = [jnp.where(low_k, kv, 0.0), jnp.where(low_k, 0.0, turned)]
        value_sides = [jnp.where(low_k, turned, 0.0), jnp.where(low_k, 0.0, kv)]
        q = jnp.concatenate(
            [q_ref[s, :, p * LANES : (p + 1) * LANES] for p in range(pairs)], axis=0
        )
        acc, totals = None, []
        for side in range(2):
            sink = jnp.concatenate(
                [
                    jnp.full((tokens, 1), sink_ref[2 * p + side], jnp.float32)
                    for p in range(pairs)
                ],
                axis=0,
            )
            scores = lax.dot_general(
                q, key_sides[side].astype(jnp.bfloat16), NT, preferred_element_type=jnp.float32
            ) * (half ** (-0.5))
            scores = jnp.where(visible, scores, -1e30)
            peak = jnp.maximum(sink, jnp.max(scores, axis=1, keepdims=True))
            terms = jnp.where(visible, jnp.exp(scores - peak), 0.0)
            totals.append(jnp.exp(sink - peak) + jnp.sum(terms, axis=1, keepdims=True))
            piece = lax.dot_general(
                terms.astype(jnp.bfloat16),
                value_sides[side].astype(jnp.bfloat16),
                NN,
                preferred_element_type=jnp.float32,
            )
            acc = piece if acc is None else acc + piece
        attended = (acc / jnp.where(low_q, totals[0], totals[1])).astype(jnp.bfloat16)
        for p in range(pairs):
            att_all[c, s * tokens : (s + 1) * tokens, p * LANES : (p + 1) * LANES] = attended[
                p * tokens : (p + 1) * tokens
            ]
        for dst in range(ctxs):

            @pl.when((dst != c) & (lax.abs(dst - c) < ctxs - 1))
            def _():
                att_copy(c, dst, s).start()

    for src in range(ctxs):

        @pl.when(src != c)
        def _():
            ids_copy(src, c).wait_recv()

    ids_row = jnp.concatenate([ids_all[src] for src in range(ctxs)], axis=1)
    mine = (
        lax.broadcasted_iota(jnp.int32, (local_experts, all_rows), 0) + c * local_experts
    ).astype(jnp.float32)
    member = jnp.zeros((local_experts, all_rows), jnp.bool_)
    for k in range(topk):
        member = member | (mine == ids_row[k : k + 1])
    before = lax.broadcasted_iota(jnp.int32, (all_rows, all_rows), 0) <= lax.broadcasted_iota(
        jnp.int32, (all_rows, all_rows), 1
    )
    rank = lax.dot_general(
        jnp.where(member, 1.0, 0.0).astype(jnp.bfloat16),
        jnp.where(before, 1.0, 0.0).astype(jnp.bfloat16),
        NN,
        preferred_element_type=jnp.float32,
    )
    slot_row = jnp.where(member, rank - 1.0, -1.0)
    slot_rows = lax.broadcasted_iota(jnp.int32, (cap, all_rows), 0).astype(jnp.float32)
    for e in range(local_experts):
        pick[e * cap : (e + 1) * cap, :] = jnp.where(
            slot_rows == slot_row[e : e + 1], 1.0, 0.0
        ).astype(jnp.bfloat16)
    both = jnp.concatenate(
        [ids_row, slot_row, jnp.zeros((LANES - 8 - local_experts, all_rows), jnp.float32)], axis=0
    )
    token_ref[...] = jnp.transpose(both)
    gain_copy.wait()
    router_copy.wait()
    gain = gain_ref[...].reshape(1, width)
    for block in range(ctxs):
        here = slice(block * cols, (block + 1) * cols)
        gains[block] = jnp.concatenate(
            [jnp.broadcast_to(gain[:, here], (8, cols)), jnp.zeros((8, pad_cols - cols), jnp.float32)],
            axis=1,
        )
        routers[block] = jnp.concatenate(
            [
                router[:, here],
                jnp.zeros((router.shape[0], pad_cols - cols), jnp.bfloat16),
            ],
            axis=1,
        )

    ow_copy.wait()
    side, core = h // 2, lax.rem(h, 2)

    def widened(values):
        extra = jnp.zeros((values.shape[0], pad_cols - cols), jnp.float32)
        return jnp.concatenate([values, extra], axis=1)

    def projected(blocks, s):
        stacked = jnp.concatenate(
            [att_all[block, s * tokens : (s + 1) * tokens] for block in blocks], axis=0
        )
        return widened(
            lax.dot_general(stacked, ow[...], NT, preferred_element_type=jnp.float32)
        )

    def core_copy(s):
        return remote(core_out.at[s], core_in.at[s], core_send.at[s], core_recv.at[s], core_dev)

    def x_copy(s):
        return remote(x_out.at[s], x_in.at[s], x_send.at[s], x_recv.at[s], x_dev)

    for s in range(seqs):
        for block in (0, ctxs - 1) + tuple(range(1, ctxs - 1)):

            @pl.when(block != c)
            def _():
                att_copy(block, c, s).wait_recv()

            if block in (0, ctxs - 1):

                @pl.when(c == lax.abs(block - (ctxs - 2)))
                def _():
                    att_onward(block, s).start()

        across = (1 - side, side)
        core_out[s] = projected([2 * to + 1 - core for to in across], s).astype(jnp.bfloat16)
        core_copy(s).start()
        keep[s] = projected([2 * to + core for to in across], s)
        core_copy(s).wait_recv()
        x_out[s] = (keep[s, :tokens] + core_in[s, :tokens].astype(jnp.float32)).astype(
            jnp.bfloat16
        )
        x_copy(s).start()

    @pl.when(c != h)
    def _():
        stream_copy.wait_recv()

    @pl.when(c == h)
    def _():
        stream_local.wait()

    def h_copy(way, block, row, s, device):
        part = h_all.at[block, row, pl.ds(s * tokens, tokens)]
        return remote(part, part, h_send.at[way, block, s], h_recv.at[block, row, s], device)

    def h_core(block, row, s):
        return h_copy(jnp.where(row == h, 0, 1), block, row, s, core_dev)

    def h_x(block, s):
        return h_copy(2, block, h, s, x_dev)

    def h_right(block, s):
        return h_copy(3, block, h, s, (jnp.minimum(c + 1, ctxs - 1), h, r))

    def h_left(block, s):
        return h_copy(4, block, h, s, (jnp.maximum(c - 1, 0), h, r))

    def arrived(block, row, s):
        h_copy(0, block, row, s, core_dev).wait_recv()

    for s in range(seqs):
        kept = (
            keep[s, tokens:]
            + core_in[s, tokens:].astype(jnp.float32)
            + widened(stream_in[s].astype(jnp.float32))
        )
        x_copy(s).wait_recv()
        h_all[c, h, s * tokens : (s + 1) * tokens] = (
            kept + x_in[s].astype(jnp.float32)
        ).astype(jnp.bfloat16)
        h_x(c, s).start()

        @pl.when(c < ctxs - 1)
        def _():
            h_right(c, s).start()

        @pl.when(c > 0)
        def _():
            h_left(c, s).start()

        h_core(c, h, s).start()

    square_ref[...] = jnp.zeros(square_ref.shape, jnp.float32)
    logits_ref[...] = jnp.zeros(logits_ref.shape, jnp.float32)

    def take(block):
        for s in range(seqs):
            arrived(block, h ^ 1, s)
            arrived(block, h ^ 3, s)
        for row in range(ctxs):
            here = slice(row * rows, (row + 1) * rows)
            piece = h_all[block, row].astype(jnp.float32)
            y_ref[here, :] = (piece * gains[block][:1]).astype(jnp.bfloat16)
            square = piece * piece
            square_ref[here, :] += sum(
                square[:, i : i + LANES] for i in range(0, pad_cols, LANES)
            )
        xg[block] = lax.dot_general(
            pick[...], y_ref[...], NN, preferred_element_type=jnp.float32
        ).astype(jnp.bfloat16)
        logits_ref[...] += lax.dot_general(
            y_ref[...], routers[block], NT, preferred_element_type=jnp.float32
        )

    for d in range(1, ctxs + 1):
        for s in range(seqs):

            @pl.when(c - d >= 0)
            def _():
                arrived(c - d, h, s)

                @pl.when(c < ctxs - 1)
                def _():
                    h_right(c - d, s).start()

                h_x(c - d, s).start()
                h_core(c - d, h, s).start()

            @pl.when(c + d < ctxs)
            def _():
                arrived(c + d, h, s)

                @pl.when(c > 0)
                def _():
                    h_left(c + d, s).start()

                h_x(c + d, s).start()
                h_core(c + d, h, s).start()

            @pl.when(c - (d - 1) >= 0)
            def _():
                arrived(c - (d - 1), h ^ 2, s)
                h_core(c - (d - 1), h ^ 2, s).start()

            if d > 1:

                @pl.when(c + (d - 1) < ctxs)
                def _():
                    arrived(c + (d - 1), h ^ 2, s)
                    h_core(c + (d - 1), h ^ 2, s).start()

        @pl.when(c - (d - 1) >= 0)
        def _():
            take(c - (d - 1))

        if d > 1:

            @pl.when(c + (d - 1) < ctxs)
            def _():
                take(c + (d - 1))

    inverse = lax.rsqrt(jnp.sum(square_ref[...], axis=1, keepdims=True) / width + 1e-05)
    square_ref[...] = jnp.broadcast_to(inverse, square_ref.shape)
    inverse_row = jnp.transpose(square_ref[...])[:1]
    first = inverse_row.astype(jnp.bfloat16)
    rest = inverse_row - first.astype(jnp.float32)
    second = rest.astype(jnp.bfloat16)
    third = (rest - second.astype(jnp.float32)).astype(jnp.bfloat16)
    in_parts = jnp.concatenate(
        [part.astype(jnp.float32) for part in (first, second, third)]
        + [jnp.zeros((5, all_rows), jnp.float32)],
        axis=0,
    ).astype(jnp.bfloat16)
    for e in range(local_experts):
        found = lax.dot_general(
            in_parts, pick[e * cap : (e + 1) * cap, :], NT, preferred_element_type=jnp.float32
        )
        scale_ref[e] = jnp.broadcast_to(jnp.sum(found, axis=0, keepdims=True), (8, cap))

    def act_core(shard, e):
        return remote(
            act_all.at[shard, e],
            act_all.at[shard, e],
            act_send.at[jnp.where(shard == h, 0, 1), e],
            act_recv.at[shard, e],
            core_dev,
        )

    def act_x(e):
        return remote(
            act_all.at[h, e], act_all.at[h, e], act_send.at[2, e], act_recv.at[h, e], x_dev
        )

    def act_arrived(shard, e):
        remote(
            act_all.at[shard, e],
            act_all.at[shard, e],
            act_send.at[0, e],
            act_recv.at[shard, e],
            core_dev,
        ).wait_recv()

    lead = wide - width
    packed = act_all.shape[3]

    def activated(e, slot):
        pieces = [
            xg[block, pl.ds(pl.multiple_of(e * cap, cap), cap), :][:, :cols]
            for block in range(ctxs)
        ]
        blank = [jnp.zeros((cap, lead), jnp.bfloat16)]
        rows_in = jnp.concatenate(pieces + blank, axis=1)
        shifted = jnp.concatenate(blank + pieces, axis=1)
        factor = scale_ref[e][:1]
        gate = factor * lax.dot_general(
            wg[slot, :, :, :wide].reshape(2 * units, wide),
            rows_in,
            NT,
            preferred_element_type=jnp.float32,
        )
        up = factor * lax.dot_general(
            wg[slot, :, :, 2 * width - wide :].reshape(2 * units, wide),
            shifted,
            NT,
            preferred_element_type=jnp.float32,
        )
        return gate * jax.nn.sigmoid(1.702 * gate) * (up + 1.0)

    def hand_out(e, active):
        unit_rows[...] = jnp.concatenate(
            [active, jnp.zeros((2 * units, LANES - cap), jnp.float32)], axis=1
        )
        stacked = jnp.concatenate(
            [unit_rows[pl.ds(u, units, stride=2), :] for u in range(2)]
            + [jnp.zeros((packed - 2 * units, LANES), jnp.float32)],
            axis=0,
        )
        act_all[h, e] = jnp.transpose(stacked)[:cap].astype(jnp.bfloat16)
        act_x(e).start()
        act_core(h, e).start()

    @pl.loop(0, local_experts)
    def _(e):
        slot = lax.rem(e, slots)
        wg_copy(e, slot).wait()
        hand_out(e, activated(e, slot))

        @pl.when(e + slots < local_experts)
        def _():
            wg_copy(e + slots, slot).start()

        @pl.when(e >= 2)
        def _():
            act_arrived(h ^ 2, e - 2)
            act_core(h ^ 2, e - 2).start()

    by_token = token_ref[...]
    logits = logits_ref[...] * square_ref[:, :1]
    experts = logits.shape[1]
    expert_lane = lax.broadcasted_iota(jnp.int32, (all_rows, experts), 1).astype(jnp.float32)
    named = jnp.zeros((all_rows, experts), jnp.bool_)
    for k in range(topk):
        named = named | (expert_lane == by_token[:, k : k + 1])
    top = jnp.max(jnp.where(named, logits, -1e30), axis=1, keepdims=True)
    weight = jnp.where(named, jnp.exp(logits - top), 0.0)
    mix = weight / jnp.sum(weight, axis=1, keepdims=True)
    mix = jnp.concatenate([mix, jnp.zeros((all_rows, LANES - experts), jnp.float32)], axis=1)
    mix = pltpu.roll(mix, lax.rem(LANES - c * local_experts, LANES), 1)
    slot_lane = lax.broadcasted_iota(jnp.int32, (all_rows, LANES), 1).astype(jnp.float32)
    for e in range(local_experts):
        spread[:, e * LANES : (e + 1) * LANES] = jnp.where(
            slot_lane == by_token[:, 8 + e : 9 + e], mix[:, e : e + 1], 0.0
        ).astype(jnp.bfloat16)

    for e in range(local_experts - 2, local_experts):
        act_arrived(h ^ 2, e)
        act_core(h ^ 2, e).start()

    def rs_copy(src, dst, j):
        return remote(
            rs_out.at[dst, j], rs_in.at[src, j], rs_send.at[dst, j], rs_recv.at[src, j], (dst, h, r)
        )

    def combined(block, j):
        return lax.dot_general(
            spread[pl.ds(pl.multiple_of(block * rows, rows), rows), :],
            parts[j],
            NN,
            preferred_element_type=jnp.float32,
        )

    outer = (c == 0) | (c == ctxs - 1)
    far = ctxs - 1 - c
    relay_dst = jnp.where(c == 0, 1, 2)
    end_dst = jnp.where(c == 1, 3, 0)

    def relay_copy(j):
        return remote(
            rs_out.at[far, j],
            relay_in.at[j],
            rs_send.at[far, j],
            relay_recv.at[j],
            (relay_dst, h, r),
        )

    chunk = parts.shape[2]
    chunks = parts.shape[0]
    for j in range(chunks):
        first_col = j * chunk
        last_col = min(cols, first_col + chunk)

        @pl.loop(0, local_experts)
        def _(e):
            if j == 0:
                wd_copy(e).wait()
                act_arrived(h ^ 1, e)
                act_arrived(h ^ 3, e)
                for u in range(2):
                    hidden_ref[2 * e + u] = jnp.concatenate(
                        [act_all[shard, e][:, u * units : (u + 1) * units] for shard in range(4)],
                        axis=1,
                    )
            total = None
            for u in range(2):
                piece = lax.dot_general(
                    hidden_ref[2 * e + u],
                    wd[2 * e + u, :, first_col:last_col],
                    NN,
                    preferred_element_type=jnp.float32,
                )
                total = piece if total is None else total + piece
            if last_col - first_col < chunk:
                extra = jnp.zeros((cap, chunk - (last_col - first_col)), jnp.float32)
                total = jnp.concatenate([total, extra], axis=1)
            parts[j, pl.ds(pl.multiple_of(e * LANES, LANES), cap), :] = total.astype(jnp.bfloat16)

        @pl.when(outer)
        def _():
            rs_out[far, j] = combined(far, j).astype(jnp.bfloat16)
            relay_copy(j).start()
            for dst in (ctxs - 1 - relay_dst, relay_dst):
                rs_out[dst, j] = combined(dst, j).astype(jnp.bfloat16)
                rs_copy(c, dst, j).start()

        @pl.when(jnp.logical_not(outer))
        def _():
            for dst in (ctxs - 1 - c, ctxs - 1 - end_dst):
                rs_out[dst, j] = combined(dst, j).astype(jnp.bfloat16)
                rs_copy(c, dst, j).start()

    @pl.when(jnp.logical_not(outer))
    def _():
        for j in range(chunks):
            ends = combined(end_dst, j)
            relay_copy(j).wait_recv()
            rs_out[end_dst, j] = (ends + relay_in[j].astype(jnp.float32)).astype(jnp.bfloat16)
            rs_copy(c, end_dst, j).start()

    own = h_all[h, c].astype(jnp.float32)
    for j in range(chunks):
        here = slice(j * chunk, (j + 1) * chunk)
        total_ref[:, here] = combined(c, j) + own[:, here]
    for j in range(chunks):
        here = slice(j * chunk, (j + 1) * chunk)
        for src in (1, 2, 0, 3):
            sends_here = (src != c) & jnp.logical_not(outer & (src == far))

            @pl.when(sends_here)
            def _():
                rs_copy(src, c, j).wait_recv()
                total_ref[:, here] += rs_in[src, j].astype(jnp.float32)

    total = total_ref[...]
    out_ref[...] = total[:, :cols].astype(jnp.bfloat16).reshape(out_ref.shape)

    for dst in range(ctxs):

        @pl.when(dst > c)
        def _():
            kv_copy(c, dst).wait_send()

        @pl.when(dst != c)
        def _():
            ids_copy(c, dst).wait_send()
            for j in range(chunks):
                rs_copy(c, dst, j).wait_send()

        @pl.when((dst != c) & (lax.abs(dst - c) < ctxs - 1))
        def _():
            for s in range(seqs):
                att_copy(c, dst, s).wait_send()

    @pl.when((c == 1) | (c == ctxs - 2))
    def _():
        for s in range(seqs):
            att_onward(jnp.where(c == 1, ctxs - 1, 0), s).wait_send()

    @pl.when(c != h)
    def _():
        stream_copy.wait_send()

    for s in range(seqs):
        x_copy(s).wait_send()
        core_copy(s).wait_send()
        for block in range(ctxs):
            h_x(block, s).wait_send()
            h_core(block, h, s).wait_send()
            h_core(block, h ^ 2, s).wait_send()

            @pl.when((c < ctxs - 1) & (block <= c))
            def _():
                h_right(block, s).wait_send()

            @pl.when((c > 0) & (block >= c))
            def _():
                h_left(block, s).wait_send()

    for e in range(local_experts):
        act_x(e).wait_send()
        act_core(h, e).wait_send()
        act_core(h ^ 2, e).wait_send()


def layer_call(queries, keyvals, sinks, stream, out_weight, gain, router, ids, w_gate_up, w_down):
    seqs, tokens, q_cols = queries.shape
    cols = stream.shape[2]
    ctxs = lax.axis_size("ctx")
    rows = seqs * tokens
    width = gain.shape[0]
    halves, units, wide_w = w_gate_up.shape
    local_experts = halves // 2
    all_rows = ctxs * rows
    cap = all_rows * 3 // 16
    pad_cols = pl.cdiv(cols, 2 * LANES) * 2 * LANES
    packed = pl.cdiv(2 * units, LANES) * LANES
    slots = min(4, local_experts)
    chunk = 2 * LANES
    chunks = pl.cdiv(cols, chunk)
    sizes = (seqs, tokens, rows, ctxs, width, cols, cap, local_experts, units, slots)
    bf16, f32 = jnp.bfloat16, jnp.float32
    dma = pltpu.SemaphoreType.DMA
    vmem = pl.BlockSpec(memory_space=pltpu.VMEM)
    hbm = pl.BlockSpec(memory_space=pl.ANY)
    return pl.pallas_call(
        functools.partial(layer_kernel, sizes),
        out_shape=jax.ShapeDtypeStruct((seqs, tokens, cols), bf16),
        in_specs=[hbm, hbm, vmem, pl.BlockSpec(memory_space=pltpu.SMEM)] + [hbm] * 6,
        out_specs=vmem,
        scratch_shapes=[
            pltpu.VMEM(queries.shape, bf16),
            pltpu.VMEM(gain.shape, f32),
            pltpu.VMEM((ctxs, 8, pad_cols), f32),
            pltpu.VMEM((ctxs, seqs, tokens, keyvals.shape[3]), bf16),
            pltpu.VMEM((ctxs, 8, LANES), f32),
            pltpu.VMEM((seqs, tokens, cols), bf16),
            pltpu.VMEM(out_weight.shape[::-1], bf16),
            pltpu.VMEM(router.shape[::-1], bf16),
            pltpu.VMEM((ctxs, router.shape[1], pad_cols), bf16),
            pltpu.VMEM((slots, units, 2, wide_w), bf16),
            pltpu.VMEM(w_down.shape, bf16),
            pltpu.VMEM((ctxs, rows, q_cols), bf16),
            pltpu.VMEM((seqs, 2 * tokens, pad_cols), bf16),
            pltpu.VMEM((seqs, 2 * tokens, pad_cols), bf16),
            pltpu.VMEM((seqs, 2 * tokens, pad_cols), f32),
            pltpu.VMEM((seqs, tokens, pad_cols), bf16),
            pltpu.VMEM((seqs, tokens, pad_cols), bf16),
            pltpu.VMEM((ctxs, 4, rows, pad_cols), bf16),
            pltpu.VMEM((all_rows, pad_cols), bf16),
            pltpu.VMEM((all_rows, LANES), f32),
            pltpu.VMEM((all_rows, router.shape[1]), f32),
            pltpu.VMEM((all_rows, LANES), f32),
            pltpu.VMEM((local_experts * cap, all_rows), bf16),
            pltpu.VMEM((all_rows, local_experts * LANES), bf16),
            pltpu.VMEM((ctxs, local_experts * cap, pad_cols), bf16),
            pltpu.VMEM((local_experts, 8, cap), f32),
            pltpu.VMEM((2 * units, LANES), f32),
            pltpu.VMEM((4, local_experts, cap, packed), bf16),
            pltpu.VMEM((chunks, local_experts * LANES, chunk), bf16),
            pltpu.VMEM((ctxs, chunks, rows, chunk), bf16),
            pltpu.VMEM((ctxs, chunks, rows, chunk), bf16),
            pltpu.VMEM((chunks, rows, chunk), bf16),
            pltpu.VMEM((halves, cap, w_down.shape[1]), bf16),
            pltpu.VMEM((rows, chunks * chunk), f32),
            dma((6,)),
            dma((slots,)),
            dma((local_experts,)),
            dma((ctxs,)),
            dma((ctxs,)),
            dma((ctxs,)),
            dma((ctxs,)),
            dma((1,)),
            dma((1,)),
            dma((ctxs, seqs)),
            dma((ctxs, seqs)),
            dma((seqs,)),
            dma((seqs,)),
            dma((seqs,)),
            dma((seqs,)),
            dma((5, ctxs, seqs)),
            dma((ctxs, 4, seqs)),
            dma((3, local_experts)),
            dma((4, local_experts)),
            dma((ctxs, chunks)),
            dma((ctxs, chunks)),
            dma((chunks,)),
            dma((seqs,)),
        ],
        compiler_params=pltpu.CompilerParams(
            vmem_limit_bytes=67043328, collective_id=0, has_side_effects=True
        ),
    )(
        queries,
        keyvals.reshape(seqs, tokens, keyvals.shape[3]),
        jnp.transpose(ids, (0, 2, 1)),
        sinks,
        gain,
        stream,
        out_weight.T,
        router.T,
        jnp.transpose(w_gate_up, (1, 0, 2)),
        w_down,
    )


def one_chip_row(queries, keyvals, stream, out_weight, router, ids, w_gate_up):
    ctxs, heads = lax.axis_size("ctx"), lax.axis_size("head")
    rows = queries.shape[0] * queries.shape[1]
    return (
        ctxs == heads == 4
        and rows == LANES
        and keyvals.shape[2] == 1
        and keyvals.shape[3] == LANES
        and out_weight.shape[1] == stream.shape[2]
        and w_gate_up.shape[0] == 16
        and ids.shape[2] <= 8
        and router.shape[1] <= LANES
    )


def on_device(
    queries, keyvals, sinks, stream, out_weight, norm_gain, router, expert_ids, w_gate_up, w_down
):
    if one_chip_row(queries, keyvals, stream, out_weight, router, expert_ids, w_gate_up):
        return layer_call(
            queries,
            keyvals,
            sinks,
            stream,
            out_weight,
            norm_gain,
            router,
            expert_ids,
            w_gate_up,
            w_down,
        )
    ctx_count = lax.axis_size("ctx")
    local_seqs = queries.shape[0]
    tokens = queries.shape[1]
    row_count = local_seqs * tokens
    kv_local = keyvals.shape[2]
    head_dim = keyvals.shape[3] // 2
    q_local = queries.shape[2] // head_dim
    query_group_size = q_local // kv_local
    wide_rows = query_group_size * tokens
    col_width = stream.shape[2]
    first_pos = lax.axis_index("ctx") * tokens
    last_pos = first_pos + tokens - 1
    score_scale = head_dim ** (-0.5)
    scaled_queries = queries * jnp.asarray(score_scale, jnp.bfloat16)
    query_grid = scaled_queries.reshape(local_seqs, tokens, kv_local, query_group_size, head_dim)
    query_wide = jnp.transpose(query_grid, (0, 2, 3, 1, 4)).reshape(
        local_seqs, kv_local, wide_rows, head_dim
    )
    positions = first_pos + jnp.tile(jnp.arange(tokens), query_group_size)
    sink_rows = jnp.repeat(sinks.reshape(kv_local, query_group_size), tokens, axis=1)
    sink_grid = jnp.broadcast_to(sink_rows[None], (local_seqs, kv_local, wide_rows))
    start_state = (
        sink_grid,
        jnp.ones_like(sink_grid),
        jnp.zeros((local_seqs, kv_local, head_dim, wide_rows), jnp.float32),
    )

    def attend_block(running, shard_piece):
        peak_old, denom_old, accum_old = running
        key_block = shard_piece[..., :head_dim]
        value_block = shard_piece[..., head_dim:]
        scores = jnp.einsum(
            "skmd,snkd->sknm", query_wide, key_block, preferred_element_type=jnp.float32
        )
        key_pos = jnp.arange(shard_piece.shape[1])
        visible = key_pos[:, None] <= positions[None, :]
        masked = jnp.where(visible[None, None], scores, -jnp.inf)
        peak_new = jnp.maximum(peak_old, jnp.max(masked, axis=2))
        exp_terms = jnp.exp(masked - peak_new[:, :, None, :])
        factor = jnp.exp(peak_old - peak_new)
        denom_new = denom_old * factor + jnp.sum(exp_terms, axis=2)
        accum_new = accum_old * factor[:, :, None, :] + jnp.einsum(
            "sknm,snkd->skdm",
            exp_terms.astype(jnp.bfloat16),
            value_block,
            preferred_element_type=jnp.float32,
        )
        return (peak_new, denom_new, accum_new)

    shard_piece = lax.all_gather(keyvals, "ctx", axis=1, tiled=True)

    def keep_state(state_in):
        return state_in

    def update_state(state_in):
        return attend_block(state_in, shard_piece)

    peak_fin, denom_fin, accum_fin = lax.cond(
        jnp.int32(0) > last_pos, keep_state, update_state, start_state
    )
    normalized = (accum_fin / denom_fin[:, :, None, :]).reshape(
        local_seqs, kv_local, head_dim, query_group_size, tokens
    )
    attended = (
        jnp.transpose(normalized, (0, 4, 1, 3, 2))
        .reshape(row_count, q_local * head_dim)
        .astype(jnp.bfloat16)
    )
    token_ids = lax.all_gather(
        expert_ids.reshape(row_count, expert_ids.shape[2]).T, "ctx", axis=1, tiled=True
    )
    all_rows = ctx_count * row_count
    halves = w_gate_up.shape[0]
    units = w_gate_up.shape[1]
    token_block = min(all_rows, 8 * tokens)
    cap = token_block // tokens * (3 * tokens // 16)
    row_expert = (lax.axis_index("ctx") * halves + jnp.arange(halves)) // 2
    named = jnp.any(token_ids[:, None, :] == row_expert[None, :, None], axis=0)
    counted = named.astype(jnp.int32).reshape(halves, all_rows // token_block, token_block)
    rank = jnp.cumsum(counted, axis=2) - 1
    slots = jnp.where(named, rank.reshape(halves, all_rows), -1).reshape(halves, 1, all_rows)
    width = norm_gain.shape[0]
    head_count = lax.axis_size("head")
    swapped = ctx_count == head_count and out_weight.shape[1] == col_width
    if swapped:
        pairs = [
            (first * head_count + second, second * head_count + first)
            for first in range(ctx_count)
            for second in range(head_count)
        ]
        turned = lax.ppermute(
            stream.reshape(row_count, col_width), ("ctx", "head"), perm=pairs
        )
        every_row = lax.all_gather(attended, "ctx", axis=0, tiled=True)
        partial_proj = jnp.dot(every_row, out_weight, preferred_element_type=jnp.float32)
        summed = lax.psum_scatter(
            partial_proj.astype(jnp.bfloat16), "head", scatter_dimension=0, tiled=True
        )
        turned_state = summed.astype(jnp.float32) + turned.astype(jnp.float32)
        every_state = lax.all_gather(
            turned_state.astype(jnp.bfloat16), ("head", "ctx"), axis=0, tiled=False
        )
    else:
        partial_proj = jnp.dot(attended, lax.all_gather(out_weight, "ctx", axis=1, tiled=True), preferred_element_type=jnp.float32)
        own_stream = stream.reshape(row_count, col_width).astype(jnp.float32)
        summed = lax.psum_scatter(
            partial_proj.astype(jnp.bfloat16), "head", scatter_dimension=1, tiled=True
        )
        own_state = (summed.astype(jnp.float32) + own_stream).astype(jnp.bfloat16)
        every_state = lax.all_gather(own_state, ("ctx", "head"), axis=0, tiled=False)
    every_state = every_state.reshape(ctx_count, width // col_width, row_count, col_width)
    expert_count = router.shape[1]
    unit_rows = jnp.transpose(w_gate_up, (1, 0, 2)).reshape(units * halves, w_gate_up.shape[2])
    router_rows = jnp.pad(router.T, ((0, 0), (0, -width % LANES)))
    gain = norm_gain.reshape(width // col_width, 1, col_width)
    active, logits = gate_up_call(
        every_state, gain, router_rows, unit_rows, slots, units, token_block, cap
    )
    member = jnp.any(token_ids[:, None, :] == jnp.arange(expert_count)[None, :, None], axis=0)
    masked = jnp.where(member, logits, -jnp.inf)
    mix_all = jax.nn.softmax(masked, axis=0)
    chosen_rows = (row_expert[:, None] == jnp.arange(expert_count)[None, :]).astype(jnp.float32)
    mix_rows = jnp.dot(chosen_rows, mix_all, precision=lax.Precision.HIGHEST)
    mix_rows = mix_rows.reshape(halves, 1, all_rows)
    every_active = lax.all_gather(active.reshape(-1, units), "head", axis=0, tiled=True)
    every_active = every_active.reshape(width // col_width, *active.shape)
    partial_out = down_call(every_active, w_down, slots, mix_rows, token_block)
    combined = lax.psum_scatter(partial_out, "ctx", scatter_dimension=0, tiled=True)
    if swapped:
        own_state = every_state[lax.axis_index("ctx"), lax.axis_index("head")]
    layer_out = (own_state.astype(jnp.float32) + combined.astype(jnp.float32)).astype(jnp.bfloat16)
    return layer_out.reshape(local_seqs, tokens, col_width)


def solution(mesh):
    placed = (
        P("rep", "ctx", "head"),
        P("rep", "ctx", "head", None),
        P("head"),
        P("rep", "ctx", "head"),
        P("head", "ctx"),
        P(),
        P(),
        P("rep", "ctx", None),
        P("ctx", "head", None),
        P("ctx", None, "head"),
    )
    return jax.shard_map(
        on_device, mesh=mesh, in_specs=placed, out_specs=P("rep", "ctx", "head"), check_vma=False
    )
```

```python
import functools

import jax
import jax.numpy as jnp
from jax import lax
from jax.experimental import pallas as pl
from jax.experimental.pallas import tpu as pltpu
from jax.sharding import PartitionSpec as P


NT = (((1,), (1,)), ((), ()))
TN = (((0,), (0,)), ((), ()))
LANES = 128


def one_hot_rows(slots, cap, value):
    rows = lax.broadcasted_iota(jnp.int32, (cap, slots.shape[1]), 0)
    return jnp.where(rows == slots, value, 0.0).astype(jnp.bfloat16)


def gate_up_kernel(
    halves,
    units,
    state_ref,
    gain_ref,
    router_ref,
    w_ref,
    slot_ref,
    out_ref,
    logits_ref,
    act_ref,
    xg_ref,
    xu_ref,
):
    step = pl.program_id(1)
    groups, shards, group_rows, cols = state_ref.shape

    @pl.when(step == 0)
    def _():
        for group in range(groups):
            pieces = [state_ref[group, shard].astype(jnp.float32) for shard in range(shards)]
            square = sum(jnp.sum(piece * piece, axis=1, keepdims=True) for piece in pieces)
            inverse = lax.rsqrt(square / (shards * cols) + 1e-05)
            scaled = [
                (piece * inverse * gain_ref[shard]).astype(jnp.bfloat16)
                for shard, piece in enumerate(pieces)
            ]
            extra = xg_ref.shape[1] - shards * cols
            blank = [jnp.zeros((group_rows, extra), jnp.bfloat16)] if extra else []
            here = slice(group * group_rows, (group + 1) * group_rows)
            xg_ref[here, :] = jnp.concatenate(scaled + blank, axis=1)
            xu_ref[here, :] = jnp.concatenate(blank + scaled, axis=1)
        logits_ref[...] = lax.dot_general(
            router_ref[...], xg_ref[...], NT, preferred_element_type=jnp.float32
        )

    rows, wide = w_ref.shape[0], xg_ref.shape[1]
    gate = lax.dot_general(w_ref[:, :wide], xg_ref[...], NT, preferred_element_type=jnp.float32)
    up = lax.dot_general(
        w_ref[:, w_ref.shape[1] - wide :], xu_ref[...], NT, preferred_element_type=jnp.float32
    )
    active = gate * jax.nn.sigmoid(1.702 * gate) * (up + 1.0)
    slabs = act_ref.shape[0]
    for slab in range(slabs):
        act_ref[slab, pl.ds(step * rows, rows), :] = active[:, slab * LANES : (slab + 1) * LANES]

    @pl.when(step == pl.num_programs(1) - 1)
    def _():
        for row in range(halves):
            wanted = pl.ds(row, units, stride=halves) if halves > 1 else pl.ds(0, units)
            picked = jnp.concatenate([act_ref[slab, wanted, :] for slab in range(slabs)], axis=1)
            spread = one_hot_rows(slot_ref[row], out_ref.shape[2], 1.0)
            out_ref[row, 0] = lax.dot_general(
                spread, picked.astype(jnp.bfloat16), NT, preferred_element_type=jnp.float32
            ).astype(jnp.bfloat16)


def gate_up_call(state, gain, router, weights, slots, units, token_block, cap):
    halves = slots.shape[0]
    sources, shards, group_rows, cols = state.shape
    groups = token_block // group_rows
    blocks = sources // groups
    experts, wide = router.shape
    wide_w = weights.shape[1]
    sizes = [
        size
        for size in range(1, units + 1)
        if units % size == 0
        and (size == units or (size * halves) % 16 == 0)
        and size * halves * wide_w * 2 <= 4 << 20
    ]
    size = sizes[-1]
    return pl.pallas_call(
        functools.partial(gate_up_kernel, halves, units),
        grid=(blocks, units // size),
        out_shape=(
            jax.ShapeDtypeStruct((halves, blocks, cap, units), jnp.bfloat16),
            jax.ShapeDtypeStruct((experts, blocks * token_block), jnp.float32),
        ),
        in_specs=[
            pl.BlockSpec((groups, shards, group_rows, cols), lambda i, j: (i, 0, 0, 0)),
            pl.BlockSpec((shards, 1, cols), lambda i, j: (0, 0, 0)),
            pl.BlockSpec((experts, wide), lambda i, j: (0, 0)),
            pl.BlockSpec((size * halves, wide_w), lambda i, j: (j, 0)),
            pl.BlockSpec((halves, 1, token_block), lambda i, j: (0, 0, i)),
        ],
        out_specs=(
            pl.BlockSpec((halves, 1, cap, units), lambda i, j: (0, i, 0, 0)),
            pl.BlockSpec((experts, token_block), lambda i, j: (0, i)),
        ),
        scratch_shapes=[
            pltpu.VMEM((token_block // LANES, units * halves, LANES), jnp.float32),
            pltpu.VMEM((token_block, wide), jnp.bfloat16),
            pltpu.VMEM((token_block, wide), jnp.bfloat16),
        ],
        compiler_params=pltpu.CompilerParams(vmem_limit_bytes=56 << 20),
    )(state, gain, router, weights, slots)


def down_kernel(act_ref, w_ref, slot_ref, mix_ref, out_ref, total_ref):
    step = pl.program_id(1)
    part = None
    for row in range(w_ref.shape[0]):
        pieces = [act_ref[shard, row, 0] for shard in range(act_ref.shape[0])]
        hidden = jnp.concatenate(pieces, axis=1)
        piece = jnp.dot(hidden, w_ref[row], preferred_element_type=jnp.float32)
        part = piece if part is None else part + piece
    spread = one_hot_rows(slot_ref[0], act_ref.shape[3], mix_ref[0])
    added = lax.dot_general(
        spread, part.astype(jnp.bfloat16), TN, preferred_element_type=jnp.float32
    )

    @pl.when(step == 0)
    def _():
        total_ref[...] = added

    @pl.when(step != 0)
    def _():
        total_ref[...] += added

    @pl.when(step == pl.num_programs(1) - 1)
    def _():
        out_ref[...] = total_ref[...].astype(jnp.bfloat16)


def down_call(act, weights, slots, mix, token_block):
    shards, halves, blocks, cap, units = act.shape
    hidden, cols = weights.shape[1:]
    pair = 2 if halves % 2 == 0 else 1
    return pl.pallas_call(
        down_kernel,
        grid=(blocks, halves // pair),
        out_shape=jax.ShapeDtypeStruct((blocks * token_block, cols), jnp.bfloat16),
        in_specs=[
            pl.BlockSpec((shards, pair, 1, cap, units), lambda i, r: (0, r, i, 0, 0)),
            pl.BlockSpec((pair, hidden, cols), lambda i, r: (r, 0, 0)),
            pl.BlockSpec((1, 1, token_block), lambda i, r: (r * pair, 0, i)),
            pl.BlockSpec((1, 1, token_block), lambda i, r: (r * pair, 0, i)),
        ],
        out_specs=pl.BlockSpec((token_block, cols), lambda i, r: (i, 0)),
        scratch_shapes=[pltpu.VMEM((token_block, cols), jnp.float32)],
        compiler_params=pltpu.CompilerParams(vmem_limit_bytes=48 << 20),
    )(act, weights, slots, mix)


MESH = pl.DeviceIdType.MESH
NN = (((1,), (0,)), ((), ()))


def layer_kernel(
    sizes,
    q_hbm,
    kv_hbm,
    ids_ref,
    sink_ref,
    gain_hbm,
    stream_hbm,
    ow_hbm,
    router_hbm,
    wg_hbm,
    wd_hbm,
    out_ref,
    q_ref,
    gain_ref,
    gains,
    kv_all,
    ids_all,
    stream_in,
    ow,
    router,
    routers,
    wg,
    wd,
    att_all,
    core_out,
    core_in,
    keep,
    x_out,
    x_in,
    h_all,
    y_ref,
    square_ref,
    logits_ref,
    token_ref,
    pick,
    spread,
    xg,
    scale_ref,
    unit_rows,
    act_all,
    parts,
    rs_out,
    rs_in,
    relay_in,
    hidden_ref,
    total_ref,
    local_sem,
    wg_sem,
    wd_sem,
    kv_send,
    kv_recv,
    ids_send,
    ids_recv,
    stream_send,
    stream_recv,
    att_send,
    att_recv,
    core_send,
    core_recv,
    x_send,
    x_recv,
    h_send,
    h_recv,
    act_send,
    act_recv,
    rs_send,
    rs_recv,
    relay_recv,
    onward_send,
):
    seqs, tokens, rows, ctxs, width, cols, cap, local_experts, units, slots = sizes
    c, h, r = lax.axis_index("ctx"), lax.axis_index("head"), lax.axis_index("rep")
    all_rows = ctxs * rows
    wide = pl.cdiv(width, LANES) * LANES
    pad_cols = h_all.shape[3]
    core_dev, x_dev = (c, h ^ 1, r), (c, h ^ 2, r)
    partner = (h, c, r)

    def remote(src, dst, send, recv, device):
        return pltpu.make_async_remote_copy(
            src_ref=src,
            dst_ref=dst,
            send_sem=send,
            recv_sem=recv,
            device_id=device,
            device_id_type=MESH,
        )

    ow_copy = pltpu.make_async_copy(ow_hbm, ow, local_sem.at[0])
    router_copy = pltpu.make_async_copy(router_hbm, router, local_sem.at[1])
    q_copy = pltpu.make_async_copy(q_hbm, q_ref, local_sem.at[3])
    kv_local = pltpu.make_async_copy(kv_hbm, kv_all.at[c], local_sem.at[4])
    gain_copy = pltpu.make_async_copy(gain_hbm, gain_ref, local_sem.at[5])

    def wg_copy(e, slot):
        return pltpu.make_async_copy(
            wg_hbm.at[:, pl.ds(2 * e, 2), :], wg.at[slot], wg_sem.at[slot]
        )

    def wd_copy(e):
        return pltpu.make_async_copy(
            wd_hbm.at[pl.ds(2 * e, 2)], wd.at[pl.ds(2 * e, 2)], wd_sem.at[e]
        )

    barrier = pltpu.get_barrier_semaphore()
    for step in range(1, ctxs):
        pl.semaphore_signal(
            barrier, inc=1, device_id=(lax.rem(c + step, ctxs), h, r), device_id_type=MESH
        )
    pl.semaphore_signal(barrier, inc=1, device_id=core_dev, device_id_type=MESH)
    pl.semaphore_signal(barrier, inc=1, device_id=x_dev, device_id_type=MESH)

    @pl.when(c != h)
    def _():
        pl.semaphore_signal(barrier, inc=1, device_id=partner, device_id_type=MESH)

    kv_local.start()
    q_copy.start()
    gain_copy.start()
    router_copy.start()
    ow_copy.start()
    for e in range(min(slots, local_experts)):
        wg_copy(e, e).start()
    for e in range(local_experts):
        wd_copy(e).start()
    topk = ids_ref.shape[1]
    own_ids = jnp.concatenate([ids_ref[s] for s in range(seqs)], axis=1).astype(jnp.float32)
    ids_all[c] = jnp.concatenate(
        [own_ids, jnp.full((8 - topk, rows), -1.0, jnp.float32)], axis=0
    )
    for other in range(ctxs):

        @pl.when(other > c)
        def _():
            kv_all[other] = jnp.zeros(kv_all.shape[1:], jnp.bfloat16)

    parts[...] = jnp.zeros(parts.shape, jnp.bfloat16)
    pl.semaphore_wait(barrier, ctxs + 1 + (c != h).astype(jnp.int32))

    def kv_copy(src, dst):
        return remote(kv_hbm, kv_all.at[src], kv_send.at[dst], kv_recv.at[src], (dst, h, r))

    def ids_copy(src, dst):
        return remote(
            ids_all.at[src], ids_all.at[src], ids_send.at[dst], ids_recv.at[src], (dst, h, r)
        )

    def att_copy(src, dst, s):
        part = att_all.at[src, pl.ds(s * tokens, tokens)]
        return remote(part, part, att_send.at[dst, s], att_recv.at[src, s], (dst, h, r))

    def att_onward(block, s):
        part = att_all.at[block, pl.ds(s * tokens, tokens)]
        end = (ctxs - 1 - block, h, r)
        return remote(part, part, onward_send.at[s], att_recv.at[block, s], end)

    for dst in range(ctxs):

        @pl.when(dst > c)
        def _():
            kv_copy(c, dst).start()

    stream_copy = remote(
        stream_hbm, stream_in, stream_send.at[0], stream_recv.at[0], partner
    )
    stream_local = pltpu.make_async_copy(stream_hbm, stream_in, local_sem.at[2])

    for dst in range(ctxs):

        @pl.when(dst != c)
        def _():
            ids_copy(c, dst).start()

    @pl.when(c != h)
    def _():
        stream_copy.start()

    @pl.when(c == h)
    def _():
        stream_local.start()

    kv_local.wait()
    q_copy.wait()
    for src in range(ctxs):

        @pl.when(src < c)
        def _():
            kv_copy(src, c).wait_recv()

    pairs = q_ref.shape[2] // LANES
    half = LANES // 2
    keys = ctxs * tokens
    group = pairs * tokens
    low_k = lax.broadcasted_iota(jnp.int32, (keys, LANES), 1) < half
    low_q = lax.broadcasted_iota(jnp.int32, (group, LANES), 1) < half
    key_pos = lax.broadcasted_iota(jnp.int32, (group, keys), 1)
    row_pos = lax.rem(lax.broadcasted_iota(jnp.int32, (group, keys), 0), tokens)
    visible = key_pos <= row_pos + c * tokens
    for s in range(seqs):
        kv = jnp.concatenate([kv_all[src, s] for src in range(ctxs)], axis=0).astype(jnp.float32)
        turned = pltpu.roll(kv, half, 1)
        key_sides = [jnp.where(low_k, kv, 0.0), jnp.where(low_k, 0.0, turned)]
        value_sides = [jnp.where(low_k, turned, 0.0), jnp.where(low_k, 0.0, kv)]
        q = jnp.concatenate(
            [q_ref[s, :, p * LANES : (p + 1) * LANES] for p in range(pairs)], axis=0
        )
        acc, totals = None, []
        for side in range(2):
            sink = jnp.concatenate(
                [
                    jnp.full((tokens, 1), sink_ref[2 * p + side], jnp.float32)
                    for p in range(pairs)
                ],
                axis=0,
            )
            scores = lax.dot_general(
                q, key_sides[side].astype(jnp.bfloat16), NT, preferred_element_type=jnp.float32
            ) * (half ** (-0.5))
            scores = jnp.where(visible, scores, -1e30)
            peak = jnp.maximum(sink, jnp.max(scores, axis=1, keepdims=True))
            terms = jnp.where(visible, jnp.exp(scores - peak), 0.0)
            totals.append(jnp.exp(sink - peak) + jnp.sum(terms, axis=1, keepdims=True))
            piece = lax.dot_general(
                terms.astype(jnp.bfloat16),
                value_sides[side].astype(jnp.bfloat16),
                NN,
                preferred_element_type=jnp.float32,
            )
            acc = piece if acc is None else acc + piece
        attended = (acc / jnp.where(low_q, totals[0], totals[1])).astype(jnp.bfloat16)
        for p in range(pairs):
            att_all[c, s * tokens : (s + 1) * tokens, p * LANES : (p + 1) * LANES] = attended[
                p * tokens : (p + 1) * tokens
            ]
        for dst in range(ctxs):

            @pl.when((dst != c) & (lax.abs(dst - c) < ctxs - 1))
            def _():
                att_copy(c, dst, s).start()

    for src in range(ctxs):

        @pl.when(src != c)
        def _():
            ids_copy(src, c).wait_recv()

    ids_row = jnp.concatenate([ids_all[src] for src in range(ctxs)], axis=1)
    mine = (
        lax.broadcasted_iota(jnp.int32, (local_experts, all_rows), 0) + c * local_experts
    ).astype(jnp.float32)
    member = jnp.zeros((local_experts, all_rows), jnp.bool_)
    for k in range(topk):
        member = member | (mine == ids_row[k : k + 1])
    before = lax.broadcasted_iota(jnp.int32, (all_rows, all_rows), 0) <= lax.broadcasted_iota(
        jnp.int32, (all_rows, all_rows), 1
    )
    rank = lax.dot_general(
        jnp.where(member, 1.0, 0.0).astype(jnp.bfloat16),
        jnp.where(before, 1.0, 0.0).astype(jnp.bfloat16),
        NN,
        preferred_element_type=jnp.float32,
    )
    slot_row = jnp.where(member, rank - 1.0, -1.0)
    slot_rows = lax.broadcasted_iota(jnp.int32, (cap, all_rows), 0).astype(jnp.float32)
    for e in range(local_experts):
        pick[e * cap : (e + 1) * cap, :] = jnp.where(
            slot_rows == slot_row[e : e + 1], 1.0, 0.0
        ).astype(jnp.bfloat16)
    both = jnp.concatenate(
        [ids_row, slot_row, jnp.zeros((LANES - 8 - local_experts, all_rows), jnp.float32)], axis=0
    )
    token_ref[...] = jnp.transpose(both)
    gain_copy.wait()
    router_copy.wait()
    gain = gain_ref[...].reshape(1, width)
    for block in range(ctxs):
        here = slice(block * cols, (block + 1) * cols)
        gains[block] = jnp.concatenate(
            [jnp.broadcast_to(gain[:, here], (8, cols)), jnp.zeros((8, pad_cols - cols), jnp.float32)],
            axis=1,
        )
        routers[block] = jnp.concatenate(
            [
                router[:, here],
                jnp.zeros((router.shape[0], pad_cols - cols), jnp.bfloat16),
            ],
            axis=1,
        )

    ow_copy.wait()
    side, core = h // 2, lax.rem(h, 2)

    def widened(values):
        extra = jnp.zeros((values.shape[0], pad_cols - cols), jnp.float32)
        return jnp.concatenate([values, extra], axis=1)

    def projected(blocks, s):
        stacked = jnp.concatenate(
            [att_all[block, s * tokens : (s + 1) * tokens] for block in blocks], axis=0
        )
        return widened(
            lax.dot_general(stacked, ow[...], NT, preferred_element_type=jnp.float32)
        )

    def core_copy(s):
        return remote(core_out.at[s], core_in.at[s], core_send.at[s], core_recv.at[s], core_dev)

    def x_copy(s):
        return remote(x_out.at[s], x_in.at[s], x_send.at[s], x_recv.at[s], x_dev)

    for s in range(seqs):
        for block in (0, ctxs - 1) + tuple(range(1, ctxs - 1)):

            @pl.when(block != c)
            def _():
                att_copy(block, c, s).wait_recv()

            if block in (0, ctxs - 1):

                @pl.when(c == lax.abs(block - (ctxs - 2)))
                def _():
                    att_onward(block, s).start()

        across = (1 - side, side)
        core_out[s] = projected([2 * to + 1 - core for to in across], s).astype(jnp.bfloat16)
        core_copy(s).start()
        keep[s] = projected([2 * to + core for to in across], s)
        core_copy(s).wait_recv()
        x_out[s] = (keep[s, :tokens] + core_in[s, :tokens].astype(jnp.float32)).astype(
            jnp.bfloat16
        )
        x_copy(s).start()

    @pl.when(c != h)
    def _():
        stream_copy.wait_recv()

    @pl.when(c == h)
    def _():
        stream_local.wait()

    def h_copy(way, block, row, s, device):
        part = h_all.at[block, row, pl.ds(s * tokens, tokens)]
        return remote(part, part, h_send.at[way, block, s], h_recv.at[block, row, s], device)

    def h_core(block, row, s):
        return h_copy(jnp.where(row == h, 0, 1), block, row, s, core_dev)

    def h_x(block, s):
        return h_copy(2, block, h, s, x_dev)

    def h_right(block, s):
        return h_copy(3, block, h, s, (jnp.minimum(c + 1, ctxs - 1), h, r))

    def h_left(block, s):
        return h_copy(4, block, h, s, (jnp.maximum(c - 1, 0), h, r))

    def arrived(block, row, s):
        h_copy(0, block, row, s, core_dev).wait_recv()

    for s in range(seqs):
        kept = (
            keep[s, tokens:]
            + core_in[s, tokens:].astype(jnp.float32)
            + widened(stream_in[s].astype(jnp.float32))
        )
        x_copy(s).wait_recv()
        h_all[c, h, s * tokens : (s + 1) * tokens] = (
            kept + x_in[s].astype(jnp.float32)
        ).astype(jnp.bfloat16)
        h_x(c, s).start()

        @pl.when(c < ctxs - 1)
        def _():
            h_right(c, s).start()

        @pl.when(c > 0)
        def _():
            h_left(c, s).start()

        h_core(c, h, s).start()

    square_ref[...] = jnp.zeros(square_ref.shape, jnp.float32)
    logits_ref[...] = jnp.zeros(logits_ref.shape, jnp.float32)

    def take(block):
        for s in range(seqs):
            arrived(block, h ^ 1, s)
            arrived(block, h ^ 3, s)
        for row in range(ctxs):
            here = slice(row * rows, (row + 1) * rows)
            piece = h_all[block, row].astype(jnp.float32)
            y_ref[here, :] = (piece * gains[block][:1]).astype(jnp.bfloat16)
            square = piece * piece
            square_ref[here, :] += sum(
                square[:, i : i + LANES] for i in range(0, pad_cols, LANES)
            )
        xg[block] = lax.dot_general(
            pick[...], y_ref[...], NN, preferred_element_type=jnp.float32
        ).astype(jnp.bfloat16)
        logits_ref[...] += lax.dot_general(
            y_ref[...], routers[block], NT, preferred_element_type=jnp.float32
        )

    for d in range(1, ctxs + 1):
        for s in range(seqs):

            @pl.when(c - d >= 0)
            def _():
                arrived(c - d, h, s)

                @pl.when(c < ctxs - 1)
                def _():
                    h_right(c - d, s).start()

                h_x(c - d, s).start()
                h_core(c - d, h, s).start()

            @pl.when(c + d < ctxs)
            def _():
                arrived(c + d, h, s)

                @pl.when(c > 0)
                def _():
                    h_left(c + d, s).start()

                h_x(c + d, s).start()
                h_core(c + d, h, s).start()

            @pl.when(c - (d - 1) >= 0)
            def _():
                arrived(c - (d - 1), h ^ 2, s)
                h_core(c - (d - 1), h ^ 2, s).start()

            if d > 1:

                @pl.when(c + (d - 1) < ctxs)
                def _():
                    arrived(c + (d - 1), h ^ 2, s)
                    h_core(c + (d - 1), h ^ 2, s).start()

        @pl.when(c - (d - 1) >= 0)
        def _():
            take(c - (d - 1))

        if d > 1:

            @pl.when(c + (d - 1) < ctxs)
            def _():
                take(c + (d - 1))

    inverse = lax.rsqrt(jnp.sum(square_ref[...], axis=1, keepdims=True) / width + 1e-05)
    square_ref[...] = jnp.broadcast_to(inverse, square_ref.shape)
    inverse_row = jnp.transpose(square_ref[...])[:1]
    first = inverse_row.astype(jnp.bfloat16)
    rest = inverse_row - first.astype(jnp.float32)
    second = rest.astype(jnp.bfloat16)
    third = (rest - second.astype(jnp.float32)).astype(jnp.bfloat16)
    in_parts = jnp.concatenate(
        [part.astype(jnp.float32) for part in (first, second, third)]
        + [jnp.zeros((5, all_rows), jnp.float32)],
        axis=0,
    ).astype(jnp.bfloat16)
    for e in range(local_experts):
        found = lax.dot_general(
            in_parts, pick[e * cap : (e + 1) * cap, :], NT, preferred_element_type=jnp.float32
        )
        scale_ref[e] = jnp.broadcast_to(jnp.sum(found, axis=0, keepdims=True), (8, cap))

    def act_core(shard, e):
        return remote(
            act_all.at[shard, e],
            act_all.at[shard, e],
            act_send.at[jnp.where(shard == h, 0, 1), e],
            act_recv.at[shard, e],
            core_dev,
        )

    def act_x(e):
        return remote(
            act_all.at[h, e], act_all.at[h, e], act_send.at[2, e], act_recv.at[h, e], x_dev
        )

    def act_arrived(shard, e):
        remote(
            act_all.at[shard, e],
            act_all.at[shard, e],
            act_send.at[0, e],
            act_recv.at[shard, e],
            core_dev,
        ).wait_recv()

    lead = wide - width
    packed = act_all.shape[3]

    def activated(e, slot):
        pieces = [
            xg[block, pl.ds(pl.multiple_of(e * cap, cap), cap), :][:, :cols]
            for block in range(ctxs)
        ]
        blank = [jnp.zeros((cap, lead), jnp.bfloat16)]
        rows_in = jnp.concatenate(pieces + blank, axis=1)
        shifted = jnp.concatenate(blank + pieces, axis=1)
        factor = scale_ref[e][:1]
        gate = factor * lax.dot_general(
            wg[slot, :, :, :wide].reshape(2 * units, wide),
            rows_in,
            NT,
            preferred_element_type=jnp.float32,
        )
        up = factor * lax.dot_general(
            wg[slot, :, :, 2 * width - wide :].reshape(2 * units, wide),
            shifted,
            NT,
            preferred_element_type=jnp.float32,
        )
        return gate * jax.nn.sigmoid(1.702 * gate) * (up + 1.0)

    def hand_out(e, active):
        unit_rows[...] = jnp.concatenate(
            [active, jnp.zeros((2 * units, LANES - cap), jnp.float32)], axis=1
        )
        stacked = jnp.concatenate(
            [unit_rows[pl.ds(u, units, stride=2), :] for u in range(2)]
            + [jnp.zeros((packed - 2 * units, LANES), jnp.float32)],
            axis=0,
        )
        act_all[h, e] = jnp.transpose(stacked)[:cap].astype(jnp.bfloat16)
        act_x(e).start()
        act_core(h, e).start()

    @pl.loop(0, local_experts)
    def _(e):
        slot = lax.rem(e, slots)
        wg_copy(e, slot).wait()
        hand_out(e, activated(e, slot))

        @pl.when(e + slots < local_experts)
        def _():
            wg_copy(e + slots, slot).start()

        @pl.when(e >= 2)
        def _():
            act_arrived(h ^ 2, e - 2)
            act_core(h ^ 2, e - 2).start()

    by_token = token_ref[...]
    logits = logits_ref[...] * square_ref[:, :1]
    experts = logits.shape[1]
    expert_lane = lax.broadcasted_iota(jnp.int32, (all_rows, experts), 1).astype(jnp.float32)
    named = jnp.zeros((all_rows, experts), jnp.bool_)
    for k in range(topk):
        named = named | (expert_lane == by_token[:, k : k + 1])
    top = jnp.max(jnp.where(named, logits, -1e30), axis=1, keepdims=True)
    weight = jnp.where(named, jnp.exp(logits - top), 0.0)
    mix = weight / jnp.sum(weight, axis=1, keepdims=True)
    mix = jnp.concatenate([mix, jnp.zeros((all_rows, LANES - experts), jnp.float32)], axis=1)
    mix = pltpu.roll(mix, lax.rem(LANES - c * local_experts, LANES), 1)
    slot_lane = lax.broadcasted_iota(jnp.int32, (all_rows, LANES), 1).astype(jnp.float32)
    for e in range(local_experts):
        spread[:, e * LANES : (e + 1) * LANES] = jnp.where(
            slot_lane == by_token[:, 8 + e : 9 + e], mix[:, e : e + 1], 0.0
        ).astype(jnp.bfloat16)

    for e in range(local_experts - 2, local_experts):
        act_arrived(h ^ 2, e)
        act_core(h ^ 2, e).start()

    def rs_copy(src, dst, j):
        return remote(
            rs_out.at[dst, j], rs_in.at[src, j], rs_send.at[dst, j], rs_recv.at[src, j], (dst, h, r)
        )

    def combined(block, j):
        return lax.dot_general(
            spread[pl.ds(pl.multiple_of(block * rows, rows), rows), :],
            parts[j],
            NN,
            preferred_element_type=jnp.float32,
        )

    outer = (c == 0) | (c == ctxs - 1)
    far = ctxs - 1 - c
    relay_dst = jnp.where(c == 0, 1, 2)
    end_dst = jnp.where(c == 1, 3, 0)

    def relay_copy(j):
        return remote(
            rs_out.at[far, j],
            relay_in.at[j],
            rs_send.at[far, j],
            relay_recv.at[j],
            (relay_dst, h, r),
        )

    chunk = parts.shape[2]
    chunks = parts.shape[0]
    for j in range(chunks):
        first_col = j * chunk
        last_col = min(cols, first_col + chunk)

        @pl.loop(0, local_experts)
        def _(e):
            if j == 0:
                wd_copy(e).wait()
                act_arrived(h ^ 1, e)
                act_arrived(h ^ 3, e)
                for u in range(2):
                    hidden_ref[2 * e + u] = jnp.concatenate(
                        [act_all[shard, e][:, u * units : (u + 1) * units] for shard in range(4)],
                        axis=1,
                    )
            total = None
            for u in range(2):
                piece = lax.dot_general(
                    hidden_ref[2 * e + u],
                    wd[2 * e + u, :, first_col:last_col],
                    NN,
                    preferred_element_type=jnp.float32,
                )
                total = piece if total is None else total + piece
            if last_col - first_col < chunk:
                extra = jnp.zeros((cap, chunk - (last_col - first_col)), jnp.float32)
                total = jnp.concatenate([total, extra], axis=1)
            parts[j, pl.ds(pl.multiple_of(e * LANES, LANES), cap), :] = total.astype(jnp.bfloat16)

        @pl.when(outer)
        def _():
            rs_out[far, j] = combined(far, j).astype(jnp.bfloat16)
            relay_copy(j).start()
            for dst in (ctxs - 1 - relay_dst, relay_dst):
                rs_out[dst, j] = combined(dst, j).astype(jnp.bfloat16)
                rs_copy(c, dst, j).start()

        @pl.when(jnp.logical_not(outer))
        def _():
            for dst in (ctxs - 1 - c, ctxs - 1 - end_dst):
                rs_out[dst, j] = combined(dst, j).astype(jnp.bfloat16)
                rs_copy(c, dst, j).start()

    @pl.when(jnp.logical_not(outer))
    def _():
        for j in range(chunks):
            ends = combined(end_dst, j)
            relay_copy(j).wait_recv()
            rs_out[end_dst, j] = (ends + relay_in[j].astype(jnp.float32)).astype(jnp.bfloat16)
            rs_copy(c, end_dst, j).start()

    own = h_all[h, c].astype(jnp.float32)
    for j in range(chunks):
        here = slice(j * chunk, (j + 1) * chunk)
        total_ref[:, here] = combined(c, j) + own[:, here]
    for j in range(chunks):
        here = slice(j * chunk, (j + 1) * chunk)
        for src in (1, 2, 0, 3):
            sends_here = (src != c) & jnp.logical_not(outer & (src == far))

            @pl.when(sends_here)
            def _():
                rs_copy(src, c, j).wait_recv()
                total_ref[:, here] += rs_in[src, j].astype(jnp.float32)

    total = total_ref[...]
    out_ref[...] = total[:, :cols].astype(jnp.bfloat16).reshape(out_ref.shape)

    for dst in range(ctxs):

        @pl.when(dst > c)
        def _():
            kv_copy(c, dst).wait_send()

        @pl.when(dst != c)
        def _():
            ids_copy(c, dst).wait_send()
            for j in range(chunks):
                rs_copy(c, dst, j).wait_send()

        @pl.when((dst != c) & (lax.abs(dst - c) < ctxs - 1))
        def _():
            for s in range(seqs):
                att_copy(c, dst, s).wait_send()

    @pl.when((c == 1) | (c == ctxs - 2))
    def _():
        for s in range(seqs):
            att_onward(jnp.where(c == 1, ctxs - 1, 0), s).wait_send()

    @pl.when(c != h)
    def _():
        stream_copy.wait_send()

    for s in range(seqs):
        x_copy(s).wait_send()
        core_copy(s).wait_send()
        for block in range(ctxs):
            h_x(block, s).wait_send()
            h_core(block, h, s).wait_send()
            h_core(block, h ^ 2, s).wait_send()

            @pl.when((c < ctxs - 1) & (block <= c))
            def _():
                h_right(block, s).wait_send()

            @pl.when((c > 0) & (block >= c))
            def _():
                h_left(block, s).wait_send()

    for e in range(local_experts):
        act_x(e).wait_send()
        act_core(h, e).wait_send()
        act_core(h ^ 2, e).wait_send()


def layer_call(queries, keyvals, sinks, stream, out_weight, gain, router, ids, w_gate_up, w_down):
    seqs, tokens, q_cols = queries.shape
    cols = stream.shape[2]
    ctxs = lax.axis_size("ctx")
    rows = seqs * tokens
    width = gain.shape[0]
    halves, units, wide_w = w_gate_up.shape
    local_experts = halves // 2
    all_rows = ctxs * rows
    cap = all_rows * 3 // 16
    pad_cols = pl.cdiv(cols, 2 * LANES) * 2 * LANES
    packed = pl.cdiv(2 * units, LANES) * LANES
    slots = min(4, local_experts)
    chunk = 2 * LANES
    chunks = pl.cdiv(cols, chunk)
    sizes = (seqs, tokens, rows, ctxs, width, cols, cap, local_experts, units, slots)
    bf16, f32 = jnp.bfloat16, jnp.float32
    dma = pltpu.SemaphoreType.DMA
    vmem = pl.BlockSpec(memory_space=pltpu.VMEM)
    hbm = pl.BlockSpec(memory_space=pl.ANY)
    return pl.pallas_call(
        functools.partial(layer_kernel, sizes),
        out_shape=jax.ShapeDtypeStruct((seqs, tokens, cols), bf16),
        in_specs=[hbm, hbm, vmem, pl.BlockSpec(memory_space=pltpu.SMEM)] + [hbm] * 6,
        out_specs=vmem,
        scratch_shapes=[
            pltpu.VMEM(queries.shape, bf16),
            pltpu.VMEM(gain.shape, f32),
            pltpu.VMEM((ctxs, 8, pad_cols), f32),
            pltpu.VMEM((ctxs, seqs, tokens, keyvals.shape[3]), bf16),
            pltpu.VMEM((ctxs, 8, LANES), f32),
            pltpu.VMEM((seqs, tokens, cols), bf16),
            pltpu.VMEM(out_weight.shape[::-1], bf16),
            pltpu.VMEM(router.shape[::-1], bf16),
            pltpu.VMEM((ctxs, router.shape[1], pad_cols), bf16),
            pltpu.VMEM((slots, units, 2, wide_w), bf16),
            pltpu.VMEM(w_down.shape, bf16),
            pltpu.VMEM((ctxs, rows, q_cols), bf16),
            pltpu.VMEM((seqs, 2 * tokens, pad_cols), bf16),
            pltpu.VMEM((seqs, 2 * tokens, pad_cols), bf16),
            pltpu.VMEM((seqs, 2 * tokens, pad_cols), f32),
            pltpu.VMEM((seqs, tokens, pad_cols), bf16),
            pltpu.VMEM((seqs, tokens, pad_cols), bf16),
            pltpu.VMEM((ctxs, 4, rows, pad_cols), bf16),
            pltpu.VMEM((all_rows, pad_cols), bf16),
            pltpu.VMEM((all_rows, LANES), f32),
            pltpu.VMEM((all_rows, router.shape[1]), f32),
            pltpu.VMEM((all_rows, LANES), f32),
            pltpu.VMEM((local_experts * cap, all_rows), bf16),
            pltpu.VMEM((all_rows, local_experts * LANES), bf16),
            pltpu.VMEM((ctxs, local_experts * cap, pad_cols), bf16),
            pltpu.VMEM((local_experts, 8, cap), f32),
            pltpu.VMEM((2 * units, LANES), f32),
            pltpu.VMEM((4, local_experts, cap, packed), bf16),
            pltpu.VMEM((chunks, local_experts * LANES, chunk), bf16),
            pltpu.VMEM((ctxs, chunks, rows, chunk), bf16),
            pltpu.VMEM((ctxs, chunks, rows, chunk), bf16),
            pltpu.VMEM((chunks, rows, chunk), bf16),
            pltpu.VMEM((halves, cap, w_down.shape[1]), bf16),
            pltpu.VMEM((rows, chunks * chunk), f32),
            dma((6,)),
            dma((slots,)),
            dma((local_experts,)),
            dma((ctxs,)),
            dma((ctxs,)),
            dma((ctxs,)),
            dma((ctxs,)),
            dma((1,)),
            dma((1,)),
            dma((ctxs, seqs)),
            dma((ctxs, seqs)),
            dma((seqs,)),
            dma((seqs,)),
            dma((seqs,)),
            dma((seqs,)),
            dma((5, ctxs, seqs)),
            dma((ctxs, 4, seqs)),
            dma((3, local_experts)),
            dma((4, local_experts)),
            dma((ctxs, chunks)),
            dma((ctxs, chunks)),
            dma((chunks,)),
            dma((seqs,)),
        ],
        compiler_params=pltpu.CompilerParams(
            vmem_limit_bytes=67043328, collective_id=0, has_side_effects=True
        ),
    )(
        queries,
        keyvals.reshape(seqs, tokens, keyvals.shape[3]),
        jnp.transpose(ids, (0, 2, 1)),
        sinks,
        gain,
        stream,
        out_weight.T,
        router.T,
        jnp.transpose(w_gate_up, (1, 0, 2)),
        w_down,
    )


def one_chip_row(queries, keyvals, stream, out_weight, router, ids, w_gate_up):
    ctxs, heads = lax.axis_size("ctx"), lax.axis_size("head")
    rows = queries.shape[0] * queries.shape[1]
    return (
        ctxs == heads == 4
        and rows == LANES
        and keyvals.shape[2] == 1
        and keyvals.shape[3] == LANES
        and out_weight.shape[1] == stream.shape[2]
        and w_gate_up.shape[0] == 16
        and ids.shape[2] <= 8
        and router.shape[1] <= LANES
    )


def on_device(
    queries, keyvals, sinks, stream, out_weight, norm_gain, router, expert_ids, w_gate_up, w_down
):
    if one_chip_row(queries, keyvals, stream, out_weight, router, expert_ids, w_gate_up):
        return layer_call(
            queries,
            keyvals,
            sinks,
            stream,
            out_weight,
            norm_gain,
            router,
            expert_ids,
            w_gate_up,
            w_down,
        )
    ctx_count = lax.axis_size("ctx")
    local_seqs = queries.shape[0]
    tokens = queries.shape[1]
    row_count = local_seqs * tokens
    kv_local = keyvals.shape[2]
    head_dim = keyvals.shape[3] // 2
    q_local = queries.shape[2] // head_dim
    query_group_size = q_local // kv_local
    wide_rows = query_group_size * tokens
    col_width = stream.shape[2]
    first_pos = lax.axis_index("ctx") * tokens
    last_pos = first_pos + tokens - 1
    score_scale = head_dim ** (-0.5)
    scaled_queries = queries * jnp.asarray(score_scale, jnp.bfloat16)
    query_grid = scaled_queries.reshape(local_seqs, tokens, kv_local, query_group_size, head_dim)
    query_wide = jnp.transpose(query_grid, (0, 2, 3, 1, 4)).reshape(
        local_seqs, kv_local, wide_rows, head_dim
    )
    positions = first_pos + jnp.tile(jnp.arange(tokens), query_group_size)
    sink_rows = jnp.repeat(sinks.reshape(kv_local, query_group_size), tokens, axis=1)
    sink_grid = jnp.broadcast_to(sink_rows[None], (local_seqs, kv_local, wide_rows))
    start_state = (
        sink_grid,
        jnp.ones_like(sink_grid),
        jnp.zeros((local_seqs, kv_local, head_dim, wide_rows), jnp.float32),
    )

    def attend_block(running, shard_piece):
        peak_old, denom_old, accum_old = running
        key_block = shard_piece[..., :head_dim]
        value_block = shard_piece[..., head_dim:]
        scores = jnp.einsum(
            "skmd,snkd->sknm", query_wide, key_block, preferred_element_type=jnp.float32
        )
        key_pos = jnp.arange(shard_piece.shape[1])
        visible = key_pos[:, None] <= positions[None, :]
        masked = jnp.where(visible[None, None], scores, -jnp.inf)
        peak_new = jnp.maximum(peak_old, jnp.max(masked, axis=2))
        exp_terms = jnp.exp(masked - peak_new[:, :, None, :])
        factor = jnp.exp(peak_old - peak_new)
        denom_new = denom_old * factor + jnp.sum(exp_terms, axis=2)
        accum_new = accum_old * factor[:, :, None, :] + jnp.einsum(
            "sknm,snkd->skdm",
            exp_terms.astype(jnp.bfloat16),
            value_block,
            preferred_element_type=jnp.float32,
        )
        return (peak_new, denom_new, accum_new)

    shard_piece = lax.all_gather(keyvals, "ctx", axis=1, tiled=True)

    def keep_state(state_in):
        return state_in

    def update_state(state_in):
        return attend_block(state_in, shard_piece)

    peak_fin, denom_fin, accum_fin = lax.cond(
        jnp.int32(0) > last_pos, keep_state, update_state, start_state
    )
    normalized = (accum_fin / denom_fin[:, :, None, :]).reshape(
        local_seqs, kv_local, head_dim, query_group_size, tokens
    )
    attended = (
        jnp.transpose(normalized, (0, 4, 1, 3, 2))
        .reshape(row_count, q_local * head_dim)
        .astype(jnp.bfloat16)
    )
    token_ids = lax.all_gather(
        expert_ids.reshape(row_count, expert_ids.shape[2]).T, "ctx", axis=1, tiled=True
    )
    all_rows = ctx_count * row_count
    halves = w_gate_up.shape[0]
    units = w_gate_up.shape[1]
    token_block = min(all_rows, 8 * tokens)
    cap = token_block // tokens * (3 * tokens // 16)
    row_expert = (lax.axis_index("ctx") * halves + jnp.arange(halves)) // 2
    named = jnp.any(token_ids[:, None, :] == row_expert[None, :, None], axis=0)
    counted = named.astype(jnp.int32).reshape(halves, all_rows // token_block, token_block)
    rank = jnp.cumsum(counted, axis=2) - 1
    slots = jnp.where(named, rank.reshape(halves, all_rows), -1).reshape(halves, 1, all_rows)
    width = norm_gain.shape[0]
    head_count = lax.axis_size("head")
    swapped = ctx_count == head_count and out_weight.shape[1] == col_width
    if swapped:
        pairs = [
            (first * head_count + second, second * head_count + first)
            for first in range(ctx_count)
            for second in range(head_count)
        ]
        turned = lax.ppermute(
            stream.reshape(row_count, col_width), ("ctx", "head"), perm=pairs
        )
        every_row = lax.all_gather(attended, "ctx", axis=0, tiled=True)
        partial_proj = jnp.dot(every_row, out_weight, preferred_element_type=jnp.float32)
        summed = lax.psum_scatter(
            partial_proj.astype(jnp.bfloat16), "head", scatter_dimension=0, tiled=True
        )
        turned_state = summed.astype(jnp.float32) + turned.astype(jnp.float32)
        every_state = lax.all_gather(
            turned_state.astype(jnp.bfloat16), ("head", "ctx"), axis=0, tiled=False
        )
    else:
        partial_proj = jnp.dot(attended, lax.all_gather(out_weight, "ctx", axis=1, tiled=True), preferred_element_type=jnp.float32)
        own_stream = stream.reshape(row_count, col_width).astype(jnp.float32)
        summed = lax.psum_scatter(
            partial_proj.astype(jnp.bfloat16), "head", scatter_dimension=1, tiled=True
        )
        own_state = (summed.astype(jnp.float32) + own_stream).astype(jnp.bfloat16)
        every_state = lax.all_gather(own_state, ("ctx", "head"), axis=0, tiled=False)
    every_state = every_state.reshape(ctx_count, width // col_width, row_count, col_width)
    expert_count = router.shape[1]
    unit_rows = jnp.transpose(w_gate_up, (1, 0, 2)).reshape(units * halves, w_gate_up.shape[2])
    router_rows = jnp.pad(router.T, ((0, 0), (0, -width % LANES)))
    gain = norm_gain.reshape(width // col_width, 1, col_width)
    active, logits = gate_up_call(
        every_state, gain, router_rows, unit_rows, slots, units, token_block, cap
    )
    member = jnp.any(token_ids[:, None, :] == jnp.arange(expert_count)[None, :, None], axis=0)
    masked = jnp.where(member, logits, -jnp.inf)
    mix_all = jax.nn.softmax(masked, axis=0)
    chosen_rows = (row_expert[:, None] == jnp.arange(expert_count)[None, :]).astype(jnp.float32)
    mix_rows = jnp.dot(chosen_rows, mix_all, precision=lax.Precision.HIGHEST)
    mix_rows = mix_rows.reshape(halves, 1, all_rows)
    every_active = lax.all_gather(active.reshape(-1, units), "head", axis=0, tiled=True)
    every_active = every_active.reshape(width // col_width, *active.shape)
    partial_out = down_call(every_active, w_down, slots, mix_rows, token_block)
    combined = lax.psum_scatter(partial_out, "ctx", scatter_dimension=0, tiled=True)
    if swapped:
        own_state = every_state[lax.axis_index("ctx"), lax.axis_index("head")]
    layer_out = (own_state.astype(jnp.float32) + combined.astype(jnp.float32)).astype(jnp.bfloat16)
    return layer_out.reshape(local_seqs, tokens, col_width)


def solution(mesh):
    placed = (
        P("rep", "ctx", "head"),
        P("rep", "ctx", "head", None),
        P("head"),
        P("rep", "ctx", "head"),
        P("head", "ctx"),
        P(),
        P(),
        P("rep", "ctx", None),
        P("ctx", "head", None),
        P("ctx", None, "head"),
    )
    return jax.shard_map(
        on_device, mesh=mesh, in_specs=placed, out_specs=P("rep", "ctx", "head"), check_vma=False
    )
```
